32 devices in a mesh: tm: 8 (over y, x, core), space: 4 (over z).
Axes of the slice: x: 2, y: 2, z: 4, core: 2. Of those that a mesh axis runs over, the one named last changes fastest.
Arguments:
- coarse_guess: float32 [8, 32, 12, 512], P('tm', 'space'), may hold values from -6 to 6
- initial_state: float32 [32, 12, 512], P('space'), may hold values from -6 to 6
- fine_volume: bfloat16 [512, 512], replicated
- coarse_volume: bfloat16 [512, 512], replicated
- lift_matrix: bfloat16 [384, 512], replicated, may hold values from -0.0390625 to 0.0390625
- wave_speed: float32 [12], replicated, may hold values from 0.1 to 0.6
- reaction_rate: float32 [24], replicated, may hold values from 0.05 to 0.5
- species_map: int32 [24, 3], replicated, may hold values from 0 to 11
- neighbour_element: int32 [32, 6], P('space'), may hold values from 0 to 7
- neighbour_rank: int32 [32, 6], P('space'), may hold values from -1 to 1
Outputs:
- iterate: float32 [32, 32, 12, 512], P('tm', 'space')
The draws below stay inside these ranges and needn't reach their ends.
All inputs are finite; a program needn't handle non-finite values.
Results may differ from the reference program's by a relative error of at most 0.025.
Values may be sent and summed in bfloat16 or wider, within the bound.
A program may use at most 64 MiB of HBM per device.

```python
import math
import jax
import jax.numpy as jnp
from jax import lax

SIDE = 8
NODES = 512
FACE_NODES = 384
VARS = 12
REACTIONS = 24
STRIDE = 4
E_DEV = 8
ELEMS = 32
NT = 32
N_TM = 8
N_SPACE = 4


def operator_draw(key, lower, upper, rough):
    diagonal = jax.random.uniform(jax.random.fold_in(key, 11), (NODES,), jnp.float32, lower, upper)
    return (jnp.diag(diagonal) + rough * (0.15 / math.sqrt(NODES))).astype(jnp.bfloat16)


def draw_fine_volume(key, part):
    inner = jax.random.fold_in(key, 101)
    rough = jax.random.normal(jax.random.fold_in(inner, 3), (NODES, NODES), jnp.float32)
    return operator_draw(inner, 0.45, 0.7, rough)


def draw_coarse_volume(key, part):
    inner = jax.random.fold_in(key, 202)
    rough = jax.random.normal(jax.random.fold_in(inner, 3), (NODES, NODES), jnp.float32)
    return operator_draw(inner, 0.35, 0.6, rough)


def with_ends(array, own_key, least, high):
    longest = array.shape.index(max(array.shape))
    spots = []
    for shift in (0, 1):
        where = [jax.random.randint(jax.random.fold_in(own_key, axis), (), 0, length) for axis, length in enumerate(array.shape)]
        where[longest] = (where[longest] + shift) % array.shape[longest]
        spots.append(tuple(where))
    return array.at[spots[0]].set(least).at[spots[1]].set(high)


def steps_of(rng, extent, shards, low, top_value):
    def one(axis_at, shards_of):
        steps = jax.random.uniform(jax.random.fold_in(jax.random.fold_in(rng, 6), axis_at), (shards_of,), jnp.float32, low / len(shards), top_value / len(shards))
        return jnp.repeat(jnp.exp(steps), extent[axis_at] // shards_of).reshape((-1,) + (1,) * (len(extent) - axis_at - 1))

    level = one(*shards[0])
    for cut in shards[1:]:
        level = level * one(*cut)
    return level


def scatter_about(own_key, extent, scale, most, shards=(), kind=jnp.bfloat16):
    entries = scale * jax.random.normal(own_key, extent, jnp.float32)
    if shards:
        entries = entries * steps_of(own_key, extent, shards, -0.22, 0.18)
    return jnp.clip(entries, -most, most).astype(kind)


def setup_inputs(seed: int = 0) -> dict:
    key_list = jax.random.split(jax.random.key(seed), 11)
    coarse_guess = scatter_about(key_list[0], (N_TM, ELEMS, VARS, NODES), 1.0, 6.0, ((0, 8), (1, 4)), jnp.float32)
    initial_state = scatter_about(key_list[1], (ELEMS, VARS, NODES), 1.0, 6.0, ((0, 4),), jnp.float32)
    fine_volume = draw_fine_volume(jax.random.fold_in(key_list[10], 71), 0)
    coarse_volume = draw_coarse_volume(jax.random.fold_in(key_list[10], 71), 0)
    lift_matrix = scatter_about(key_list[4], (FACE_NODES, NODES), (64 * FACE_NODES) ** -0.5, 0.0390625)
    wave_speed = jnp.clip(jnp.exp(jax.random.uniform(key_list[5], (VARS,), jnp.float32, math.log(0.1), math.log(0.6))), 0.1, 0.6)
    reaction_rate = jnp.clip(jnp.exp(jax.random.uniform(key_list[6], (REACTIONS,), jnp.float32, math.log(0.05), math.log(0.5))), 0.05, 0.5)
    species_map = with_ends(jax.random.randint(key_list[7], (REACTIONS, 3), 0, VARS), jax.random.fold_in(key_list[7], 1), 0, VARS - 1).astype(jnp.int32)
    neighbour_element = with_ends(jax.random.randint(key_list[8], (ELEMS, 6), 0, E_DEV), jax.random.fold_in(key_list[8], 1), 0, E_DEV - 1).astype(jnp.int32)
    neighbour_rank = with_ends(jax.random.randint(key_list[9], (ELEMS, 6), -1, 2), jax.random.fold_in(key_list[9], 1), -1, 1).astype(jnp.int32)
    return dict(coarse_guess=coarse_guess, initial_state=initial_state, fine_volume=fine_volume, coarse_volume=coarse_volume, lift_matrix=lift_matrix, wave_speed=wave_speed, reaction_rate=reaction_rate, species_map=species_map, neighbour_element=neighbour_element, neighbour_rank=neighbour_rank)


coarse_gain = 4.0


def face_cut(rounded):
    blocked = rounded.reshape(rounded.shape[:-1] + (SIDE, SIDE, SIDE))
    planes = [blocked[..., 0, :, :], blocked[..., -1, :, :], blocked[..., :, 0, :],
              blocked[..., :, -1, :], blocked[..., :, :, 0], blocked[..., :, :, -1]]
    return jnp.stack([plane.reshape(rounded.shape[:-1] + (SIDE * SIDE,)) for plane in planes], axis=-2)


def selections(species_map):
    labels = jnp.arange(VARS, dtype=jnp.int32)[None, :]
    first_table = (species_map[:, 0:1] == labels).astype(jnp.float32)
    second_table = (species_map[:, 1:2] == labels).astype(jnp.float32)
    made_table = (species_map[:, 2:3] == labels).astype(jnp.float32)
    return first_table, second_table, made_table - first_table


def react(state, tables, scaled_rates):
    first_table, second_table, change_table = tables
    first_amount = jnp.einsum('rv,...vn->...rn', first_table, state, precision=lax.Precision.HIGHEST)
    second_amount = jnp.einsum('rv,...vn->...rn', second_table, state, precision=lax.Precision.HIGHEST)
    speed_term = scaled_rates[:, None] * first_amount * second_amount / (
        1.0 + first_amount * first_amount + second_amount * second_amount)
    return state + jnp.einsum('rv,...rn->...vn', change_table, speed_term, precision=lax.Precision.HIGHEST)


def reference(coarse_guess, initial_state, fine_volume, coarse_volume, lift_matrix, wave_speed,
              reaction_rate, species_map, neighbour_element, neighbour_rank):
    tables = selections(species_map)
    home_block = (jnp.arange(ELEMS, dtype=jnp.int32) // E_DEV)[:, None]
    partner = (((home_block + neighbour_rank) % N_SPACE) * E_DEV + neighbour_element).astype(jnp.int32)

    def substep(state, volume, gain):
        rounded = state.astype(jnp.bfloat16)
        own_faces = face_cut(rounded)
        across = jnp.stack([jnp.take(own_faces[..., which_face ^ 1, :], partner[:, which_face], axis=-3)
                            for which_face in range(6)], axis=-2)
        jumps = (wave_speed[:, None, None] * (across.astype(jnp.float32) - own_faces.astype(jnp.float32)))
        jumps = jumps.astype(jnp.bfloat16).reshape(state.shape[:-1] + (FACE_NODES,))
        moved = jnp.dot(rounded, volume, preferred_element_type=jnp.float32)
        moved = moved + jnp.dot(jumps, lift_matrix, preferred_element_type=jnp.float32)
        return react(moved, tables, reaction_rate * gain)

    def fine_step(state):
        return substep(substep(state, fine_volume, 1.0), fine_volume, 1.0)

    def coarse_step(state):
        return substep(state, coarse_volume, coarse_gain)

    def relax(starts):
        points = []
        current = starts
        for number in range(STRIDE - 1):
            current = fine_step(current)
            points.append(current)
        return points

    starts = jnp.concatenate([initial_state[None], coarse_guess[1:]], axis=0)
    relaxed = fine_step(relax(starts)[-1])
    second = jnp.concatenate([initial_state[None], relaxed[:-1]], axis=0)
    correction = fine_step(relax(second)[-1]) - coarse_step(second)

    def chain(value, term):
        updated = coarse_step(value) + term
        return updated, updated

    final_value, coarse_values = lax.scan(chain, initial_state, correction)
    third = jnp.concatenate([initial_state[None], coarse_values[:-1]], axis=0)
    points = relax(third) + [coarse_values]
    stacked = jnp.stack(points, axis=1)
    return stacked.reshape((NT, ELEMS, VARS, NODES))
```

```python
import jax
import jax.numpy as jnp
import numpy as np
from jax import lax
from jax.experimental import pallas as pl
from jax.experimental.pallas import tpu as pltpu
from jax.sharding import PartitionSpec as P

SIDE = 8
STRIDE = 4
COARSE_GAIN = 4.0
VMEM = pltpu.VMEM
SMEM = pltpu.SMEM
MESH = pl.DeviceIdType.MESH
BF16 = jnp.bfloat16
F32 = jnp.float32


def face_table(side):
    plane = side * side
    inner = np.arange(plane)
    first, second = inner // side, inner % side
    last = side - 1
    node_lists = [
        first * plane + second,
        first * plane + last * side + second,
        first * plane + second * side,
        first * plane + second * side + last,
    ]
    table = np.zeros((side**3, 4 * plane), np.float32)
    for f in range(4):
        table[node_lists[f], f * plane + inner] = 1.0
    return table


def find_jumps(c):
    xj, idx, rank, speed = c["xj"], c["idx"], c["rank"], c["speed"]
    variables, elems, nodes = c["a"].shape
    block = c["block"]
    blocks = elems // block
    pair = idx.shape[2]
    picked = jnp.dot(xj[:, 0:nodes], c["table"][...], preferred_element_type=F32)
    low = lax.broadcasted_iota(jnp.int32, (elems, pair), 1) < pair // 2
    for k in range(3):
        spots = [idx[k, s * block : (s + 1) * block, :] for s in range(blocks)]
        offsets = [rank[k, s * block : (s + 1) * block, :] for s in range(blocks)]
        for v in range(variables):
            rows = slice(v * elems, (v + 1) * elems)
            if k == 0:
                faces = jnp.where(
                    low,
                    xj[rows, 0:pair].astype(F32),
                    xj[rows, nodes - pair : nodes].astype(F32),
                )
            else:
                faces = picked[rows, (k - 1) * pair : k * pair]
            own = [faces[s * block : (s + 1) * block] for s in range(blocks)]
            parts = []
            for s in range(blocks):
                before, here, after = [
                    jnp.take_along_axis(
                        own[(s + d) % blocks], spots[s], axis=0, mode="promise_in_bounds"
                    )
                    for d in (-1, 0, 1)
                ]
                across = jnp.where(
                    offsets[s] < 0, before, jnp.where(offsets[s] > 0, after, here)
                )
                parts.append(speed[v] * (across - pltpu.roll(own[s], pair // 2, 1)))
            xj[rows, nodes + k * pair : nodes + (k + 1) * pair] = jnp.concatenate(
                parts, axis=0
            ).astype(BF16)


def transport_react(c, weights, gain, finish):
    a, m, h, gain_ref, loss_ref = c["a"], c["m"], c["h"], c["made"], c["used"]
    species, rates = c["species"], c["rates"]
    variables, elems, nodes = a.shape
    moved = jnp.dot(c["xj"][...], weights[...], preferred_element_type=F32)
    for v in range(variables):
        own = moved[v * elems : (v + 1) * elems]
        a[v] = own
        m[v] = own.astype(BF16)
        h[v] = (own * own + 0.5).astype(BF16)
        zero = jnp.zeros((elems, nodes), BF16)
        gain_ref[v] = zero
        loss_ref[v] = zero
    for r in range(species.shape[1]):
        s0, s1, s2 = species[0, r], species[1, r], species[2, r]
        factor = (rates[r] * gain).astype(BF16)
        rate = factor * (m[s0] * m[s1]) / (h[s0] + h[s1])
        gain_ref[s2] += rate
        loss_ref[s0] += rate
    for v in range(variables):
        finish(v, a[v] + (gain_ref[v].astype(F32) - loss_ref[v].astype(F32)))


def store_x(c, v, new):
    elems, nodes = new.shape
    c["xj"][v * elems : (v + 1) * elems, 0:nodes] = new.astype(BF16)


def fine_substep(c):
    find_jumps(c)

    def finish(v, new):
        c["a"][v] = new
        store_x(c, v, new)

    transport_react(c, c["fine"], 1.0, finish)


def coarse_substep(c, finish):
    find_jumps(c)
    transport_react(c, c["coarse"], COARSE_GAIN, finish)


CONSTS = ("table", "codes", "lift_in", "fine_in", "coarse_in", "speed", "rates", "species")
IN_SMEM = ("speed", "rates", "species")
SCRATCH = ("xj", "a", "idx", "rank", "fine", "coarse", "m", "h", "made", "used")


def phase_scratch(dims, faces):
    variables, elems, nodes = dims
    slab = VMEM(dims, BF16)
    table = VMEM((3, elems, faces // 3), jnp.int32)
    weights = VMEM((nodes + faces, nodes), BF16)
    wide = VMEM((variables * elems, nodes + faces), BF16)
    return [wide, VMEM(dims, F32), table, table, weights, weights, slab, slab, slab, slab]


def begin(refs, count):
    c = dict(zip(CONSTS, refs))
    others = refs[len(CONSTS) : len(CONSTS) + count]
    scratch = refs[len(CONSTS) + count :]
    c.update(zip(SCRATCH, scratch))
    codes = c["codes"]
    blocks, _, block, _ = codes.shape
    c["block"] = block
    for s in range(blocks):
        for k in range(3):
            code = codes[s, k]
            rows = slice(s * block, (s + 1) * block)
            c["idx"][k, rows, :] = lax.rem(code, block)
            c["rank"][k, rows, :] = lax.div(code, block) - 1
    nodes = c["fine_in"].shape[0]
    c["fine"][0:nodes, :] = c["fine_in"][...]
    c["coarse"][0:nodes, :] = c["coarse_in"][...]
    half = c["idx"].shape[2] // 2
    for f in range(6):
        part = c["lift_in"][(f ^ 1) * half : (f ^ 1) * half + half, :]
        c["fine"][nodes + f * half : nodes + (f + 1) * half, :] = part
        c["coarse"][nodes + f * half : nodes + (f + 1) * half, :] = part
    return c, others, scratch[len(SCRATCH) :]


def unpack(ref, v, blocks, block):
    both = [ref[s, v * block : (v + 2) * block, :].astype(F32) for s in range(blocks)]
    return [
        jnp.concatenate([b[w * block : (w + 1) * block] for b in both], axis=0) for w in (0, 1)
    ]


def loop(count, fn):
    def one(i, carry):
        fn(i)
        return carry

    lax.fori_loop(0, count, one, 0)


def chain_kernel(*refs):
    c, (starts, message, early), (corr, point, sem) = begin(refs, 3)
    variables, elems, nodes = c["a"].shape
    block = c["block"]
    blocks = elems // block
    here, own = lax.axis_index("tm"), lax.axis_index("space")
    mine = pl.ds(pl.multiple_of(own * block, block), block)
    for v in range(0, variables, 2):
        for w, part in enumerate(unpack(starts, v, blocks, block)):
            store_x(c, v + w, part)

    def phase(q):
        def fine(i):
            fine_substep(c)

            @pl.when(jnp.logical_and(here == 0, i % 2 == 1))
            def _():
                point[...] = c["a"][:, mine, :]
                copy = pltpu.make_async_copy(point, early.at[q * STRIDE + i // 2], sem)
                copy.start()
                copy.wait()

        loop(2 * STRIDE, fine)

        @pl.when(q == 0)
        def _():
            def finish(v, new):
                corr[v] = new

            coarse_substep(c, finish)

    loop(2, phase)
    keep = jnp.where(jnp.logical_or(here == 0, here == 2), 0.0, 1.0)
    for v in range(0, variables, 2):
        ends = [c["a"][v + w] - keep * corr[v + w] for w in (0, 1)]
        for s in range(blocks):
            both = jnp.concatenate([e[s * block : (s + 1) * block] for e in ends], axis=0)
            message[s, v * block : (v + 2) * block, :] = both.astype(BF16)


def finish_kernel(*refs):
    c, (messages, last, early, other, out), (sem,) = begin(refs, 5)
    variables, elems, nodes = c["a"].shape
    block = c["block"]
    blocks = elems // block
    here, own = lax.axis_index("tm"), lax.axis_index("space")
    mine = pl.ds(pl.multiple_of(own * block, block), block)

    @pl.when(here == 0)
    def _():
        copy = pltpu.make_async_copy(early.at[pl.ds(0, STRIDE)], out, sem)
        copy.start()
        copy.wait()

    @pl.when(here == 1)
    def _():
        copy = pltpu.make_async_copy(other, out, sem)
        copy.start()
        copy.wait()

    @pl.when(here >= 2)
    def _():
        for v in range(0, variables, 2):
            for w, part in enumerate(unpack(messages.at[0], v, blocks, block)):
                store_x(c, v + w, part)

        def advance(i):
            terms = {}

            def finish(v, new):
                if v % 2 == 0:
                    terms[v], terms[v + 1] = unpack(messages.at[i + 1], v, blocks, block)
                store_x(c, v, new + terms[v])

            coarse_substep(c, finish)

        loop(here - 2, advance)

        def keep(v, new):
            c["a"][v] = new

        coarse_substep(c, keep)
        for v in range(0, variables, 2):
            both = last[v * block : (v + 2) * block, :].astype(F32)
            for w in (0, 1):
                term = both[w * block : (w + 1) * block]
                out[STRIDE - 1, v + w] = c["a"][v + w, mine, :] + term

        def fine(i):
            fine_substep(c)

            @pl.when(i % 2 == 1)
            def _():
                out[i // 2] = c["a"][:, mine, :]

        loop(2 * (STRIDE - 1), fine)


def remote(src, dst, send, recv, target):
    return pltpu.make_async_remote_copy(
        src_ref=src,
        dst_ref=dst,
        send_sem=send,
        recv_sem=recv,
        device_id=target,
        device_id_type=MESH,
    )


def start_kernel(
    guess,
    initial,
    element,
    rank,
    starts,
    codes,
    mine,
    first,
    code,
    send,
    recv,
    first_send,
    code_send,
    code_recv,
    local,
):
    me, size = lax.axis_index("space"), lax.axis_size("space")
    here, rows = lax.axis_index("tm"), lax.axis_size("tm")
    variables, block, _ = initial.shape
    lanes = code.shape[2]
    value = element[...] + block * (rank[...] + 1)
    low = lax.broadcasted_iota(jnp.int32, (block, lanes), 1) < lanes // 2
    for k in range(3):
        code[k] = jnp.where(low, value[:, 2 * k + 1 : 2 * k + 2], value[:, 2 * k : 2 * k + 1])
    for v in range(0, variables, 2):
        both = jnp.concatenate([guess[0, v], guess[0, v + 1]], axis=0)
        mine[v * block : (v + 2) * block, :] = both.astype(BF16)
        both = jnp.concatenate([initial[v], initial[v + 1]], axis=0)
        first[v * block : (v + 2) * block, :] = both.astype(BF16)

    from_first = jnp.logical_or(here == 0, here == 2)
    sends = jnp.logical_and(here >= 1, here <= rows - 2)
    target = jnp.where(here == rows - 2, 1, lax.rem(here + 2, rows))
    source = jnp.where(here == 1, rows - 2, lax.rem(here + rows - 2, rows))

    barrier = pltpu.get_barrier_semaphore()
    for d in range(1, size):
        mate = {"tm": here, "space": lax.rem(me + d, size)}
        pl.semaphore_signal(barrier, inc=1, device_id=mate, device_id_type=MESH)

    @pl.when(jnp.logical_not(from_first))
    def _():
        for d in range(size):
            mate = {"tm": source, "space": lax.rem(me + d, size)}
            pl.semaphore_signal(barrier, inc=1, device_id=mate, device_id_type=MESH)

    pl.semaphore_wait(barrier, size - 1 + size * sends.astype(jnp.int32))

    def code_copy(d):
        mate = {"tm": here, "space": lax.rem(me + d, size)}
        return remote(code, codes.at[me], code_send.at[d - 1], code_recv.at[d - 1], mate)

    def first_copy(d):
        mate = {"tm": here, "space": lax.rem(me + d, size)}
        return remote(first, starts.at[me], first_send.at[d - 1], recv.at[d], mate)

    def guess_copy(d):
        mate = {"tm": target, "space": lax.rem(me + d, size)}
        return remote(mine, starts.at[me], send.at[d], recv.at[d], mate)

    keep_code = pltpu.make_async_copy(code, codes.at[me], local.at[0])
    keep_first = pltpu.make_async_copy(first, starts.at[me], local.at[1])

    @pl.when(from_first)
    def _():
        for d in range(1, size):
            first_copy(d).start()
        keep_first.start()

    @pl.when(sends)
    def _():
        for d in range(size):
            guess_copy(d).start()

    for d in range(1, size):
        code_copy(d).start()
    keep_code.start()
    keep_code.wait()

    @pl.when(from_first)
    def _():
        keep_first.wait()
        for d in range(1, size):
            first_copy(d).wait_recv()

    @pl.when(jnp.logical_not(from_first))
    def _():
        for d in range(size):
            guess_copy(d).wait_recv()

    for d in range(1, size):
        code_copy(d).wait_recv()

    @pl.when(from_first)
    def _():
        for d in range(1, size):
            first_copy(d).wait_send()

    @pl.when(sends)
    def _():
        for d in range(size):
            guess_copy(d).wait_send()

    for d in range(1, size):
        code_copy(d).wait_send()


def spread_kernel(
    message,
    early,
    messages,
    last,
    other,
    send,
    pass_send,
    recv,
    last_send,
    last_recv,
    other_sems,
    local,
):
    me, size = lax.axis_index("tm"), lax.axis_size("tm")
    own = lax.axis_index("space")
    chip, core = me // 2, me % 2
    blocks = message.shape[0]
    sibling = me + 1 - 2 * core
    barrier = pltpu.get_barrier_semaphore()
    for d in range(1, size):
        mate = {"tm": lax.rem(me + d, size), "space": own}
        pl.semaphore_signal(barrier, inc=1, device_id=mate, device_id_type=MESH)
    pl.semaphore_wait(barrier, size - 1)

    def at(target):
        return {"tm": target, "space": own}

    def out_copy(slot, q, target):
        return remote(
            message.at[q], messages.at[me - 2, q], send.at[slot, q], recv.at[me, q], at(target)
        )

    def pass_copy(k, q):
        slot = messages.at[k - 2, q]
        return remote(slot, slot, pass_send.at[k, q], recv.at[k, q], at(sibling))

    back = jnp.where(me == 1, size - 1, lax.rem(me + size - 1, size))
    last_copy = remote(message.at[own], last, last_send, last_recv, at(back))
    gives_last = jnp.logical_or(me == 1, me >= 3)
    other_copy = remote(
        early.at[pl.ds(STRIDE, STRIDE)], other, other_sems.at[0], other_sems.at[1], at(1)
    )

    @pl.when(me == 0)
    def _():
        other_copy.start()

    def outgoing(act):
        for p in range(size // 2 - 1, 1, -1):

            @pl.when(jnp.logical_and(me >= 2, chip < p))
            def _():
                for q in range(blocks):
                    act(out_copy(p, q, 2 * p + core))

        @pl.when(jnp.logical_and(me >= 2, core == 0))
        def _():
            for q in range(blocks):
                act(out_copy(0, q, me + 1))

    outgoing(lambda copy: copy.start())

    @pl.when(gives_last)
    def _():
        last_copy.start()

    @pl.when(me >= 2)
    def _():
        keep = pltpu.make_async_copy(message, messages.at[me - 2], local)
        keep.start()
        keep.wait()

    for k in range(2, size - 1):

        @pl.when(me > k)
        def _():
            for q in range(blocks):
                pass_copy(k, q).wait_recv()

                @pl.when(jnp.logical_and(chip > k // 2, core == k % 2))
                def _():
                    pass_copy(k, q).start()

    @pl.when(me >= 2)
    def _():
        last_copy.wait_recv()

    @pl.when(me == 1)
    def _():
        other_copy.wait_recv()

    for k in range(2, size - 1):

        @pl.when(jnp.logical_and(chip > k // 2, core == k % 2))
        def _():
            for q in range(blocks):
                pass_copy(k, q).wait_send()

    outgoing(lambda copy: copy.wait_send())

    @pl.when(gives_last)
    def _():
        last_copy.wait_send()

    @pl.when(me == 0)
    def _():
        other_copy.wait_send()


def transfer(kernel, cid, arrays, outs, scratch, spaces, out_spaces):
    return pl.pallas_call(
        kernel,
        out_shape=outs,
        in_specs=[pl.BlockSpec(memory_space=space) for space in spaces],
        out_specs=[pl.BlockSpec(memory_space=space) for space in out_spaces],
        scratch_shapes=scratch,
        compiler_params=pltpu.CompilerParams(collective_id=cid, has_side_effects=True),
    )(*arrays)


def run_phase(kernel, consts, arrays, spaces, outs, out_spaces, scratch):
    specs = [
        pl.BlockSpec(memory_space=SMEM if name in IN_SMEM else VMEM) for name in CONSTS
    ]
    specs += [pl.BlockSpec(memory_space=space) for space in spaces]
    return pl.pallas_call(
        kernel,
        out_shape=outs,
        in_specs=specs,
        out_specs=[pl.BlockSpec(memory_space=space) for space in out_spaces],
        scratch_shapes=scratch,
        compiler_params=pltpu.CompilerParams(vmem_limit_bytes=60 * 1024 * 1024),
    )(*consts, *arrays)


def body(
    coarse_guess,
    initial_state,
    fine_volume,
    coarse_volume,
    lift_matrix,
    wave_speed,
    reaction_rate,
    species_map,
    neighbour_element,
    neighbour_rank,
):
    block, variables, nodes = initial_state.shape
    blocks, rows = lax.axis_size("space"), lax.axis_size("tm")
    faces = lift_matrix.shape[0]
    pair = faces // 3
    packed = (variables * block, nodes)
    state = jax.ShapeDtypeStruct((blocks,) + packed, BF16)
    dma = pltpu.SemaphoreType.DMA
    any_space = pl.ANY
    starts, codes = transfer(
        start_kernel,
        0,
        (
            jnp.transpose(coarse_guess, (0, 2, 1, 3)),
            jnp.transpose(initial_state, (1, 0, 2)),
            neighbour_element,
            neighbour_rank,
        ),
        [state, jax.ShapeDtypeStruct((blocks, 3, block, pair), jnp.int32)],
        [
            VMEM(packed, BF16),
            VMEM(packed, BF16),
            VMEM((3, block, pair), jnp.int32),
            dma((blocks,)),
            dma((blocks,)),
            dma((blocks - 1,)),
            dma((blocks - 1,)),
            dma((blocks - 1,)),
            dma((2,)),
        ],
        [VMEM] * 4,
        [VMEM] * 2,
    )
    consts = (
        jnp.asarray(face_table(SIDE)).astype(BF16),
        codes,
        lift_matrix,
        fine_volume,
        coarse_volume,
        wave_speed,
        reaction_rate,
        jnp.transpose(species_map),
    )
    dims = (variables, blocks * block, nodes)
    scratch = phase_scratch(dims, faces)
    points = (variables, block, nodes)
    message, early = run_phase(
        chain_kernel,
        consts,
        (starts,),
        [VMEM],
        [state, jax.ShapeDtypeStruct((2 * STRIDE,) + points, F32)],
        [VMEM, any_space],
        scratch + [VMEM(dims, F32), VMEM(points, F32), dma(())],
    )
    messages, last, other = transfer(
        spread_kernel,
        1,
        (message, early),
        [
            jax.ShapeDtypeStruct((rows - 2,) + state.shape, BF16),
            jax.ShapeDtypeStruct(packed, BF16),
            jax.ShapeDtypeStruct((STRIDE,) + points, F32),
        ],
        [
            dma((rows // 2, blocks)),
            dma((rows, blocks)),
            dma((rows, blocks)),
            dma(()),
            dma(()),
            dma((2,)),
            dma(()),
        ],
        [VMEM, any_space],
        [VMEM, VMEM, any_space],
    )
    (out,) = run_phase(
        finish_kernel,
        consts,
        (messages, last, early, other),
        [VMEM, VMEM, any_space, any_space],
        [jax.ShapeDtypeStruct((STRIDE,) + points, F32)],
        [VMEM],
        scratch + [dma(())],
    )
    return jnp.transpose(out, (0, 2, 1, 3))


def solution(mesh):
    placed = (
        P("tm", "space", None, None),
        P("space", None, None),
        P(),
        P(),
        P(),
        P(),
        P(),
        P(),
        P("space", None),
        P("space", None),
    )
    return jax.shard_map(
        body, mesh=mesh, in_specs=placed, out_specs=P("tm", "space", None, None), check_vma=False
    )
```

```python
import jax
import jax.numpy as jnp
import numpy as np
from jax import lax
from jax.experimental import pallas as pl
from jax.experimental.pallas import tpu as pltpu
from jax.sharding import PartitionSpec as P

SIDE = 8
STRIDE = 4
COARSE_GAIN = 4.0
VMEM = pltpu.VMEM
SMEM = pltpu.SMEM
MESH = pl.DeviceIdType.MESH
BF16 = jnp.bfloat16
F32 = jnp.float32


def face_table(side):
    plane = side * side
    inner = np.arange(plane)
    first, second = inner // side, inner % side
    last = side - 1
    node_lists = [
        first * plane + second,
        first * plane + last * side + second,
        first * plane + second * side,
        first * plane + second * side + last,
    ]
    table = np.zeros((side**3, 4 * plane), np.float32)
    for f in range(4):
        table[node_lists[f], f * plane + inner] = 1.0
    return table


def find_jumps(c):
    xj, idx, rank, speed = c["xj"], c["idx"], c["rank"], c["speed"]
    variables, elems, nodes = c["a"].shape
    block = c["block"]
    blocks = elems // block
    pair = idx.shape[2]
    picked = jnp.dot(xj[:, 0:nodes], c["table"][...], preferred_element_type=F32)
    low = lax.broadcasted_iota(jnp.int32, (elems, pair), 1) < pair // 2
    for k in range(3):
        spots = [idx[k, s * block : (s + 1) * block, :] for s in range(blocks)]
        offsets = [rank[k, s * block : (s + 1) * block, :] for s in range(blocks)]
        for v in range(variables):
            rows = slice(v * elems, (v + 1) * elems)
            if k == 0:
                faces = jnp.where(
                    low,
                    xj[rows, 0:pair].astype(F32),
                    xj[rows, nodes - pair : nodes].astype(F32),
                )
            else:
                faces = picked[rows, (k - 1) * pair : k * pair]
            own = [faces[s * block : (s + 1) * block] for s in range(blocks)]
            parts = []
            for s in range(blocks):
                before, here, after = [
                    jnp.take_along_axis(
                        own[(s + d) % blocks], spots[s], axis=0, mode="promise_in_bounds"
                    )
                    for d in (-1, 0, 1)
                ]
                across = jnp.where(
                    offsets[s] < 0, before, jnp.where(offsets[s] > 0, after, here)
                )
                parts.append(speed[v] * (across - pltpu.roll(own[s], pair // 2, 1)))
            xj[rows, nodes + k * pair : nodes + (k + 1) * pair] = jnp.concatenate(
                parts, axis=0
            ).astype(BF16)


def transport_react(c, weights, gain, finish):
    a, m, h, gain_ref, loss_ref = c["a"], c["m"], c["h"], c["made"], c["used"]
    species, rates = c["species"], c["rates"]
    variables, elems, nodes = a.shape
    moved = jnp.dot(c["xj"][...], weights[...], preferred_element_type=F32)
    for v in range(variables):
        own = moved[v * elems : (v + 1) * elems]
        a[v] = own
        m[v] = own.astype(BF16)
        h[v] = (own * own + 0.5).astype(BF16)
        zero = jnp.zeros((elems, nodes), BF16)
        gain_ref[v] = zero
        loss_ref[v] = zero
    for r in range(species.shape[1]):
        s0, s1, s2 = species[0, r], species[1, r], species[2, r]
        factor = (rates[r] * gain).astype(BF16)
        rate = factor * (m[s0] * m[s1]) / (h[s0] + h[s1])
        gain_ref[s2] += rate
        loss_ref[s0] += rate
    for v in range(variables):
        finish(v, a[v] + (gain_ref[v].astype(F32) - loss_ref[v].astype(F32)))


def store_x(c, v, new):
    elems, nodes = new.shape
    c["xj"][v * elems : (v + 1) * elems, 0:nodes] = new.astype(BF16)


def fine_substep(c):
    find_jumps(c)

    def finish(v, new):
        c["a"][v] = new
        store_x(c, v, new)

    transport_react(c, c["fine"], 1.0, finish)


def coarse_substep(c, finish):
    find_jumps(c)
    transport_react(c, c["coarse"], COARSE_GAIN, finish)


CONSTS = ("table", "codes", "lift_in", "fine_in", "coarse_in", "speed", "rates", "species")
IN_SMEM = ("speed", "rates", "species")
SCRATCH = ("xj", "a", "idx", "rank", "fine", "coarse", "m", "h", "made", "used")


def phase_scratch(dims, faces):
    variables, elems, nodes = dims
    slab = VMEM(dims, BF16)
    table = VMEM((3, elems, faces // 3), jnp.int32)
    weights = VMEM((nodes + faces, nodes), BF16)
    wide = VMEM((variables * elems, nodes + faces), BF16)
    return [wide, VMEM(dims, F32), table, table, weights, weights, slab, slab, slab, slab]


def begin(refs, count):
    c = dict(zip(CONSTS, refs))
    others = refs[len(CONSTS) : len(CONSTS) + count]
    scratch = refs[len(CONSTS) + count :]
    c.update(zip(SCRATCH, scratch))
    codes = c["codes"]
    blocks, _, block, _ = codes.shape
    c["block"] = block
    for s in range(blocks):
        for k in range(3):
            code = codes[s, k]
            rows = slice(s * block, (s + 1) * block)
            c["idx"][k, rows, :] = lax.rem(code, block)
            c["rank"][k, rows, :] = lax.div(code, block) - 1
    nodes = c["fine_in"].shape[0]
    c["fine"][0:nodes, :] = c["fine_in"][...]
    c["coarse"][0:nodes, :] = c["coarse_in"][...]
    half = c["idx"].shape[2] // 2
    for f in range(6):
        part = c["lift_in"][(f ^ 1) * half : (f ^ 1) * half + half, :]
        c["fine"][nodes + f * half : nodes + (f + 1) * half, :] = part
        c["coarse"][nodes + f * half : nodes + (f + 1) * half, :] = part
    return c, others, scratch[len(SCRATCH) :]


def unpack(ref, v, blocks, block):
    both = [ref[s, v * block : (v + 2) * block, :].astype(F32) for s in range(blocks)]
    return [
        jnp.concatenate([b[w * block : (w + 1) * block] for b in both], axis=0) for w in (0, 1)
    ]


def loop(count, fn):
    def one(i, carry):
        fn(i)
        return carry

    lax.fori_loop(0, count, one, 0)


def pack(values, ref, v, blocks, block):
    for s in range(blocks):
        both = jnp.concatenate([e[s * block : (s + 1) * block] for e in values], axis=0)
        ref[s, v * block : (v + 2) * block, :] = both.astype(BF16)


def chain_kernel(*refs):
    c, (starts, message, relaxed), (corr,) = begin(refs, 3)
    variables, elems, nodes = c["a"].shape
    block = c["block"]
    blocks = elems // block
    here = lax.axis_index("tm")
    for v in range(0, variables, 2):
        for w, part in enumerate(unpack(starts, v, blocks, block)):
            store_x(c, v + w, part)

    def phase(q):
        loop(2 * STRIDE, lambda i: fine_substep(c))

        @pl.when(q == 0)
        def _():
            @pl.when(here == 0)
            def _():
                for v in range(0, variables, 2):
                    pack([c["a"][v], c["a"][v + 1]], relaxed, v, blocks, block)

            def finish(v, new):
                corr[v] = new

            coarse_substep(c, finish)

    loop(2, phase)
    keep = jnp.where(here == 0, 0.0, 1.0)
    for v in range(0, variables, 2):
        ends = [c["a"][v + w] - keep * corr[v + w] for w in (0, 1)]
        pack(ends, message, v, blocks, block)


def finish_kernel(*refs):
    c, (messages, last, out), _ = begin(refs, 3)
    variables, elems, nodes = c["a"].shape
    block = c["block"]
    blocks = elems // block
    here, own = lax.axis_index("tm"), lax.axis_index("space")
    mine = pl.ds(pl.multiple_of(own * block, block), block)
    for v in range(0, variables, 2):
        for w, part in enumerate(unpack(messages.at[0], v, blocks, block)):
            store_x(c, v + w, part)
        both = last[v * block : (v + 2) * block, :].astype(F32)
        for w in (0, 1):
            out[STRIDE - 1, v + w] = both[w * block : (w + 1) * block]

    def advance(i):
        terms = {}

        def finish(v, new):
            if v % 2 == 0:
                terms[v], terms[v + 1] = unpack(messages.at[i + 1], v, blocks, block)
            store_x(c, v, new + terms[v])

        coarse_substep(c, finish)

    loop(here - 2, advance)

    @pl.when(here >= 2)
    def _():
        def keep(v, new):
            c["a"][v] = new

        coarse_substep(c, keep)
        for v in range(variables):
            out[STRIDE - 1, v] += c["a"][v, mine, :]

    def fine(i):
        fine_substep(c)

        @pl.when(i % 2 == 1)
        def _():
            out[i // 2] = c["a"][:, mine, :]

    loop(2 * (STRIDE - 1), fine)


def remote(src, dst, send, recv, target):
    return pltpu.make_async_remote_copy(
        src_ref=src,
        dst_ref=dst,
        send_sem=send,
        recv_sem=recv,
        device_id=target,
        device_id_type=MESH,
    )


def start_kernel(
    guess, initial, element, rank, starts, codes, mine, code, send, recv, code_send, code_recv, local
):
    me, size = lax.axis_index("space"), lax.axis_size("space")
    here, rows = lax.axis_index("tm"), lax.axis_size("tm")
    variables, block, _ = initial.shape
    lanes = code.shape[2]
    value = element[...] + block * (rank[...] + 1)
    low = lax.broadcasted_iota(jnp.int32, (block, lanes), 1) < lanes // 2
    for k in range(3):
        code[k] = jnp.where(low, value[:, 2 * k + 1 : 2 * k + 2], value[:, 2 * k : 2 * k + 1])

    def take(ref):
        for v in range(0, variables, 2):
            both = jnp.concatenate([ref[v], ref[v + 1]], axis=0)
            mine[v * block : (v + 2) * block, :] = both.astype(BF16)

    @pl.when(here == 0)
    def _():
        take(initial)

    @pl.when(here > 0)
    def _():
        take(guess.at[0])

    stays = here <= rows - 5
    moves = jnp.logical_and(here >= rows - 4, here <= rows - 2)
    comes = jnp.logical_or(here == rows - 4, here >= rows - 2)
    target = jnp.where(here == rows - 2, rows - 4, lax.rem(here + 2, rows))
    source = jnp.where(here == rows - 4, rows - 2, lax.rem(here + rows - 2, rows))

    def mate(row, d):
        return {"tm": row, "space": lax.rem(me + d, size)}

    barrier = pltpu.get_barrier_semaphore()
    for d in range(1, size):
        pl.semaphore_signal(barrier, inc=1, device_id=mate(here, d), device_id_type=MESH)

    @pl.when(comes)
    def _():
        for d in range(size):
            pl.semaphore_signal(barrier, inc=1, device_id=mate(source, d), device_id_type=MESH)

    pl.semaphore_wait(barrier, size - 1 + size * moves.astype(jnp.int32))

    def code_copy(d):
        return remote(code, codes.at[me], code_send.at[d], code_recv.at[d], mate(here, d))

    def stay_copy(d):
        return remote(mine, starts.at[me], send.at[d], recv.at[d], mate(here, d))

    def move_copy(d):
        return remote(mine, starts.at[me], send.at[d], recv.at[d], mate(target, d))

    keep_code = pltpu.make_async_copy(code, codes.at[me], local.at[0])
    keep_mine = pltpu.make_async_copy(mine, starts.at[me], local.at[1])

    @pl.when(stays)
    def _():
        for d in range(1, size):
            stay_copy(d).start()
        keep_mine.start()

    @pl.when(moves)
    def _():
        for d in range(size):
            move_copy(d).start()

    for d in range(1, size):
        code_copy(d).start()
    keep_code.start()
    keep_code.wait()

    @pl.when(stays)
    def _():
        keep_mine.wait()
        for d in range(1, size):
            stay_copy(d).wait_recv()

    @pl.when(comes)
    def _():
        for d in range(size):
            move_copy(d).wait_recv()

    for d in range(1, size):
        code_copy(d).wait_recv()

    @pl.when(stays)
    def _():
        for d in range(1, size):
            stay_copy(d).wait_send()

    @pl.when(moves)
    def _():
        for d in range(size):
            move_copy(d).wait_send()

    for d in range(1, size):
        code_copy(d).wait_send()


def tree(chips, source):
    if chips == 4:
        return ({1: 0, 2: 0, 3: 2}, {3: 1, 2: 3})[source]
    return {chip: source for chip in range(source + 1, chips)}


def spread_kernel(
    message,
    relaxed,
    starts,
    messages,
    last,
    send,
    pass_send,
    recv,
    last_send,
    last_recv,
    local,
):
    me, size = lax.axis_index("tm"), lax.axis_size("tm")
    own = lax.axis_index("space")
    chip, core = me // 2, me % 2
    blocks = message.shape[0]
    chips = size // 2
    sibling = me + 1 - 2 * core
    barrier = pltpu.get_barrier_semaphore()
    for d in range(1, size):
        mate = {"tm": lax.rem(me + d, size), "space": own}
        pl.semaphore_signal(barrier, inc=1, device_id=mate, device_id_type=MESH)
    pl.semaphore_wait(barrier, size - 1)

    def copy(src, k, q, sem, target):
        return remote(
            src.at[q],
            messages.at[k, q],
            sem,
            recv.at[k, q],
            {"tm": target, "space": own},
        )

    def hop(k, q, child, first):
        src = message if first else messages.at[k]
        return copy(src, k, q, send.at[k, child, q], 2 * child + k % 2)

    def side(k, q, src, target):
        return copy(src, k, q, pass_send.at[k, q], target)

    def pair_first(act):
        @pl.when(me == 0)
        def _():
            for q in range(blocks):
                act(side(0, q, relaxed, 1))

        @pl.when(me == size - 2)
        def _():
            for q in range(blocks):
                act(side(size - 4, q, message, size - 1))

    back = jnp.where(
        me == size - 4,
        size - 1,
        jnp.where(me >= size - 2, lax.rem(me + size - 1, size), lax.rem(me + 1, size)),
    )
    last_copy = remote(
        message.at[own], last, last_send, last_recv, {"tm": back, "space": own}
    )

    for k in range(size - 4):

        @pl.when(me == k)
        def _():
            for q in range(blocks):
                for child, parent in tree(chips, k // 2).items():
                    if parent == k // 2:
                        hop(k, q, child, True).start()

    pair_first(lambda c: c.start())

    @pl.when(me != size - 3)
    def _():
        last_copy.start()

    def local_copy(src, dst):
        keep = pltpu.make_async_copy(src, dst, local)
        keep.start()
        keep.wait()

    @pl.when(me == 0)
    def _():
        local_copy(starts, messages.at[0])
        local_copy(relaxed.at[own], last)

    @pl.when(me == size - 2)
    def _():
        local_copy(message, messages.at[size - 4])

    @pl.when(me == size - 1)
    def _():
        local_copy(message, messages.at[size - 3])

    def needs(device, k):
        return k <= device - 2

    for c in range(1, chips):
        for w in (0, 1):

            @pl.when(me == 2 * c + w)
            def _():
                order = [k for k in range(size - 4) if k // 2 < c and k % 2 == w]
                order.sort(key=lambda k: tree(chips, k // 2)[c] != k // 2)
                for q in range(blocks):
                    for k in order:
                        hop(k, q, c, True).wait_recv()
                        for child, parent in tree(chips, k // 2).items():
                            if parent == c:
                                hop(k, q, child, False).start()
                        if needs(2 * c + 1 - w, k):
                            side(k, q, messages.at[k], sibling).start()
                for q in range(blocks):
                    for k in range(size - 4):
                        if k // 2 < c and k % 2 != w and needs(2 * c + w, k):
                            side(k, q, messages.at[k], sibling).wait_recv()

    @pl.when(me == 1)
    def _():
        for q in range(blocks):
            side(0, q, relaxed, 1).wait_recv()

    @pl.when(me == size - 1)
    def _():
        for q in range(blocks):
            side(size - 4, q, message, size - 1).wait_recv()

    @pl.when(me >= 1)
    def _():
        last_copy.wait_recv()

    for k in range(size - 4):

        @pl.when(me == k)
        def _():
            for q in range(blocks):
                for child, parent in tree(chips, k // 2).items():
                    if parent == k // 2:
                        hop(k, q, child, True).wait_send()

    pair_first(lambda c: c.wait_send())

    @pl.when(me != size - 3)
    def _():
        last_copy.wait_send()

    for c in range(1, chips):
        for w in (0, 1):

            @pl.when(me == 2 * c + w)
            def _():
                for q in range(blocks):
                    for k in range(size - 4):
                        if k // 2 < c and k % 2 == w:
                            for child, parent in tree(chips, k // 2).items():
                                if parent == c:
                                    hop(k, q, child, False).wait_send()
                            if needs(2 * c + 1 - w, k):
                                side(k, q, messages.at[k], sibling).wait_send()


def transfer(kernel, cid, arrays, outs, scratch):
    return pl.pallas_call(
        kernel,
        out_shape=outs,
        in_specs=[pl.BlockSpec(memory_space=VMEM)] * len(arrays),
        out_specs=[pl.BlockSpec(memory_space=VMEM)] * len(outs),
        scratch_shapes=scratch,
        compiler_params=pltpu.CompilerParams(collective_id=cid, has_side_effects=True),
    )(*arrays)


def run_phase(kernel, consts, arrays, outs, scratch):
    specs = [
        pl.BlockSpec(memory_space=SMEM if name in IN_SMEM else VMEM) for name in CONSTS
    ]
    return pl.pallas_call(
        kernel,
        out_shape=outs,
        in_specs=specs + [pl.BlockSpec(memory_space=VMEM)] * len(arrays),
        out_specs=[pl.BlockSpec(memory_space=VMEM)] * len(outs),
        scratch_shapes=scratch,
        compiler_params=pltpu.CompilerParams(vmem_limit_bytes=60 * 1024 * 1024),
    )(*consts, *arrays)


def body(
    coarse_guess,
    initial_state,
    fine_volume,
    coarse_volume,
    lift_matrix,
    wave_speed,
    reaction_rate,
    species_map,
    neighbour_element,
    neighbour_rank,
):
    block, variables, nodes = initial_state.shape
    blocks, rows = lax.axis_size("space"), lax.axis_size("tm")
    faces = lift_matrix.shape[0]
    pair = faces // 3
    packed = (variables * block, nodes)
    state = jax.ShapeDtypeStruct((blocks,) + packed, BF16)
    dma = pltpu.SemaphoreType.DMA
    starts, codes = transfer(
        start_kernel,
        0,
        (
            jnp.transpose(coarse_guess, (0, 2, 1, 3)),
            jnp.transpose(initial_state, (1, 0, 2)),
            neighbour_element,
            neighbour_rank,
        ),
        [state, jax.ShapeDtypeStruct((blocks, 3, block, pair), jnp.int32)],
        [
            VMEM(packed, BF16),
            VMEM((3, block, pair), jnp.int32),
            dma((blocks,)),
            dma((blocks,)),
            dma((blocks,)),
            dma((blocks,)),
            dma((2,)),
        ],
    )
    consts = (
        jnp.asarray(face_table(SIDE)).astype(BF16),
        codes,
        lift_matrix,
        fine_volume,
        coarse_volume,
        wave_speed,
        reaction_rate,
        jnp.transpose(species_map),
    )
    dims = (variables, blocks * block, nodes)
    scratch = phase_scratch(dims, faces)
    message, relaxed = run_phase(
        chain_kernel, consts, (starts,), [state, state], scratch + [VMEM(dims, F32)]
    )
    messages, last = transfer(
        spread_kernel,
        1,
        (message, relaxed, starts),
        [
            jax.ShapeDtypeStruct((rows - 2,) + state.shape, BF16),
            jax.ShapeDtypeStruct(packed, BF16),
        ],
        [
            dma((rows - 4, rows // 2, blocks)),
            dma((rows - 2, blocks)),
            dma((rows - 2, blocks)),
            dma(()),
            dma(()),
            dma(()),
        ],
    )
    (out,) = run_phase(
        finish_kernel,
        consts,
        (messages, last),
        [jax.ShapeDtypeStruct((STRIDE, variables, block, nodes), F32)],
        scratch,
    )
    return jnp.transpose(out, (0, 2, 1, 3))


def solution(mesh):
    placed = (
        P("tm", "space", None, None),
        P("space", None, None),
        P(),
        P(),
        P(),
        P(),
        P(),
        P(),
        P("space", None),
        P("space", None),
    )
    return jax.shard_map(
        body, mesh=mesh, in_specs=placed, out_specs=P("tm", "space", None, None), check_vma=False
    )
```

```python
import jax
import jax.numpy as jnp
import numpy as np
from jax import lax
from jax.experimental import pallas as pl
from jax.experimental.pallas import tpu as pltpu
from jax.sharding import PartitionSpec as P

SIDE = 8
STRIDE = 4
COARSE_GAIN = 4.0
WINDOW = 2
VMEM = pltpu.VMEM
SMEM = pltpu.SMEM
MESH = pl.DeviceIdType.MESH
BF16 = jnp.bfloat16
F32 = jnp.float32


def face_table(side):
    plane = side * side
    inner = np.arange(plane)
    first, second = inner // side, inner % side
    last = side - 1
    node_lists = [
        first * plane + second,
        first * plane + last * side + second,
        first * plane + second * side,
        first * plane + second * side + last,
    ]
    table = np.zeros((side**3, 4 * plane), np.float32)
    for f in range(4):
        table[node_lists[f], f * plane + inner] = 1.0
    return table


def find_jumps(c):
    xj, idx, rank, speed = c["xj"], c["idx"], c["rank"], c["speed"]
    variables, elems, nodes = c["a"].shape
    block = c["block"]
    blocks = elems // block
    pair = idx.shape[2]
    picked = jnp.dot(xj[:, 0:nodes], c["table"][...], preferred_element_type=F32)
    low = lax.broadcasted_iota(jnp.int32, (elems, pair), 1) < pair // 2
    for k in range(3):
        spots = [idx[k, s * block : (s + 1) * block, :] for s in range(blocks)]
        offsets = [rank[k, s * block : (s + 1) * block, :] for s in range(blocks)]
        for v in range(variables):
            rows = slice(v * elems, (v + 1) * elems)
            if k == 0:
                faces = jnp.where(
                    low,
                    xj[rows, 0:pair].astype(F32),
                    xj[rows, nodes - pair : nodes].astype(F32),
                )
            else:
                faces = picked[rows, (k - 1) * pair : k * pair]
            own = [faces[s * block : (s + 1) * block] for s in range(blocks)]
            parts = []
            for s in range(blocks):
                before, here, after = [
                    jnp.take_along_axis(
                        own[(s + d) % blocks], spots[s], axis=0, mode="promise_in_bounds"
                    )
                    for d in (-1, 0, 1)
                ]
                across = jnp.where(
                    offsets[s] < 0, before, jnp.where(offsets[s] > 0, after, here)
                )
                parts.append(speed[v] * (across - pltpu.roll(own[s], pair // 2, 1)))
            xj[rows, nodes + k * pair : nodes + (k + 1) * pair] = jnp.concatenate(
                parts, axis=0
            ).astype(BF16)


def transport_react(c, weights, gain, finish):
    a, m, h, gain_ref, loss_ref = c["a"], c["m"], c["h"], c["made"], c["used"]
    species, rates = c["species"], c["rates"]
    variables, elems, nodes = a.shape
    moved = jnp.dot(c["xj"][...], weights[...], preferred_element_type=F32)
    for v in range(variables):
        own = moved[v * elems : (v + 1) * elems]
        a[v] = own
        m[v] = own.astype(BF16)
        h[v] = (own * own + 0.5).astype(BF16)
        zero = jnp.zeros((elems, nodes), BF16)
        gain_ref[v] = zero
        loss_ref[v] = zero
    for r in range(species.shape[1]):
        s0, s1, s2 = species[0, r], species[1, r], species[2, r]
        factor = (rates[r] * gain).astype(BF16)
        rate = factor * (m[s0] * m[s1]) / (h[s0] + h[s1])
        gain_ref[s2] += rate
        loss_ref[s0] += rate
    for v in range(variables):
        finish(v, a[v] + (gain_ref[v].astype(F32) - loss_ref[v].astype(F32)))


def store_x(c, v, new):
    elems, nodes = new.shape
    c["xj"][v * elems : (v + 1) * elems, 0:nodes] = new.astype(BF16)


def fine_substep(c):
    find_jumps(c)

    def finish(v, new):
        c["a"][v] = new
        store_x(c, v, new)

    transport_react(c, c["fine"], 1.0, finish)


def coarse_substep(c, finish):
    find_jumps(c)
    transport_react(c, c["coarse"], COARSE_GAIN, finish)


CONSTS = ("table", "codes", "lift_in", "fine_in", "coarse_in", "speed", "rates", "species")
IN_SMEM = ("speed", "rates", "species")
SCRATCH = ("xj", "a", "idx", "rank", "fine", "coarse", "m", "h", "made", "used")


def phase_scratch(dims, faces):
    variables, elems, nodes = dims
    slab = VMEM(dims, BF16)
    table = VMEM((3, elems, faces // 3), jnp.int32)
    weights = VMEM((nodes + faces, nodes), BF16)
    wide = VMEM((variables * elems, nodes + faces), BF16)
    return [wide, VMEM(dims, F32), table, table, weights, weights, slab, slab, slab, slab]


def begin(refs, count):
    c = dict(zip(CONSTS, refs))
    others = refs[len(CONSTS) : len(CONSTS) + count]
    scratch = refs[len(CONSTS) + count :]
    c.update(zip(SCRATCH, scratch))
    codes = c["codes"]
    blocks, _, block, _ = codes.shape
    c["block"] = block
    for s in range(blocks):
        for k in range(3):
            code = codes[s, k]
            rows = slice(s * block, (s + 1) * block)
            c["idx"][k, rows, :] = lax.rem(code, block)
            c["rank"][k, rows, :] = lax.div(code, block) - 1
    nodes = c["fine_in"].shape[0]
    c["fine"][0:nodes, :] = c["fine_in"][...]
    c["coarse"][0:nodes, :] = c["coarse_in"][...]
    half = c["idx"].shape[2] // 2
    for f in range(6):
        part = c["lift_in"][(f ^ 1) * half : (f ^ 1) * half + half, :]
        c["fine"][nodes + f * half : nodes + (f + 1) * half, :] = part
        c["coarse"][nodes + f * half : nodes + (f + 1) * half, :] = part
    return c, others, scratch[len(SCRATCH) :]


def unpack(ref, v, blocks, block):
    both = [ref[s, v * block : (v + 2) * block, :].astype(F32) for s in range(blocks)]
    return [
        jnp.concatenate([b[w * block : (w + 1) * block] for b in both], axis=0) for w in (0, 1)
    ]


def loop(count, fn):
    def one(i, carry):
        fn(i)
        return carry

    lax.fori_loop(0, count, one, 0)


def pack(values, ref, v, blocks, block):
    for s in range(blocks):
        both = jnp.concatenate([e[s * block : (s + 1) * block] for e in values], axis=0)
        ref[s, v * block : (v + 2) * block, :] = both.astype(BF16)


def chain_kernel(*refs):
    c, (starts, message, relaxed), (corr,) = begin(refs, 3)
    variables, elems, nodes = c["a"].shape
    block = c["block"]
    blocks = elems // block
    here = lax.axis_index("tm")
    for v in range(0, variables, 2):
        for w, part in enumerate(unpack(starts, v, blocks, block)):
            store_x(c, v + w, part)

    def phase(q):
        loop(2 * STRIDE, lambda i: fine_substep(c))

        @pl.when(q == 0)
        def _():
            @pl.when(here == 0)
            def _():
                for v in range(0, variables, 2):
                    pack([c["a"][v], c["a"][v + 1]], relaxed, v, blocks, block)

            def finish(v, new):
                corr[v] = new

            coarse_substep(c, finish)

    loop(2, phase)
    keep = jnp.where(here == 0, 0.0, 1.0)
    for v in range(0, variables, 2):
        ends = [c["a"][v + w] - keep * corr[v + w] for w in (0, 1)]
        pack(ends, message, v, blocks, block)


def finish_kernel(*refs):
    c, (messages, last, out), _ = begin(refs, 3)
    variables, elems, nodes = c["a"].shape
    block = c["block"]
    blocks = elems // block
    here, own = lax.axis_index("tm"), lax.axis_index("space")
    mine = pl.ds(pl.multiple_of(own * block, block), block)
    for v in range(0, variables, 2):
        for w, part in enumerate(unpack(messages.at[0], v, blocks, block)):
            store_x(c, v + w, part)
        both = last[v * block : (v + 2) * block, :].astype(F32)
        for w in (0, 1):
            out[STRIDE - 1, v + w] = both[w * block : (w + 1) * block]

    def advance(i):
        terms = {}

        def finish(v, new):
            if v % 2 == 0:
                terms[v], terms[v + 1] = unpack(messages.at[i + 1], v, blocks, block)
            store_x(c, v, new + terms[v])

        coarse_substep(c, finish)

    loop(here - 2, advance)

    @pl.when(here >= 2)
    def _():
        def keep(v, new):
            c["a"][v] = new

        coarse_substep(c, keep)
        for v in range(variables):
            out[STRIDE - 1, v] += c["a"][v, mine, :]

    def fine(i):
        fine_substep(c)

        @pl.when(i % 2 == 1)
        def _():
            out[i // 2] = c["a"][:, mine, :]

    loop(2 * (STRIDE - 1), fine)


def remote(src, dst, send, recv, target):
    return pltpu.make_async_remote_copy(
        src_ref=src,
        dst_ref=dst,
        send_sem=send,
        recv_sem=recv,
        device_id=target,
        device_id_type=MESH,
    )


def start_kernel(
    guess, initial, element, rank, starts, codes, mine, code, send, recv, code_send, code_recv, local
):
    me, size = lax.axis_index("space"), lax.axis_size("space")
    here, rows = lax.axis_index("tm"), lax.axis_size("tm")
    variables, block, _ = initial.shape
    lanes = code.shape[2]
    value = element[...] + block * (rank[...] + 1)
    low = lax.broadcasted_iota(jnp.int32, (block, lanes), 1) < lanes // 2
    for k in range(3):
        code[k] = jnp.where(low, value[:, 2 * k + 1 : 2 * k + 2], value[:, 2 * k : 2 * k + 1])

    def take(ref):
        for v in range(0, variables, 2):
            both = jnp.concatenate([ref[v], ref[v + 1]], axis=0)
            mine[v * block : (v + 2) * block, :] = both.astype(BF16)

    @pl.when(here == 0)
    def _():
        take(initial)

    @pl.when(here > 0)
    def _():
        take(guess.at[0])

    stays = here <= rows - 5
    moves = jnp.logical_and(here >= rows - 4, here <= rows - 2)
    comes = jnp.logical_or(here == rows - 4, here >= rows - 2)
    target = jnp.where(here == rows - 2, rows - 4, lax.rem(here + 2, rows))
    source = jnp.where(here == rows - 4, rows - 2, lax.rem(here + rows - 2, rows))

    def mate(row, d):
        return {"tm": row, "space": lax.rem(me + d, size)}

    barrier = pltpu.get_barrier_semaphore()
    for d in range(1, size):
        pl.semaphore_signal(barrier, inc=1, device_id=mate(here, d), device_id_type=MESH)

    @pl.when(comes)
    def _():
        for d in range(size):
            pl.semaphore_signal(barrier, inc=1, device_id=mate(source, d), device_id_type=MESH)

    pl.semaphore_wait(barrier, size - 1 + size * moves.astype(jnp.int32))

    def code_copy(d):
        return remote(code, codes.at[me], code_send.at[d], code_recv.at[d], mate(here, d))

    def stay_copy(d):
        return remote(mine, starts.at[me], send.at[d], recv.at[d], mate(here, d))

    def move_copy(d):
        return remote(mine, starts.at[me], send.at[d], recv.at[d], mate(target, d))

    keep_code = pltpu.make_async_copy(code, codes.at[me], local.at[0])
    keep_mine = pltpu.make_async_copy(mine, starts.at[me], local.at[1])

    @pl.when(stays)
    def _():
        for d in range(1, size):
            stay_copy(d).start()
        keep_mine.start()

    @pl.when(moves)
    def _():
        for d in range(size):
            move_copy(d).start()

    for d in range(1, size):
        code_copy(d).start()
    keep_code.start()
    keep_code.wait()

    @pl.when(stays)
    def _():
        keep_mine.wait()
        for d in range(1, size):
            stay_copy(d).wait_recv()

    @pl.when(comes)
    def _():
        for d in range(size):
            move_copy(d).wait_recv()

    for d in range(1, size):
        code_copy(d).wait_recv()

    @pl.when(stays)
    def _():
        for d in range(1, size):
            stay_copy(d).wait_send()

    @pl.when(moves)
    def _():
        for d in range(size):
            move_copy(d).wait_send()

    for d in range(1, size):
        code_copy(d).wait_send()


def tree(chips, source):
    if chips == 4:
        return ({1: 0, 2: 0, 3: 2}, {3: 1, 2: 3})[source]
    return {chip: source for chip in range(source + 1, chips)}


def spread_kernel(
    message,
    relaxed,
    starts,
    messages,
    last,
    send,
    pass_send,
    recv,
    last_send,
    last_recv,
    local,
):
    me, size = lax.axis_index("tm"), lax.axis_size("tm")
    own = lax.axis_index("space")
    chip, core = me // 2, me % 2
    blocks = message.shape[0]
    chips = size // 2
    sibling = me + 1 - 2 * core
    barrier = pltpu.get_barrier_semaphore()
    for d in range(1, size):
        mate = {"tm": lax.rem(me + d, size), "space": own}
        pl.semaphore_signal(barrier, inc=1, device_id=mate, device_id_type=MESH)
    pl.semaphore_wait(barrier, size - 1)

    def copy(src, k, q, sem, target):
        return remote(
            src.at[q],
            messages.at[k, q],
            sem,
            recv.at[k, q],
            {"tm": target, "space": own},
        )

    def hop(k, q, child, first):
        src = message if first else messages.at[k]
        return copy(src, k, q, send.at[k, child, q], 2 * child + k % 2)

    def side(k, q, src, target):
        return copy(src, k, q, pass_send.at[k, q], target)

    def pair_first(act):
        @pl.when(me == 0)
        def _():
            for q in range(blocks):
                act(side(0, q, relaxed, 1))

        @pl.when(me == size - 2)
        def _():
            for q in range(blocks):
                act(side(size - 4, q, message, size - 1))

    back = jnp.where(
        me == size - 4,
        size - 1,
        jnp.where(me >= size - 2, lax.rem(me + size - 1, size), lax.rem(me + 1, size)),
    )
    last_copy = remote(
        message.at[own], last, last_send, last_recv, {"tm": back, "space": own}
    )

    pair_first(lambda c: c.start())

    @pl.when(me != size - 3)
    def _():
        last_copy.start()

    for k in range(size - 4):

        @pl.when(me == k)
        def _():
            for q in range(blocks):
                for child, parent in tree(chips, k // 2).items():
                    if parent == k // 2:
                        if q >= WINDOW:
                            hop(k, q - WINDOW, child, True).wait_send()
                        hop(k, q, child, True).start()

    def local_copy(src, dst):
        keep = pltpu.make_async_copy(src, dst, local)
        keep.start()
        keep.wait()

    @pl.when(me == 0)
    def _():
        local_copy(starts, messages.at[0])
        local_copy(relaxed.at[own], last)

    @pl.when(me == size - 2)
    def _():
        local_copy(message, messages.at[size - 4])

    @pl.when(me == size - 1)
    def _():
        local_copy(message, messages.at[size - 3])

    def needs(device, k):
        return k <= device - 2

    for c in range(1, chips):
        for w in (0, 1):

            @pl.when(me == 2 * c + w)
            def _():
                order = [k for k in range(size - 4) if k // 2 < c and k % 2 == w]
                order.sort(key=lambda k: tree(chips, k // 2)[c] != k // 2)
                for q in range(blocks):
                    for k in order:
                        hop(k, q, c, True).wait_recv()
                        for child, parent in tree(chips, k // 2).items():
                            if parent == c:
                                hop(k, q, child, False).start()
                        if needs(2 * c + 1 - w, k):
                            side(k, q, messages.at[k], sibling).start()
                for q in range(blocks):
                    for k in range(size - 4):
                        if k // 2 < c and k % 2 != w and needs(2 * c + w, k):
                            side(k, q, messages.at[k], sibling).wait_recv()

    @pl.when(me == 1)
    def _():
        for q in range(blocks):
            side(0, q, relaxed, 1).wait_recv()

    @pl.when(me == size - 1)
    def _():
        for q in range(blocks):
            side(size - 4, q, message, size - 1).wait_recv()

    @pl.when(me >= 1)
    def _():
        last_copy.wait_recv()

    for k in range(size - 4):

        @pl.when(me == k)
        def _():
            for q in range(blocks - WINDOW, blocks):
                for child, parent in tree(chips, k // 2).items():
                    if parent == k // 2:
                        hop(k, q, child, True).wait_send()

    pair_first(lambda c: c.wait_send())

    @pl.when(me != size - 3)
    def _():
        last_copy.wait_send()

    for c in range(1, chips):
        for w in (0, 1):

            @pl.when(me == 2 * c + w)
            def _():
                for q in range(blocks):
                    for k in range(size - 4):
                        if k // 2 < c and k % 2 == w:
                            for child, parent in tree(chips, k // 2).items():
                                if parent == c:
                                    hop(k, q, child, False).wait_send()
                            if needs(2 * c + 1 - w, k):
                                side(k, q, messages.at[k], sibling).wait_send()


def transfer(kernel, cid, arrays, outs, scratch):
    return pl.pallas_call(
        kernel,
        out_shape=outs,
        in_specs=[pl.BlockSpec(memory_space=VMEM)] * len(arrays),
        out_specs=[pl.BlockSpec(memory_space=VMEM)] * len(outs),
        scratch_shapes=scratch,
        compiler_params=pltpu.CompilerParams(collective_id=cid, has_side_effects=True),
    )(*arrays)


def run_phase(kernel, consts, arrays, outs, scratch):
    specs = [
        pl.BlockSpec(memory_space=SMEM if name in IN_SMEM else VMEM) for name in CONSTS
    ]
    return pl.pallas_call(
        kernel,
        out_shape=outs,
        in_specs=specs + [pl.BlockSpec(memory_space=VMEM)] * len(arrays),
        out_specs=[pl.BlockSpec(memory_space=VMEM)] * len(outs),
        scratch_shapes=scratch,
        compiler_params=pltpu.CompilerParams(vmem_limit_bytes=60 * 1024 * 1024),
    )(*consts, *arrays)


def body(
    coarse_guess,
    initial_state,
    fine_volume,
    coarse_volume,
    lift_matrix,
    wave_speed,
    reaction_rate,
    species_map,
    neighbour_element,
    neighbour_rank,
):
    block, variables, nodes = initial_state.shape
    blocks, rows = lax.axis_size("space"), lax.axis_size("tm")
    faces = lift_matrix.shape[0]
    pair = faces // 3
    packed = (variables * block, nodes)
    state = jax.ShapeDtypeStruct((blocks,) + packed, BF16)
    dma = pltpu.SemaphoreType.DMA
    starts, codes = transfer(
        start_kernel,
        0,
        (
            jnp.transpose(coarse_guess, (0, 2, 1, 3)),
            jnp.transpose(initial_state, (1, 0, 2)),
            neighbour_element,
            neighbour_rank,
        ),
        [state, jax.ShapeDtypeStruct((blocks, 3, block, pair), jnp.int32)],
        [
            VMEM(packed, BF16),
            VMEM((3, block, pair), jnp.int32),
            dma((blocks,)),
            dma((blocks,)),
            dma((blocks,)),
            dma((blocks,)),
            dma((2,)),
        ],
    )
    consts = (
        jnp.asarray(face_table(SIDE)).astype(BF16),
        codes,
        lift_matrix,
        fine_volume,
        coarse_volume,
        wave_speed,
        reaction_rate,
        jnp.transpose(species_map),
    )
    dims = (variables, blocks * block, nodes)
    scratch = phase_scratch(dims, faces)
    message, relaxed = run_phase(
        chain_kernel, consts, (starts,), [state, state], scratch + [VMEM(dims, F32)]
    )
    messages, last = transfer(
        spread_kernel,
        1,
        (message, relaxed, starts),
        [
            jax.ShapeDtypeStruct((rows - 2,) + state.shape, BF16),
            jax.ShapeDtypeStruct(packed, BF16),
        ],
        [
            dma((rows - 4, rows // 2, blocks)),
            dma((rows - 2, blocks)),
            dma((rows - 2, blocks)),
            dma(()),
            dma(()),
            dma(()),
        ],
    )
    (out,) = run_phase(
        finish_kernel,
        consts,
        (messages, last),
        [jax.ShapeDtypeStruct((STRIDE, variables, block, nodes), F32)],
        scratch,
    )
    return jnp.transpose(out, (0, 2, 1, 3))


def solution(mesh):
    placed = (
        P("tm", "space", None, None),
        P("space", None, None),
        P(),
        P(),
        P(),
        P(),
        P(),
        P(),
        P("space", None),
        P("space", None),
    )
    return jax.shard_map(
        body, mesh=mesh, in_specs=placed, out_specs=P("tm", "space", None, None), check_vma=False
    )
```

```python
import jax
import jax.numpy as jnp
import numpy as np
from jax import lax
from jax.experimental import pallas as pl
from jax.experimental.pallas import tpu as pltpu
from jax.sharding import PartitionSpec as P

SIDE = 8
STRIDE = 4
COARSE_GAIN = 4.0
WINDOW = 2
VMEM = pltpu.VMEM
SMEM = pltpu.SMEM
MESH = pl.DeviceIdType.MESH
BF16 = jnp.bfloat16
F32 = jnp.float32


def face_table(side):
    plane = side * side
    inner = np.arange(plane)
    first, second = inner // side, inner % side
    last = side - 1
    node_lists = [
        first * plane + second,
        first * plane + last * side + second,
        first * plane + second * side,
        first * plane + second * side + last,
    ]
    table = np.zeros((side**3, 4 * plane), np.float32)
    for f in range(4):
        table[node_lists[f], f * plane + inner] = 1.0
    return table


def find_jumps(c):
    xj, idx, rank, speed = c["xj"], c["idx"], c["rank"], c["speed"]
    variables, elems, nodes = c["a"].shape
    block = c["block"]
    blocks = elems // block
    pair = idx.shape[2]
    picked = jnp.dot(xj[:, 0:nodes], c["table"][...], preferred_element_type=F32)
    low = lax.broadcasted_iota(jnp.int32, (elems, pair), 1) < pair // 2
    for k in range(3):
        spots = [idx[k, s * block : (s + 1) * block, :] for s in range(blocks)]
        offsets = [rank[k, s * block : (s + 1) * block, :] for s in range(blocks)]
        for v in range(variables):
            rows = slice(v * elems, (v + 1) * elems)
            if k == 0:
                faces = jnp.where(
                    low,
                    xj[rows, 0:pair].astype(F32),
                    xj[rows, nodes - pair : nodes].astype(F32),
                )
            else:
                faces = picked[rows, (k - 1) * pair : k * pair]
            own = [faces[s * block : (s + 1) * block] for s in range(blocks)]
            parts = []
            for s in range(blocks):
                before, here, after = [
                    jnp.take_along_axis(
                        own[(s + d) % blocks], spots[s], axis=0, mode="promise_in_bounds"
                    )
                    for d in (-1, 0, 1)
                ]
                across = jnp.where(
                    offsets[s] < 0, before, jnp.where(offsets[s] > 0, after, here)
                )
                parts.append(speed[v] * (across - pltpu.roll(own[s], pair // 2, 1)))
            xj[rows, nodes + k * pair : nodes + (k + 1) * pair] = jnp.concatenate(
                parts, axis=0
            ).astype(BF16)


def transport_react(c, weights, gain, finish):
    a, m, h, gain_ref, loss_ref = c["a"], c["m"], c["h"], c["made"], c["used"]
    species, rates = c["species"], c["rates"]
    variables, elems, nodes = a.shape
    moved = jnp.dot(c["xj"][...], weights[...], preferred_element_type=F32)
    for v in range(variables):
        own = moved[v * elems : (v + 1) * elems]
        a[v] = own
        m[v] = own.astype(BF16)
        h[v] = (own * own + 0.5).astype(BF16)
        zero = jnp.zeros((elems, nodes), BF16)
        gain_ref[v] = zero
        loss_ref[v] = zero
    for r in range(species.shape[1]):
        s0, s1, s2 = species[0, r], species[1, r], species[2, r]
        factor = (rates[r] * gain).astype(BF16)
        rate = factor * (m[s0] * m[s1]) / (h[s0] + h[s1])
        gain_ref[s2] += rate
        loss_ref[s0] += rate
    for v in range(variables):
        finish(v, a[v] + (gain_ref[v].astype(F32) - loss_ref[v].astype(F32)))


def store_x(c, v, new):
    elems, nodes = new.shape
    c["xj"][v * elems : (v + 1) * elems, 0:nodes] = new.astype(BF16)


def fine_substep(c):
    find_jumps(c)

    def finish(v, new):
        c["a"][v] = new
        store_x(c, v, new)

    transport_react(c, c["fine"], 1.0, finish)


def coarse_substep(c, finish):
    find_jumps(c)
    transport_react(c, c["coarse"], COARSE_GAIN, finish)


CONSTS = ("table", "codes", "lift_in", "fine_in", "coarse_in", "speed", "rates", "species")
IN_SMEM = ("speed", "rates", "species")
SCRATCH = ("xj", "a", "idx", "rank", "fine", "coarse", "m", "h", "made", "used")


def phase_scratch(dims, faces):
    variables, elems, nodes = dims
    slab = VMEM(dims, BF16)
    table = VMEM((3, elems, faces // 3), jnp.int32)
    weights = VMEM((nodes + faces, nodes), BF16)
    wide = VMEM((variables * elems, nodes + faces), BF16)
    return [wide, VMEM(dims, F32), table, table, weights, weights, slab, slab, slab, slab]


def begin(refs, count):
    c = dict(zip(CONSTS, refs))
    others = refs[len(CONSTS) : len(CONSTS) + count]
    scratch = refs[len(CONSTS) + count :]
    c.update(zip(SCRATCH, scratch))
    codes = c["codes"]
    blocks, _, block, _ = codes.shape
    c["block"] = block
    for s in range(blocks):
        for k in range(3):
            code = codes[s, k]
            rows = slice(s * block, (s + 1) * block)
            c["idx"][k, rows, :] = lax.rem(code, block)
            c["rank"][k, rows, :] = lax.div(code, block) - 1
    nodes = c["fine_in"].shape[0]
    c["fine"][0:nodes, :] = c["fine_in"][...]
    c["coarse"][0:nodes, :] = c["coarse_in"][...]
    half = c["idx"].shape[2] // 2
    for f in range(6):
        part = c["lift_in"][(f ^ 1) * half : (f ^ 1) * half + half, :]
        c["fine"][nodes + f * half : nodes + (f + 1) * half, :] = part
        c["coarse"][nodes + f * half : nodes + (f + 1) * half, :] = part
    return c, others, scratch[len(SCRATCH) :]


def unpack(ref, v, blocks, block):
    both = [ref[s, v * block : (v + 2) * block, :].astype(F32) for s in range(blocks)]
    return [
        jnp.concatenate([b[w * block : (w + 1) * block] for b in both], axis=0) for w in (0, 1)
    ]


def loop(count, fn):
    def one(i, carry):
        fn(i)
        return carry

    lax.fori_loop(0, count, one, 0)


def pack(values, ref, v, blocks, block):
    for s in range(blocks):
        both = jnp.concatenate([e[s * block : (s + 1) * block] for e in values], axis=0)
        ref[s, v * block : (v + 2) * block, :] = both.astype(BF16)


def chain_kernel(*refs):
    c, (starts, message, relaxed), (corr,) = begin(refs, 3)
    variables, elems, nodes = c["a"].shape
    block = c["block"]
    blocks = elems // block
    here = lax.axis_index("tm")
    for v in range(0, variables, 2):
        for w, part in enumerate(unpack(starts, v, blocks, block)):
            store_x(c, v + w, part)

    def phase(q):
        loop(2 * STRIDE, lambda i: fine_substep(c))

        @pl.when(q == 0)
        def _():
            @pl.when(here == 0)
            def _():
                for v in range(0, variables, 2):
                    pack([c["a"][v], c["a"][v + 1]], relaxed, v, blocks, block)

            def finish(v, new):
                corr[v] = new

            coarse_substep(c, finish)

    loop(2, phase)
    keep = jnp.where(here == 0, 0.0, 1.0)
    for v in range(0, variables, 2):
        ends = [c["a"][v + w] - keep * corr[v + w] for w in (0, 1)]
        pack(ends, message, v, blocks, block)


def finish_kernel(*refs):
    c, (messages, last, out), _ = begin(refs, 3)
    variables, elems, nodes = c["a"].shape
    block = c["block"]
    blocks = elems // block
    here, own = lax.axis_index("tm"), lax.axis_index("space")
    mine = pl.ds(pl.multiple_of(own * block, block), block)
    for v in range(0, variables, 2):
        for w, part in enumerate(unpack(messages.at[0], v, blocks, block)):
            store_x(c, v + w, part)
        both = last[v * block : (v + 2) * block, :].astype(F32)
        for w in (0, 1):
            out[STRIDE - 1, v + w] = both[w * block : (w + 1) * block]

    def advance(i):
        terms = {}

        def finish(v, new):
            if v % 2 == 0:
                terms[v], terms[v + 1] = unpack(messages.at[i + 1], v, blocks, block)
            store_x(c, v, new + terms[v])

        coarse_substep(c, finish)

    loop(here - 2, advance)

    @pl.when(here >= 2)
    def _():
        def keep(v, new):
            c["a"][v] = new

        coarse_substep(c, keep)
        for v in range(variables):
            out[STRIDE - 1, v] += c["a"][v, mine, :]

    def fine(i):
        fine_substep(c)

        @pl.when(i % 2 == 1)
        def _():
            out[i // 2] = c["a"][:, mine, :]

    loop(2 * (STRIDE - 1), fine)


def remote(src, dst, send, recv, target):
    return pltpu.make_async_remote_copy(
        src_ref=src,
        dst_ref=dst,
        send_sem=send,
        recv_sem=recv,
        device_id=target,
        device_id_type=MESH,
    )


def start_kernel(
    guess, initial, element, rank, starts, codes, mine, code, send, recv, code_send, code_recv, local
):
    me, size = lax.axis_index("space"), lax.axis_size("space")
    here, rows = lax.axis_index("tm"), lax.axis_size("tm")
    variables, block, _ = initial.shape
    lanes = code.shape[2]
    value = element[...] + block * (rank[...] + 1)
    low = lax.broadcasted_iota(jnp.int32, (block, lanes), 1) < lanes // 2
    for k in range(3):
        code[k] = jnp.where(low, value[:, 2 * k + 1 : 2 * k + 2], value[:, 2 * k : 2 * k + 1])

    def take(ref):
        for v in range(0, variables, 2):
            both = jnp.concatenate([ref[v], ref[v + 1]], axis=0)
            mine[v * block : (v + 2) * block, :] = both.astype(BF16)

    @pl.when(here == 0)
    def _():
        take(initial)

    @pl.when(here > 0)
    def _():
        take(guess.at[0])

    stays = here <= rows - 5
    moves = jnp.logical_and(here >= rows - 4, here <= rows - 2)
    comes = jnp.logical_or(here == rows - 4, here >= rows - 2)
    target = jnp.where(here == rows - 2, rows - 4, lax.rem(here + 2, rows))
    source = jnp.where(here == rows - 4, rows - 2, lax.rem(here + rows - 2, rows))

    def mate(row, d):
        return {"tm": row, "space": lax.rem(me + d, size)}

    barrier = pltpu.get_barrier_semaphore()
    for d in range(1, size):
        pl.semaphore_signal(barrier, inc=1, device_id=mate(here, d), device_id_type=MESH)

    @pl.when(comes)
    def _():
        for d in range(size):
            pl.semaphore_signal(barrier, inc=1, device_id=mate(source, d), device_id_type=MESH)

    pl.semaphore_wait(barrier, size - 1 + size * moves.astype(jnp.int32))

    def code_copy(d):
        return remote(code, codes.at[me], code_send.at[d], code_recv.at[d], mate(here, d))

    def stay_copy(d):
        return remote(mine, starts.at[me], send.at[d], recv.at[d], mate(here, d))

    def move_copy(d):
        return remote(mine, starts.at[me], send.at[d], recv.at[d], mate(target, d))

    keep_code = pltpu.make_async_copy(code, codes.at[me], local.at[0])
    keep_mine = pltpu.make_async_copy(mine, starts.at[me], local.at[1])

    @pl.when(stays)
    def _():
        for d in range(1, size):
            stay_copy(d).start()
        keep_mine.start()

    @pl.when(moves)
    def _():
        for d in range(size):
            move_copy(d).start()

    for d in range(1, size):
        code_copy(d).start()
    keep_code.start()
    keep_code.wait()

    @pl.when(stays)
    def _():
        keep_mine.wait()
        for d in range(1, size):
            stay_copy(d).wait_recv()

    @pl.when(comes)
    def _():
        for d in range(size):
            move_copy(d).wait_recv()

    for d in range(1, size):
        code_copy(d).wait_recv()

    @pl.when(stays)
    def _():
        for d in range(1, size):
            stay_copy(d).wait_send()

    @pl.when(moves)
    def _():
        for d in range(size):
            move_copy(d).wait_send()

    for d in range(1, size):
        code_copy(d).wait_send()


def tree(chips, source):
    if chips == 4:
        return ({1: 0, 2: 0, 3: 2}, {3: 1, 2: 3})[source]
    return {chip: source for chip in range(source + 1, chips)}


def spread_kernel(
    message,
    relaxed,
    starts,
    messages,
    last,
    send,
    pass_send,
    recv,
    last_send,
    last_recv,
    local,
):
    me, size = lax.axis_index("tm"), lax.axis_size("tm")
    own = lax.axis_index("space")
    chip, core = me // 2, me % 2
    blocks = message.shape[0]
    chips = size // 2
    sibling = me + 1 - 2 * core
    barrier = pltpu.get_barrier_semaphore()
    for d in range(1, size):
        mate = {"tm": lax.rem(me + d, size), "space": own}
        pl.semaphore_signal(barrier, inc=1, device_id=mate, device_id_type=MESH)
    pl.semaphore_wait(barrier, size - 1)

    def copy(src, k, q, sem, target):
        return remote(
            src.at[q],
            messages.at[k, q],
            sem,
            recv.at[k, q],
            {"tm": target, "space": own},
        )

    def hop(k, q, child, first):
        src = message if first else messages.at[k]
        return copy(src, k, q, send.at[k, child, q], 2 * child + k % 2)

    def side(k, q, src, target):
        return copy(src, k, q, pass_send.at[k, q], target)

    def pair_first(act):
        @pl.when(me == 0)
        def _():
            for q in range(blocks):
                act(side(0, q, relaxed, 1))

        @pl.when(me == size - 2)
        def _():
            for q in range(blocks):
                act(side(size - 4, q, message, size - 1))

    back = jnp.where(
        me == size - 4,
        size - 1,
        jnp.where(me >= size - 2, lax.rem(me + size - 1, size), lax.rem(me + 1, size)),
    )
    last_copy = remote(
        message.at[own], last, last_send, last_recv, {"tm": back, "space": own}
    )

    pair_first(lambda c: c.start())

    @pl.when(me != size - 3)
    def _():
        last_copy.start()

    for k in range(size - 4):

        @pl.when(me == k)
        def _():
            for q in range(blocks):
                for child, parent in tree(chips, k // 2).items():
                    if parent == k // 2:
                        if q >= WINDOW:
                            hop(k, q - WINDOW, child, True).wait_send()
                        hop(k, q, child, True).start()

    def local_copy(src, dst):
        keep = pltpu.make_async_copy(src, dst, local)
        keep.start()
        keep.wait()

    @pl.when(me == 0)
    def _():
        local_copy(starts, messages.at[0])
        local_copy(relaxed.at[own], last)

    @pl.when(me == size - 2)
    def _():
        local_copy(message, messages.at[size - 4])

    @pl.when(me == size - 1)
    def _():
        local_copy(message, messages.at[size - 3])

    def needs(device, k):
        return k <= device - 2

    for c in range(1, chips):
        for w in (0, 1):

            @pl.when(me == 2 * c + w)
            def _():
                order = [(k, q) for k in range(size - 4) for q in range(blocks)]
                order = [(k, q) for k, q in order if k // 2 < c and k % 2 == w]
                order.sort(key=lambda e: (tree(chips, e[0] // 2)[c] != e[0] // 2, e[1]))
                for k, q in order:
                    hop(k, q, c, True).wait_recv()
                    for child, parent in tree(chips, k // 2).items():
                        if parent == c:
                            hop(k, q, child, False).start()
                    if needs(2 * c + 1 - w, k):
                        side(k, q, messages.at[k], sibling).start()
                for q in range(blocks):
                    for k in range(size - 4):
                        if k // 2 < c and k % 2 != w and needs(2 * c + w, k):
                            side(k, q, messages.at[k], sibling).wait_recv()

    @pl.when(me == 1)
    def _():
        for q in range(blocks):
            side(0, q, relaxed, 1).wait_recv()

    @pl.when(me == size - 1)
    def _():
        for q in range(blocks):
            side(size - 4, q, message, size - 1).wait_recv()

    @pl.when(me >= 1)
    def _():
        last_copy.wait_recv()

    for k in range(size - 4):

        @pl.when(me == k)
        def _():
            for q in range(blocks - WINDOW, blocks):
                for child, parent in tree(chips, k // 2).items():
                    if parent == k // 2:
                        hop(k, q, child, True).wait_send()

    pair_first(lambda c: c.wait_send())

    @pl.when(me != size - 3)
    def _():
        last_copy.wait_send()

    for c in range(1, chips):
        for w in (0, 1):

            @pl.when(me == 2 * c + w)
            def _():
                for q in range(blocks):
                    for k in range(size - 4):
                        if k // 2 < c and k % 2 == w:
                            for child, parent in tree(chips, k // 2).items():
                                if parent == c:
                                    hop(k, q, child, False).wait_send()
                            if needs(2 * c + 1 - w, k):
                                side(k, q, messages.at[k], sibling).wait_send()


def transfer(kernel, cid, arrays, outs, scratch):
    return pl.pallas_call(
        kernel,
        out_shape=outs,
        in_specs=[pl.BlockSpec(memory_space=VMEM)] * len(arrays),
        out_specs=[pl.BlockSpec(memory_space=VMEM)] * len(outs),
        scratch_shapes=scratch,
        compiler_params=pltpu.CompilerParams(collective_id=cid, has_side_effects=True),
    )(*arrays)


def run_phase(kernel, consts, arrays, outs, scratch):
    specs = [
        pl.BlockSpec(memory_space=SMEM if name in IN_SMEM else VMEM) for name in CONSTS
    ]
    return pl.pallas_call(
        kernel,
        out_shape=outs,
        in_specs=specs + [pl.BlockSpec(memory_space=VMEM)] * len(arrays),
        out_specs=[pl.BlockSpec(memory_space=VMEM)] * len(outs),
        scratch_shapes=scratch,
        compiler_params=pltpu.CompilerParams(vmem_limit_bytes=60 * 1024 * 1024),
    )(*consts, *arrays)


def body(
    coarse_guess,
    initial_state,
    fine_volume,
    coarse_volume,
    lift_matrix,
    wave_speed,
    reaction_rate,
    species_map,
    neighbour_element,
    neighbour_rank,
):
    block, variables, nodes = initial_state.shape
    blocks, rows = lax.axis_size("space"), lax.axis_size("tm")
    faces = lift_matrix.shape[0]
    pair = faces // 3
    packed = (variables * block, nodes)
    state = jax.ShapeDtypeStruct((blocks,) + packed, BF16)
    dma = pltpu.SemaphoreType.DMA
    starts, codes = transfer(
        start_kernel,
        0,
        (
            jnp.transpose(coarse_guess, (0, 2, 1, 3)),
            jnp.transpose(initial_state, (1, 0, 2)),
            neighbour_element,
            neighbour_rank,
        ),
        [state, jax.ShapeDtypeStruct((blocks, 3, block, pair), jnp.int32)],
        [
            VMEM(packed, BF16),
            VMEM((3, block, pair), jnp.int32),
            dma((blocks,)),
            dma((blocks,)),
            dma((blocks,)),
            dma((blocks,)),
            dma((2,)),
        ],
    )
    consts = (
        jnp.asarray(face_table(SIDE)).astype(BF16),
        codes,
        lift_matrix,
        fine_volume,
        coarse_volume,
        wave_speed,
        reaction_rate,
        jnp.transpose(species_map),
    )
    dims = (variables, blocks * block, nodes)
    scratch = phase_scratch(dims, faces)
    message, relaxed = run_phase(
        chain_kernel, consts, (starts,), [state, state], scratch + [VMEM(dims, F32)]
    )
    messages, last = transfer(
        spread_kernel,
        1,
        (message, relaxed, starts),
        [
            jax.ShapeDtypeStruct((rows - 2,) + state.shape, BF16),
            jax.ShapeDtypeStruct(packed, BF16),
        ],
        [
            dma((rows - 4, rows // 2, blocks)),
            dma((rows - 2, blocks)),
            dma((rows - 2, blocks)),
            dma(()),
            dma(()),
            dma(()),
        ],
    )
    (out,) = run_phase(
        finish_kernel,
        consts,
        (messages, last),
        [jax.ShapeDtypeStruct((STRIDE, variables, block, nodes), F32)],
        scratch,
    )
    return jnp.transpose(out, (0, 2, 1, 3))


def solution(mesh):
    placed = (
        P("tm", "space", None, None),
        P("space", None, None),
        P(),
        P(),
        P(),
        P(),
        P(),
        P(),
        P("space", None),
        P("space", None),
    )
    return jax.shard_map(
        body, mesh=mesh, in_specs=placed, out_specs=P("tm", "space", None, None), check_vma=False
    )
```

```python
import jax
import jax.numpy as jnp
import numpy as np
from jax import lax
from jax.experimental import pallas as pl
from jax.experimental.pallas import tpu as pltpu
from jax.sharding import PartitionSpec as P

SIDE = 8
STRIDE = 4
COARSE_GAIN = 4.0
VMEM = pltpu.VMEM
SMEM = pltpu.SMEM
MESH = pl.DeviceIdType.MESH
BF16 = jnp.bfloat16
F32 = jnp.float32


def face_table(side):
    plane = side * side
    inner = np.arange(plane)
    first, second = inner // side, inner % side
    last = side - 1
    node_lists = [
        first * plane + second,
        first * plane + last * side + second,
        first * plane + second * side,
        first * plane + second * side + last,
    ]
    table = np.zeros((side**3, 4 * plane), np.float32)
    for f in range(4):
        table[node_lists[f], f * plane + inner] = 1.0
    return table


def find_jumps(c):
    xj, idx, rank, speed = c["xj"], c["idx"], c["rank"], c["speed"]
    variables, elems, nodes = c["a"].shape
    block = c["block"]
    blocks = elems // block
    pair = idx.shape[2]
    picked = jnp.dot(xj[:, 0:nodes], c["table"][...], preferred_element_type=F32)
    low = lax.broadcasted_iota(jnp.int32, (elems, pair), 1) < pair // 2
    for k in range(3):
        spots = [idx[k, s * block : (s + 1) * block, :] for s in range(blocks)]
        offsets = [rank[k, s * block : (s + 1) * block, :] for s in range(blocks)]
        for v in range(variables):
            rows = slice(v * elems, (v + 1) * elems)
            if k == 0:
                faces = jnp.where(
                    low,
                    xj[rows, 0:pair].astype(F32),
                    xj[rows, nodes - pair : nodes].astype(F32),
                )
            else:
                faces = picked[rows, (k - 1) * pair : k * pair]
            own = [faces[s * block : (s + 1) * block] for s in range(blocks)]
            parts = []
            for s in range(blocks):
                before, here, after = [
                    jnp.take_along_axis(
                        own[(s + d) % blocks], spots[s], axis=0, mode="promise_in_bounds"
                    )
                    for d in (-1, 0, 1)
                ]
                across = jnp.where(
                    offsets[s] < 0, before, jnp.where(offsets[s] > 0, after, here)
                )
                parts.append(speed[v] * (across - pltpu.roll(own[s], pair // 2, 1)))
            xj[rows, nodes + k * pair : nodes + (k + 1) * pair] = jnp.concatenate(
                parts, axis=0
            ).astype(BF16)


def transport_react(c, weights, gain, finish):
    a, m, h, rates, used, made = c["a"], c["m"], c["h"], c["rate"], c["used"], c["made"]
    whole, part = c["whole"], c["part"]
    variables, elems, nodes = a.shape
    moved = jnp.dot(c["xj"][...], weights[...], preferred_element_type=F32)
    for v in range(variables):
        own = moved[v * elems : (v + 1) * elems]
        a[v] = own
        m[v] = own.astype(BF16)
        h[v] = (own * own + 0.5).astype(BF16)
    total = None
    for q in range(rates.shape[0]):
        s0, s1 = whole[0, q], whole[1, q]
        factor = (part[0, q] * gain).astype(BF16)
        rate = factor * (m[s0] * m[s1]) / (h[s0] + h[s1])
        rates[q] = rate
        total = rate if q == 0 else total * part[1, q].astype(BF16) + rate
        used[q] = total
    total = None
    for q in range(rates.shape[0]):
        rate = rates[whole[2, q]]
        total = rate if q == 0 else total * part[2, q].astype(BF16) + rate
        made[q] = total
    for v in range(variables):
        plus = made[whole[4, v]].astype(F32) * part[4, v]
        minus = used[whole[3, v]].astype(F32) * part[3, v]
        finish(v, a[v] + (plus - minus))


def sort_reactions(c, order, order_smem, sem):
    down, across = c["species_down"], c["species_across"]
    count = down.shape[0]
    variables = c["a"].shape[0]
    r_down = lax.broadcasted_iota(jnp.int32, (count, 1), 0)
    r_across = lax.broadcasted_iota(jnp.int32, (1, count), 1)
    lane = lax.broadcasted_iota(jnp.int32, (count, 128), 1)

    def places(which):
        key_down = down[:, which : which + 1] * count + r_down
        key_across = across[which : which + 1, :] * count + r_across
        before = (key_across < key_down).astype(jnp.int32)
        place_down = jnp.sum(before, axis=1, keepdims=True)
        return place_down, jnp.where(lane == place_down, r_down, 0)

    place, ordered = places(0)
    _, ordered_made = places(2)
    order[...] = jnp.zeros(order.shape, jnp.int32)
    order[0:1, :] = jnp.sum(ordered, axis=0, keepdims=True)
    order[1:2, :] = jnp.sum(jnp.where(lane == r_down, place, 0), axis=0, keepdims=True)
    order[2:3, :] = jnp.sum(ordered_made, axis=0, keepdims=True)
    for row, which in ((3, 0), (5, 2)):
        species = down[:, which : which + 1]
        order[row : row + 1, :] = jnp.sum(
            (species <= lane).astype(jnp.int32), axis=0, keepdims=True
        )
        order[row + 1 : row + 2, :] = jnp.sum(
            (species == lane).astype(jnp.int32), axis=0, keepdims=True
        )
    copy = pltpu.make_async_copy(order, order_smem, sem)
    copy.start()
    copy.wait()
    whole, part, flat = c["whole"], c["part"], c["species"]
    for q in range(count):
        r, s = order_smem[0, q], order_smem[2, q]
        whole[0, q] = flat[0, r]
        whole[1, q] = flat[1, r]
        whole[2, q] = order_smem[1, s]
        part[0, q] = c["rates"][r]
        if q > 0:
            r, s = order_smem[0, q - 1], order_smem[2, q - 1]
            part[1, q] = jnp.where(flat[0, r] == whole[0, q], 1.0, 0.0)
            now = flat[2, order_smem[2, q]]
            part[2, q] = jnp.where(flat[2, s] == now, 1.0, 0.0)
    for v in range(variables):
        for row, at in ((3, 3), (5, 4)):
            whole[at, v] = jnp.maximum(order_smem[row, v] - 1, 0)
            part[at, v] = jnp.where(order_smem[row + 1, v] > 0, 1.0, 0.0)


def store_x(c, v, new):
    elems, nodes = new.shape
    c["xj"][v * elems : (v + 1) * elems, 0:nodes] = new.astype(BF16)


def fine_substep(c):
    find_jumps(c)

    def finish(v, new):
        c["a"][v] = new
        store_x(c, v, new)

    transport_react(c, c["fine"], 1.0, finish)


def coarse_substep(c, finish):
    find_jumps(c)
    transport_react(c, c["coarse"], COARSE_GAIN, finish)


def unpack(ref, v, blocks, block):
    both = [ref[s, v * block : (v + 2) * block, :].astype(F32) for s in range(blocks)]
    return [
        jnp.concatenate([b[w * block : (w + 1) * block] for b in both], axis=0) for w in (0, 1)
    ]


def pack(values, ref, v, blocks, block):
    for s in range(blocks):
        both = jnp.concatenate([e[s * block : (s + 1) * block] for e in values], axis=0)
        ref[s, v * block : (v + 2) * block, :] = both.astype(BF16)


def loop(count, fn):
    def one(i, carry):
        fn(i)
        return carry

    lax.fori_loop(0, count, one, 0)


def remote(src, dst, send, recv, target):
    return pltpu.make_async_remote_copy(
        src_ref=src,
        dst_ref=dst,
        send_sem=send,
        recv_sem=recv,
        device_id=target,
        device_id_type=MESH,
    )


def places_of_chains(rows):
    if rows == 8:
        return [4, 2, 5, 3, 6, 7, 1]
    return [k + 2 for k in range(rows - 2)] + [1]


def choose(me, values):
    value = jnp.int32(values[0])
    for i, other in enumerate(values[1:], 1):
        value = jnp.where(me == i, other, value)
    return value


def routes(rows):
    home = places_of_chains(rows)
    out = []
    for k in range(rows - 2):
        src = home[k]
        core = src % 2
        needs = [i for i in range(k + 2, rows) if i != src]
        pairs = []
        for chip in range(rows // 2):
            mine = [i for i in needs if i // 2 == chip]
            if not mine:
                continue
            if chip == src // 2:
                pairs.append((src, mine[0]))
                continue
            front = 2 * chip + core
            if front not in mine:
                front = mine[0]
            if rows == 8 and k == 0 and chip == 1:
                pairs += [(src, 0), (0, front)]
            else:
                pairs.append((src, front))
            pairs += [(front, i) for i in mine if i != front]
        out.append(pairs)
    return out


INPUTS = (
    "guess",
    "initial",
    "element",
    "neighbour",
    "table",
    "lift_in",
    "fine_in",
    "coarse_in",
    "speed",
    "rates",
    "species",
    "species_down",
    "species_across",
)
IN_SMEM = ("speed", "rates", "species")
IN_ANY = ("lift_in", "fine_in", "coarse_in")


def whole_kernel(names, *refs):
    c = dict(zip(names, refs))
    me, size = lax.axis_index("space"), lax.axis_size("space")
    here, rows = lax.axis_index("tm"), lax.axis_size("tm")
    variables, elems, nodes = c["a"].shape
    block = c["block"] = elems // size
    blocks = size
    guess, initial = c["guess"], c["initial"]
    starts, messages, message, last = c["starts"], c["messages"], c["message"], c["last"]
    relaxed, codes, code, out = c["relaxed"], c["codes"], c["code"], c["out"]
    home = places_of_chains(rows)
    mine = pl.ds(pl.multiple_of(me * block, block), block)

    half = code.shape[2] // 2
    loads = []
    for i, (name, src) in enumerate((("fine", "fine_in"), ("coarse", "coarse_in"))):
        loads.append((c[src], c[name].at[0:nodes], c["load"].at[i, 6]))
        for f in range(6):
            rows_in = c["lift_in"].at[(f ^ 1) * half : (f ^ 1) * half + half]
            rows_out = c[name].at[nodes + f * half : nodes + (f + 1) * half]
            loads.append((rows_in, rows_out, c["load"].at[i, f]))
    loads = [pltpu.make_async_copy(*load) for load in loads]
    for load in loads:
        load.start()

    lanes = code.shape[2]
    value = c["element"][...] + block * (c["neighbour"][...] + 1)
    low = lax.broadcasted_iota(jnp.int32, (block, lanes), 1) < lanes // 2
    for k in range(3):
        code[k] = jnp.where(low, value[:, 2 * k + 1 : 2 * k + 2], value[:, 2 * k : 2 * k + 1])
    for dst, src in ((c["own_guess"], guess.at[0]), (c["own_first"], initial)):
        for v in range(0, variables, 2):
            both = jnp.concatenate([src[v], src[v + 1]], axis=0)
            dst[v * block : (v + 2) * block, :] = both.astype(BF16)

    chain = [home.index(t) if t in home else -1 for t in range(rows)]
    target = choose(here, [0] + home[1:] + [0])
    source = choose(here, [max(k, 0) for k in chain])
    gives = jnp.logical_and(here >= 1, here <= rows - 2)
    stays = jnp.logical_and(gives, target == here)
    moves = jnp.logical_and(gives, target != here)
    busy = choose(here, [int(k >= 0) for k in chain]) == 1
    zero = jnp.logical_or(here == 0, here == home[0])
    comes = jnp.logical_and(source > 0, source != here)

    def mate(row, d):
        return {"tm": row, "space": lax.rem(me + d, size)}

    barrier = pltpu.get_barrier_semaphore()
    for d in range(1, rows):
        friend = {"tm": lax.rem(here + d, rows), "space": me}
        pl.semaphore_signal(barrier, inc=1, device_id=friend, device_id_type=MESH)
    for d in range(1, size):
        pl.semaphore_signal(barrier, inc=1, device_id=mate(here, d), device_id_type=MESH)

    @pl.when(comes)
    def _():
        for d in range(1, size):
            pl.semaphore_signal(barrier, inc=1, device_id=mate(source, d), device_id_type=MESH)

    pl.semaphore_wait(barrier, rows + size - 2 + (size - 1) * moves.astype(jnp.int32))

    def code_copy(d):
        return remote(code, codes.at[me], c["code_send"].at[d], c["code_recv"].at[d], mate(here, d))

    def start_copy(src, sems, row, d):
        return remote(src, starts.at[me], sems.at[d], c["start_recv"].at[d], mate(row, d))

    def first_copy(d):
        return start_copy(c["own_first"], c["first_send"], here, d)

    def guess_copy(row, d):
        return start_copy(c["own_guess"], c["guess_send"], row, d)

    keep_code = pltpu.make_async_copy(code, codes.at[me], c["local"].at[0])
    keep_first = pltpu.make_async_copy(c["own_first"], starts.at[me], c["local"].at[1])
    keep_guess = pltpu.make_async_copy(c["own_guess"], starts.at[me], c["local"].at[1])

    @pl.when(zero)
    def _():
        for d in range(1, size):
            first_copy(d).start()
        keep_first.start()

    @pl.when(stays)
    def _():
        for d in range(1, size):
            guess_copy(here, d).start()
        keep_guess.start()

    @pl.when(moves)
    def _():
        for d in range(size):
            guess_copy(target, d).start()

    for d in range(1, size):
        code_copy(d).start()
    keep_code.start()
    sort_reactions(c, c["order"], c["order_smem"], c["local"].at[2])
    keep_code.wait()
    for d in range(1, size):
        code_copy(d).wait_recv()
    for s in range(blocks):
        for k in range(3):
            found = codes[s, k]
            spots = slice(s * block, (s + 1) * block)
            c["idx"][k, spots, :] = lax.rem(found, block)
            c["rank"][k, spots, :] = lax.div(found, block) - 1
    for load in loads:
        load.wait()

    @pl.when(zero)
    def _():
        keep_first.wait()
        for d in range(1, size):
            first_copy(d).wait_recv()

    @pl.when(stays)
    def _():
        keep_guess.wait()
        for d in range(1, size):
            guess_copy(here, d).wait_recv()

    @pl.when(comes)
    def _():
        for d in range(size):
            guess_copy(target, d).wait_recv()

    def load_x(ref):
        for v in range(0, variables, 2):
            for w, part in enumerate(unpack(ref, v, blocks, block)):
                store_x(c, v + w, part)

    @pl.when(busy)
    def _():
        load_x(starts)

        def phase(q):
            loop(2 * STRIDE, lambda i: fine_substep(c))

            @pl.when(q == 0)
            def _():
                @pl.when(here == home[0])
                def _():
                    for v in range(0, variables, 2):
                        pack([c["a"][v], c["a"][v + 1]], relaxed, v, blocks, block)

                def finish(v, new):
                    c["corr"][v] = new

                coarse_substep(c, finish)

        loop(2, phase)
        keep = jnp.where(here == home[0], 0.0, 1.0)
        for v in range(0, variables, 2):
            ends = [c["a"][v + w] - keep * c["corr"][v + w] for w in (0, 1)]
            pack(ends, message, v, blocks, block)

    plan = routes(rows)

    def hop(k, n, q):
        sender, receiver = plan[k][n]
        src = message if sender == home[k] else messages.at[k]
        return remote(
            src.at[q],
            messages.at[k, q],
            c["send"].at[k, n, q],
            c["recv"].at[k, q],
            {"tm": receiver, "space": me},
        )

    def side(q):
        return remote(
            relaxed.at[q],
            messages.at[0, q],
            c["side_send"].at[q],
            c["recv"].at[0, q],
            {"tm": 1, "space": me},
        )

    def last_copy(src, to, n):
        return remote(
            src.at[me], last, c["last_send"].at[n], c["last_recv"], {"tm": to, "space": me}
        )

    next_row = choose(here, [k + 1 if k >= 0 else 0 for k in chain])

    for k in range(rows - 2):

        @pl.when(here == home[k])
        def _():
            for q in range(blocks):
                for n, (sender, _) in enumerate(plan[k]):
                    if sender == home[k]:
                        hop(k, n, q).start()

    sends_last = jnp.logical_and(busy, next_row != here)
    keep_last = pltpu.make_async_copy(message.at[me], last, c["local"].at[3])

    @pl.when(sends_last)
    def _():
        last_copy(message, next_row, 0).start()

    @pl.when(here == home[0])
    def _():
        for q in range(blocks):
            side(q).start()
        last_copy(relaxed, 0, 1).start()

    for k in range(rows - 2):
        if home[k] >= k + 2:

            @pl.when(here == home[k])
            def _():
                keep = pltpu.make_async_copy(message, messages.at[k], c["local"].at[3])
                keep.start()
                keep.wait()

    for t in range(rows):
        todo = []
        for k in range(rows - 2):
            for n, (sender, receiver) in enumerate(plan[k]):
                if receiver == t:
                    todo.append((k, n))
        direct = [e for e in todo if plan[e[0]][e[1]][0] == home[e[0]]]
        rest = [e for e in todo if e not in direct]
        if todo:

            @pl.when(here == t)
            def _():
                for group in (direct, rest):
                    for q in range(blocks):
                        for k, n in group:
                            hop(k, n, q).wait_recv()
                            for n2, (sender, _) in enumerate(plan[k]):
                                if sender == t:
                                    hop(k, n2, q).start()

    @pl.when(here == 1)
    def _():
        for q in range(blocks):
            side(q).wait_recv()

    @pl.when(here == 0)
    def _():
        load_x(starts)

    @pl.when(here > 0)
    def _():
        load_x(messages.at[0])

    def advance(i):
        terms = {}

        def finish(v, new):
            if v % 2 == 0:
                terms[v], terms[v + 1] = unpack(messages.at[i + 1], v, blocks, block)
            store_x(c, v, new + terms[v])

        coarse_substep(c, finish)

    loop(here - 2, advance)
    own_last = jnp.logical_and(busy, next_row == here)

    @pl.when(own_last)
    def _():
        keep_last.start()
        keep_last.wait()

    @pl.when(jnp.logical_not(own_last))
    def _():
        last_copy(message, next_row, 0).wait_recv()

    for v in range(0, variables, 2):
        both = last[v * block : (v + 2) * block, :].astype(F32)
        for w in (0, 1):
            out[STRIDE - 1, v + w] = both[w * block : (w + 1) * block]

    @pl.when(here >= 2)
    def _():
        def keep(v, new):
            c["a"][v] = new

        coarse_substep(c, keep)
        for v in range(variables):
            out[STRIDE - 1, v] += c["a"][v, mine, :]

    def fine(i):
        fine_substep(c)

        @pl.when(i % 2 == 1)
        def _():
            out[i // 2] = c["a"][:, mine, :]

    loop(2 * (STRIDE - 1), fine)

    @pl.when(zero)
    def _():
        for d in range(1, size):
            first_copy(d).wait_send()

    @pl.when(stays)
    def _():
        for d in range(1, size):
            guess_copy(here, d).wait_send()

    @pl.when(moves)
    def _():
        for d in range(size):
            guess_copy(target, d).wait_send()

    for d in range(1, size):
        code_copy(d).wait_send()
    for k in range(rows - 2):
        for n, (sender, _) in enumerate(plan[k]):

            @pl.when(here == sender)
            def _():
                for q in range(blocks):
                    hop(k, n, q).wait_send()

    @pl.when(sends_last)
    def _():
        last_copy(message, next_row, 0).wait_send()

    @pl.when(here == home[0])
    def _():
        for q in range(blocks):
            side(q).wait_send()
        last_copy(relaxed, 0, 1).wait_send()


def body(
    coarse_guess,
    initial_state,
    fine_volume,
    coarse_volume,
    lift_matrix,
    wave_speed,
    reaction_rate,
    species_map,
    neighbour_element,
    neighbour_rank,
):
    block, variables, nodes = initial_state.shape
    blocks, rows = lax.axis_size("space"), lax.axis_size("tm")
    faces, reactions = lift_matrix.shape[0], species_map.shape[0]
    elems, pair = blocks * block, faces // 3
    dma = pltpu.SemaphoreType.DMA
    packed = (variables * block, nodes)
    state = VMEM((blocks,) + packed, BF16)
    slab = VMEM((variables, elems, nodes), BF16)
    sums = VMEM((reactions, elems, nodes), BF16)
    full = VMEM((variables, elems, nodes), F32)
    weights = VMEM((nodes + faces, nodes), BF16)
    table = VMEM((3, elems, pair), jnp.int32)
    hops = max(len(pairs) for pairs in routes(rows))
    scratch = {
        "starts": state,
        "message": state,
        "relaxed": state,
        "messages": VMEM((rows - 2, blocks) + packed, BF16),
        "last": VMEM(packed, BF16),
        "own_guess": VMEM(packed, BF16),
        "own_first": VMEM(packed, BF16),
        "code": VMEM((3, block, pair), jnp.int32),
        "codes": VMEM((blocks, 3, block, pair), jnp.int32),
        "xj": VMEM((variables * elems, nodes + faces), BF16),
        "a": full,
        "corr": full,
        "idx": table,
        "rank": table,
        "fine": weights,
        "coarse": weights,
        "m": slab,
        "h": slab,
        "rate": sums,
        "used": sums,
        "made": sums,
        "order": VMEM((8, 128), jnp.int32),
        "order_smem": SMEM((8, 128), jnp.int32),
        "whole": SMEM((5, reactions), jnp.int32),
        "part": SMEM((5, reactions), F32),
        "load": dma((2, 7)),
        "local": dma((4,)),
        "code_send": dma((blocks,)),
        "code_recv": dma((blocks,)),
        "start_recv": dma((blocks,)),
        "first_send": dma((blocks,)),
        "guess_send": dma((blocks,)),
        "send": dma((rows - 2, hops, blocks)),
        "recv": dma((rows - 2, blocks)),
        "side_send": dma((blocks,)),
        "last_send": dma((2,)),
        "last_recv": dma(()),
    }
    inputs = (
        jnp.transpose(coarse_guess, (0, 2, 1, 3)),
        jnp.transpose(initial_state, (1, 0, 2)),
        neighbour_element,
        neighbour_rank,
        jnp.asarray(face_table(SIDE)).astype(BF16),
        lift_matrix,
        fine_volume,
        coarse_volume,
        wave_speed,
        reaction_rate,
        jnp.transpose(species_map),
        species_map,
        jnp.transpose(species_map),
    )
    spaces = [
        SMEM if name in IN_SMEM else pl.ANY if name in IN_ANY else VMEM for name in INPUTS
    ]
    out = pl.pallas_call(
        lambda *refs: whole_kernel(INPUTS + ("out",) + tuple(scratch), *refs),
        out_shape=jax.ShapeDtypeStruct((STRIDE, variables, block, nodes), F32),
        in_specs=[pl.BlockSpec(memory_space=space) for space in spaces],
        out_specs=pl.BlockSpec(memory_space=VMEM),
        scratch_shapes=list(scratch.values()),
        compiler_params=pltpu.CompilerParams(
            collective_id=0, has_side_effects=True, vmem_limit_bytes=60 * 1024 * 1024
        ),
    )(*inputs)
    return jnp.transpose(out, (0, 2, 1, 3))


def solution(mesh):
    placed = (
        P("tm", "space", None, None),
        P("space", None, None),
        P(),
        P(),
        P(),
        P(),
        P(),
        P(),
        P("space", None),
        P("space", None),
    )
    return jax.shard_map(
        body, mesh=mesh, in_specs=placed, out_specs=P("tm", "space", None, None), check_vma=False
    )
```

```python
import jax
import jax.numpy as jnp
import numpy as np
from jax import lax
from jax.experimental import pallas as pl
from jax.experimental.pallas import tpu as pltpu
from jax.sharding import PartitionSpec as P

SIDE = 8
STRIDE = 4
COARSE_GAIN = 4.0
VMEM = pltpu.VMEM
SMEM = pltpu.SMEM
MESH = pl.DeviceIdType.MESH
BF16 = jnp.bfloat16
F32 = jnp.float32


def face_table(side):
    plane = side * side
    inner = np.arange(plane)
    first, second = inner // side, inner % side
    last = side - 1
    node_lists = [
        first * plane + second,
        first * plane + last * side + second,
        first * plane + second * side,
        first * plane + second * side + last,
    ]
    table = np.zeros((side**3, 4 * plane), np.float32)
    for f in range(4):
        table[node_lists[f], f * plane + inner] = 1.0
    return table


def find_jumps(c):
    xj, idx, rank, speed = c["xj"], c["idx"], c["rank"], c["speed"]
    variables, elems, nodes = c["a"].shape
    block = c["block"]
    blocks = elems // block
    pair = idx.shape[2]
    picked = jnp.dot(xj[:, 0:nodes], c["table"][...], preferred_element_type=F32)
    low = lax.broadcasted_iota(jnp.int32, (elems, pair), 1) < pair // 2
    for k in range(3):
        spots = [idx[k, s * block : (s + 1) * block, :] for s in range(blocks)]
        offsets = [rank[k, s * block : (s + 1) * block, :] for s in range(blocks)]
        for v in range(variables):
            rows = slice(v * elems, (v + 1) * elems)
            if k == 0:
                faces = jnp.where(
                    low,
                    xj[rows, 0:pair].astype(F32),
                    xj[rows, nodes - pair : nodes].astype(F32),
                )
            else:
                faces = picked[rows, (k - 1) * pair : k * pair]
            own = [faces[s * block : (s + 1) * block] for s in range(blocks)]
            parts = []
            for s in range(blocks):
                before, here, after = [
                    jnp.take_along_axis(
                        own[(s + d) % blocks], spots[s], axis=0, mode="promise_in_bounds"
                    )
                    for d in (-1, 0, 1)
                ]
                across = jnp.where(
                    offsets[s] < 0, before, jnp.where(offsets[s] > 0, after, here)
                )
                parts.append(speed[v] * (across - pltpu.roll(own[s], pair // 2, 1)))
            xj[rows, nodes + k * pair : nodes + (k + 1) * pair] = jnp.concatenate(
                parts, axis=0
            ).astype(BF16)


def transport_react(c, weights, gain, finish):
    a, m, h, rates, used, made = c["a"], c["m"], c["h"], c["rate"], c["used"], c["made"]
    whole, part = c["whole"], c["part"]
    variables, elems, nodes = a.shape
    moved = jnp.dot(c["xj"][...], weights[...], preferred_element_type=F32)
    for v in range(variables):
        own = moved[v * elems : (v + 1) * elems]
        a[v] = own
        m[v] = own.astype(BF16)
        h[v] = (own * own + 0.5).astype(BF16)
    total = None
    for q in range(rates.shape[0]):
        s0, s1 = whole[0, q], whole[1, q]
        factor = (part[0, q] * gain).astype(BF16)
        rate = factor * (m[s0] * m[s1]) / (h[s0] + h[s1])
        rates[q] = rate
        total = rate if q == 0 else total * part[1, q].astype(BF16) + rate
        used[q] = total
    total = None
    for q in range(rates.shape[0]):
        rate = rates[whole[2, q]]
        total = rate if q == 0 else total * part[2, q].astype(BF16) + rate
        made[q] = total
    for v in range(variables):
        plus = made[whole[4, v]].astype(F32) * part[4, v]
        minus = used[whole[3, v]].astype(F32) * part[3, v]
        finish(v, a[v] + (plus - minus))


def sort_reactions(c, order, order_smem, sem):
    across = c["species_across"]
    count = across.shape[1]
    variables = c["a"].shape[0]
    r_down = lax.broadcasted_iota(jnp.int32, (count, 1), 0)
    r_across = lax.broadcasted_iota(jnp.int32, (1, count), 1)
    lane = lax.broadcasted_iota(jnp.int32, (count, 128), 1)

    def down(which):
        here = jnp.where(r_down == r_across, across[which : which + 1, :], 0)
        return jnp.sum(here, axis=1, keepdims=True)

    def places(which):
        key_down = down(which) * count + r_down
        key_across = across[which : which + 1, :] * count + r_across
        before = (key_across < key_down).astype(jnp.int32)
        place_down = jnp.sum(before, axis=1, keepdims=True)
        return place_down, jnp.where(lane == place_down, r_down, 0)

    place, ordered = places(0)
    _, ordered_made = places(2)
    order[...] = jnp.zeros(order.shape, jnp.int32)
    order[0:1, :] = jnp.sum(ordered, axis=0, keepdims=True)
    order[1:2, :] = jnp.sum(jnp.where(lane == r_down, place, 0), axis=0, keepdims=True)
    order[2:3, :] = jnp.sum(ordered_made, axis=0, keepdims=True)
    for row, which in ((3, 0), (5, 2)):
        species = down(which)
        order[row : row + 1, :] = jnp.sum(
            (species <= lane).astype(jnp.int32), axis=0, keepdims=True
        )
        order[row + 1 : row + 2, :] = jnp.sum(
            (species == lane).astype(jnp.int32), axis=0, keepdims=True
        )
    copy = pltpu.make_async_copy(order, order_smem, sem)
    copy.start()
    copy.wait()
    whole, part, flat = c["whole"], c["part"], c["species"]
    for q in range(count):
        r, s = order_smem[0, q], order_smem[2, q]
        whole[0, q] = flat[0, r]
        whole[1, q] = flat[1, r]
        whole[2, q] = order_smem[1, s]
        part[0, q] = c["rates"][r]
        if q > 0:
            r, s = order_smem[0, q - 1], order_smem[2, q - 1]
            part[1, q] = jnp.where(flat[0, r] == whole[0, q], 1.0, 0.0)
            now = flat[2, order_smem[2, q]]
            part[2, q] = jnp.where(flat[2, s] == now, 1.0, 0.0)
    for v in range(variables):
        for row, at in ((3, 3), (5, 4)):
            whole[at, v] = jnp.maximum(order_smem[row, v] - 1, 0)
            part[at, v] = jnp.where(order_smem[row + 1, v] > 0, 1.0, 0.0)


def store_x(c, v, new):
    elems, nodes = new.shape
    c["xj"][v * elems : (v + 1) * elems, 0:nodes] = new.astype(BF16)


def fine_substep(c):
    find_jumps(c)
    fine_rest(c)


def fine_rest(c):
    def finish(v, new):
        c["a"][v] = new
        store_x(c, v, new)

    transport_react(c, c["fine"], 1.0, finish)


def coarse_substep(c, finish):
    find_jumps(c)
    transport_react(c, c["coarse"], COARSE_GAIN, finish)


def unpack(ref, v, blocks, block):
    both = [ref[s, v * block : (v + 2) * block, :].astype(F32) for s in range(blocks)]
    return [
        jnp.concatenate([b[w * block : (w + 1) * block] for b in both], axis=0) for w in (0, 1)
    ]


def pack(values, ref, v, blocks, block):
    for s in range(blocks):
        both = jnp.concatenate([e[s * block : (s + 1) * block] for e in values], axis=0)
        ref[s, v * block : (v + 2) * block, :] = both.astype(BF16)


def loop(count, fn):
    def one(i, carry):
        fn(i)
        return carry

    lax.fori_loop(0, count, one, 0)


def remote(src, dst, send, recv, target):
    return pltpu.make_async_remote_copy(
        src_ref=src,
        dst_ref=dst,
        send_sem=send,
        recv_sem=recv,
        device_id=target,
        device_id_type=MESH,
    )


def places_of_chains(rows):
    if rows == 8:
        return [4, 2, 5, 3, 6, 7, 1]
    return [k + 2 for k in range(rows - 2)] + [1]


def choose(me, values):
    value = jnp.int32(values[0])
    for i, other in enumerate(values[1:], 1):
        value = jnp.where(me == i, other, value)
    return value


def routes(rows):
    home = places_of_chains(rows)
    out = []
    for k in range(rows - 2):
        src = home[k]
        core = src % 2
        needs = [i for i in range(k + 2, rows) if i != src]
        pairs = []
        for chip in range(rows // 2):
            mine = [i for i in needs if i // 2 == chip]
            if not mine:
                continue
            if chip == src // 2:
                pairs.append((src, mine[0]))
                continue
            front = 2 * chip + core
            if front not in mine:
                front = mine[0]
            if rows == 8 and k == 0 and chip == 1:
                pairs += [(src, 0), (0, front)]
            else:
                pairs.append((src, front))
            pairs += [(front, i) for i in mine if i != front]
        out.append(pairs)
    return out


INPUTS = (
    "guess",
    "initial",
    "element",
    "neighbour",
    "table_in",
    "lift_in",
    "fine_in",
    "coarse_in",
    "speed",
    "rates",
    "species",
    "species_across",
)
IN_SMEM = ("speed", "rates", "species")
IN_ANY = ("guess", "initial", "table_in", "lift_in", "fine_in", "coarse_in")


def whole_kernel(names, *refs):
    c = dict(zip(names, refs))
    me, size = lax.axis_index("space"), lax.axis_size("space")
    here, rows = lax.axis_index("tm"), lax.axis_size("tm")
    variables, elems, nodes = c["a"].shape
    block = c["block"] = elems // size
    blocks = size
    starts, messages, message, last = c["starts"], c["messages"], c["message"], c["last"]
    relaxed, codes, code, out = c["relaxed"], c["codes"], c["code"], c["out"]
    home = places_of_chains(rows)
    mine = pl.ds(pl.multiple_of(me * block, block), block)

    chain = [home.index(t) if t in home else -1 for t in range(rows)]
    target = choose(here, [0] + home[1:] + [0])
    source = choose(here, [max(k, 0) for k in chain])
    gives = jnp.logical_and(here >= 1, here <= rows - 2)
    stays = jnp.logical_and(gives, target == here)
    moves = jnp.logical_and(gives, target != here)
    busy = choose(here, [int(k >= 0) for k in chain]) == 1
    zero = jnp.logical_or(here == 0, here == home[0])
    comes = jnp.logical_and(source > 0, source != here)

    def mate(row, d):
        return {"tm": row, "space": lax.rem(me + d, size)}

    barrier = pltpu.get_barrier_semaphore()
    for d in range(1, rows):
        friend = {"tm": lax.rem(here + d, rows), "space": me}
        pl.semaphore_signal(barrier, inc=1, device_id=friend, device_id_type=MESH)
    for d in range(1, size):
        pl.semaphore_signal(barrier, inc=1, device_id=mate(here, d), device_id_type=MESH)

    @pl.when(comes)
    def _():
        for d in range(1, size):
            pl.semaphore_signal(barrier, inc=1, device_id=mate(source, d), device_id_type=MESH)

    fetches = [("guess_held", c["guess"].at[0]), ("initial_held", c["initial"])]
    fetches = [
        pltpu.make_async_copy(src, c[dst], c["fetch"].at[i]) for i, (dst, src) in enumerate(fetches)
    ]
    for fetch in fetches:
        fetch.start()
    table_load = pltpu.make_async_copy(c["table_in"], c["table"], c["fetch"].at[2])

    half = code.shape[2] // 2
    loads = []
    for i, (name, src) in enumerate((("fine", "fine_in"), ("coarse", "coarse_in"))):
        loads.append((c[src], c[name].at[0:nodes], c["load"].at[i, 6]))
        for f in range(6):
            rows_in = c["lift_in"].at[(f ^ 1) * half : (f ^ 1) * half + half]
            rows_out = c[name].at[nodes + f * half : nodes + (f + 1) * half]
            loads.append((rows_in, rows_out, c["load"].at[i, f]))
    loads = [pltpu.make_async_copy(*load) for load in loads]
    loads.append(table_load)
    for load in loads:
        load.start()

    lanes = code.shape[2]
    value = c["element"][...] + block * (c["neighbour"][...] + 1)
    low = lax.broadcasted_iota(jnp.int32, (block, lanes), 1) < lanes // 2
    for k in range(3):
        code[k] = jnp.where(low, value[:, 2 * k + 1 : 2 * k + 2], value[:, 2 * k : 2 * k + 1])
    for fetch in fetches:
        fetch.wait()
    for dst, src in ((c["own_guess"], c["guess_held"]), (c["own_first"], c["initial_held"])):
        for v in range(0, variables, 2):
            both = jnp.concatenate([src[v], src[v + 1]], axis=0)
            dst[v * block : (v + 2) * block, :] = both.astype(BF16)

    pl.semaphore_wait(barrier, rows + size - 2 + (size - 1) * moves.astype(jnp.int32))

    def code_copy(d):
        return remote(code, codes.at[me], c["code_send"].at[d], c["code_recv"].at[d], mate(here, d))

    def start_copy(src, sems, row, d):
        return remote(src, starts.at[me], sems.at[d], c["start_recv"].at[d], mate(row, d))

    def first_copy(d):
        return start_copy(c["own_first"], c["first_send"], here, d)

    def guess_copy(row, d):
        return start_copy(c["own_guess"], c["guess_send"], row, d)

    keep_code = pltpu.make_async_copy(code, codes.at[me], c["local"].at[0])
    keep_first = pltpu.make_async_copy(c["own_first"], starts.at[me], c["local"].at[1])
    keep_guess = pltpu.make_async_copy(c["own_guess"], starts.at[me], c["local"].at[1])

    @pl.when(zero)
    def _():
        for d in range(1, size):
            first_copy(d).start()
        keep_first.start()

    @pl.when(stays)
    def _():
        for d in range(1, size):
            guess_copy(here, d).start()
        keep_guess.start()

    @pl.when(moves)
    def _():
        for d in range(size):
            guess_copy(target, d).start()

    for d in range(1, size):
        code_copy(d).start()
    keep_code.start()
    sort_reactions(c, c["order"], c["order_smem"], c["local"].at[2])
    keep_code.wait()
    for d in range(1, size):
        code_copy(d).wait_recv()
    for s in range(blocks):
        for k in range(3):
            found = codes[s, k]
            spots = slice(s * block, (s + 1) * block)
            c["idx"][k, spots, :] = lax.rem(found, block)
            c["rank"][k, spots, :] = lax.div(found, block) - 1
    for load in loads:
        load.wait()

    @pl.when(zero)
    def _():
        keep_first.wait()
        for d in range(1, size):
            first_copy(d).wait_recv()

    @pl.when(stays)
    def _():
        keep_guess.wait()
        for d in range(1, size):
            guess_copy(here, d).wait_recv()

    @pl.when(comes)
    def _():
        for d in range(size):
            guess_copy(target, d).wait_recv()

    def load_x(ref):
        for v in range(0, variables, 2):
            for w, part in enumerate(unpack(ref, v, blocks, block)):
                store_x(c, v + w, part)

    @pl.when(busy)
    def _():
        load_x(starts)
        loop(2 * STRIDE, lambda i: fine_substep(c))

        @pl.when(here == home[0])
        def _():
            for v in range(0, variables, 2):
                pack([c["a"][v], c["a"][v + 1]], relaxed, v, blocks, block)

        def finish(v, new):
            c["corr"][v] = new

        coarse_substep(c, finish)
        fine_rest(c)
        loop(2 * STRIDE - 1, lambda i: fine_substep(c))
        keep = jnp.where(here == home[0], 0.0, 1.0)
        for v in range(0, variables, 2):
            ends = [c["a"][v + w] - keep * c["corr"][v + w] for w in (0, 1)]
            pack(ends, message, v, blocks, block)

    plan = routes(rows)
    firsts = [k for k in (0, 1) if rows == 8]
    first_turn = [home[k] for k in firsts]

    def hop(k, n, q):
        sender, receiver = plan[k][n]
        src = message if sender == home[k] else messages.at[k]
        return remote(
            src.at[q],
            messages.at[k, q],
            c["send"].at[k, n, q],
            c["recv"].at[k, q],
            {"tm": receiver, "space": me},
        )

    def side(q):
        return remote(
            relaxed.at[q],
            messages.at[0, q],
            c["side_send"].at[q],
            c["recv"].at[0, q],
            {"tm": 1, "space": me},
        )

    def last_copy(src, to, n):
        return remote(
            src.at[me], last, c["last_send"].at[n], c["last_recv"], {"tm": to, "space": me}
        )

    next_row = choose(here, [k + 1 if k >= 0 else 0 for k in chain])

    for k in range(rows - 2):

        @pl.when(here == home[k])
        def _():
            if home[k] ^ 1 in first_turn and k not in firsts:
                pl.semaphore_wait(c["turn"], 1)
            far = [n for n, pair in enumerate(plan[k]) if pair[0] == home[k]]
            near = [n for n in far if plan[k][n][1] // 2 == home[k] // 2]
            far = [n for n in far if n not in near]
            for q in range(blocks):
                for n in far + near:
                    if n in far and k in firsts and q >= 2:
                        hop(k, n, q - 2).wait_send()
                    hop(k, n, q).start()
            if k in firsts:
                for q in range(blocks - 2, blocks):
                    for n in far:
                        hop(k, n, q).wait_send()
                pl.semaphore_signal(
                    c["turn"],
                    inc=1,
                    device_id={"tm": home[k] ^ 1, "space": me},
                    device_id_type=MESH,
                )

    sends_last = jnp.logical_and(busy, next_row != here)
    keep_last = pltpu.make_async_copy(message.at[me], last, c["local"].at[3])

    @pl.when(sends_last)
    def _():
        last_copy(message, next_row, 0).start()

    @pl.when(here == home[0])
    def _():
        for q in range(blocks):
            side(q).start()
        last_copy(relaxed, 0, 1).start()

    for k in range(rows - 2):
        if home[k] >= k + 2:

            @pl.when(here == home[k])
            def _():
                keep = pltpu.make_async_copy(message, messages.at[k], c["local"].at[3])
                keep.start()
                keep.wait()

    def receive(wanted):
        for t in range(rows):
            todo = []
            for k in wanted:
                for n, (sender, receiver) in enumerate(plan[k]):
                    if receiver == t:
                        todo.append((k, n))
            direct = [e for e in todo if plan[e[0]][e[1]][0] == home[e[0]]]
            rest = [e for e in todo if e not in direct]
            if todo:
                receive_at(t, (direct, rest))

    def receive_at(t, groups):
        @pl.when(here == t)
        def _():
            for group in groups:
                for q in range(blocks):
                    for k, n in group:
                        hop(k, n, q).wait_recv()
                        for n2, (sender, _) in enumerate(plan[k]):
                            if sender == t:
                                hop(k, n2, q).start()

    receive(range(2))

    @pl.when(here == 1)
    def _():
        for q in range(blocks):
            side(q).wait_recv()

    @pl.when(here == 0)
    def _():
        load_x(starts)

    @pl.when(here > 0)
    def _():
        load_x(messages.at[0])

    def advance(i):
        @pl.when(i == 1)
        def _():
            receive(range(2, rows - 2))

        terms = {}

        def finish(v, new):
            if v % 2 == 0:
                terms[v], terms[v + 1] = unpack(messages.at[i + 1], v, blocks, block)
            store_x(c, v, new + terms[v])

        coarse_substep(c, finish)

    loop(here - 2, advance)
    own_last = jnp.logical_and(busy, next_row == here)

    @pl.when(own_last)
    def _():
        keep_last.start()
        keep_last.wait()

    @pl.when(jnp.logical_not(own_last))
    def _():
        last_copy(message, next_row, 0).wait_recv()

    for v in range(0, variables, 2):
        both = last[v * block : (v + 2) * block, :].astype(F32)
        for w in (0, 1):
            out[STRIDE - 1, v + w] = both[w * block : (w + 1) * block]

    find_jumps(c)

    @pl.when(here >= 2)
    def _():
        def keep(v, new):
            c["a"][v] = new

        transport_react(c, c["coarse"], COARSE_GAIN, keep)
        for v in range(variables):
            out[STRIDE - 1, v] += c["a"][v, mine, :]

    fine_rest(c)

    def fine(i):
        fine_substep(c)

        @pl.when(i % 2 == 0)
        def _():
            out[i // 2] = c["a"][:, mine, :]

    loop(2 * (STRIDE - 1) - 1, fine)

    @pl.when(zero)
    def _():
        for d in range(1, size):
            first_copy(d).wait_send()

    @pl.when(stays)
    def _():
        for d in range(1, size):
            guess_copy(here, d).wait_send()

    @pl.when(moves)
    def _():
        for d in range(size):
            guess_copy(target, d).wait_send()

    for d in range(1, size):
        code_copy(d).wait_send()
    for k in range(rows - 2):
        for n, (sender, receiver) in enumerate(plan[k]):
            if k in firsts and sender == home[k] and receiver // 2 != sender // 2:
                continue

            @pl.when(here == sender)
            def _():
                for q in range(blocks):
                    hop(k, n, q).wait_send()

    @pl.when(sends_last)
    def _():
        last_copy(message, next_row, 0).wait_send()

    @pl.when(here == home[0])
    def _():
        for q in range(blocks):
            side(q).wait_send()
        last_copy(relaxed, 0, 1).wait_send()


def body(
    coarse_guess,
    initial_state,
    fine_volume,
    coarse_volume,
    lift_matrix,
    wave_speed,
    reaction_rate,
    species_map,
    neighbour_element,
    neighbour_rank,
):
    block, variables, nodes = initial_state.shape
    blocks, rows = lax.axis_size("space"), lax.axis_size("tm")
    faces, reactions = lift_matrix.shape[0], species_map.shape[0]
    elems, pair = blocks * block, faces // 3
    dma = pltpu.SemaphoreType.DMA
    packed = (variables * block, nodes)
    state = VMEM((blocks,) + packed, BF16)
    slab = VMEM((variables, elems, nodes), BF16)
    sums = VMEM((reactions, elems, nodes), BF16)
    full = VMEM((variables, elems, nodes), F32)
    weights = VMEM((nodes + faces, nodes), BF16)
    table = VMEM((3, elems, pair), jnp.int32)
    hops = max(len(pairs) for pairs in routes(rows))
    scratch = {
        "guess_held": VMEM((variables, block, nodes), F32),
        "initial_held": VMEM((variables, block, nodes), F32),
        "table": VMEM((nodes, 2 * pair), BF16),
        "starts": state,
        "message": state,
        "relaxed": state,
        "messages": VMEM((rows - 2, blocks) + packed, BF16),
        "last": VMEM(packed, BF16),
        "own_guess": VMEM(packed, BF16),
        "own_first": VMEM(packed, BF16),
        "code": VMEM((3, block, pair), jnp.int32),
        "codes": VMEM((blocks, 3, block, pair), jnp.int32),
        "xj": VMEM((variables * elems, nodes + faces), BF16),
        "a": full,
        "corr": full,
        "idx": table,
        "rank": table,
        "fine": weights,
        "coarse": weights,
        "m": slab,
        "h": slab,
        "rate": sums,
        "used": sums,
        "made": sums,
        "order": VMEM((8, 128), jnp.int32),
        "order_smem": SMEM((8, 128), jnp.int32),
        "whole": SMEM((5, reactions), jnp.int32),
        "part": SMEM((5, reactions), F32),
        "load": dma((2, 7)),
        "fetch": dma((3,)),
        "turn": pltpu.SemaphoreType.REGULAR,
        "local": dma((4,)),
        "code_send": dma((blocks,)),
        "code_recv": dma((blocks,)),
        "start_recv": dma((blocks,)),
        "first_send": dma((blocks,)),
        "guess_send": dma((blocks,)),
        "send": dma((rows - 2, hops, blocks)),
        "recv": dma((rows - 2, blocks)),
        "side_send": dma((blocks,)),
        "last_send": dma((2,)),
        "last_recv": dma(()),
    }
    inputs = (
        jnp.transpose(coarse_guess, (0, 2, 1, 3)),
        jnp.transpose(initial_state, (1, 0, 2)),
        neighbour_element,
        neighbour_rank,
        jnp.asarray(face_table(SIDE)).astype(BF16),
        lift_matrix,
        fine_volume,
        coarse_volume,
        wave_speed,
        reaction_rate,
        jnp.transpose(species_map),
        jnp.transpose(species_map),
    )
    spaces = [
        SMEM if name in IN_SMEM else pl.ANY if name in IN_ANY else VMEM for name in INPUTS
    ]
    out = pl.pallas_call(
        lambda *refs: whole_kernel(INPUTS + ("out",) + tuple(scratch), *refs),
        out_shape=jax.ShapeDtypeStruct((STRIDE, variables, block, nodes), F32),
        in_specs=[pl.BlockSpec(memory_space=space) for space in spaces],
        out_specs=pl.BlockSpec(memory_space=VMEM),
        scratch_shapes=list(scratch.values()),
        compiler_params=pltpu.CompilerParams(
            collective_id=0, has_side_effects=True, vmem_limit_bytes=60 * 1024 * 1024
        ),
    )(*inputs)
    return jnp.transpose(out, (0, 2, 1, 3))


def solution(mesh):
    placed = (
        P("tm", "space", None, None),
        P("space", None, None),
        P(),
        P(),
        P(),
        P(),
        P(),
        P(),
        P("space", None),
        P("space", None),
    )
    return jax.shard_map(
        body, mesh=mesh, in_specs=placed, out_specs=P("tm", "space", None, None), check_vma=False
    )
```

```python
import jax
import jax.numpy as jnp
import numpy as np
from jax import lax
from jax.experimental import pallas as pl
from jax.experimental.pallas import tpu as pltpu
from jax.sharding import PartitionSpec as P

SIDE = 8
STRIDE = 4
COARSE_GAIN = 4.0
VMEM = pltpu.VMEM
SMEM = pltpu.SMEM
MESH = pl.DeviceIdType.MESH
BF16 = jnp.bfloat16
F32 = jnp.float32


def face_table(side):
    plane = side * side
    inner = np.arange(plane)
    first, second = inner // side, inner % side
    last = side - 1
    node_lists = [
        first * plane + second,
        first * plane + last * side + second,
        first * plane + second * side,
        first * plane + second * side + last,
    ]
    table = np.zeros((side**3, 4 * plane), np.float32)
    for f in range(4):
        table[node_lists[f], f * plane + inner] = 1.0
    return table


def find_jumps(c):
    xj, idx, rank, speed = c["xj"], c["idx"], c["rank"], c["speed"]
    variables, elems, nodes = c["a"].shape
    block = c["block"]
    blocks = elems // block
    pair = idx.shape[2]
    picked = jnp.dot(xj[:, 0:nodes], c["table"][...], preferred_element_type=F32)
    low = lax.broadcasted_iota(jnp.int32, (elems, pair), 1) < pair // 2
    for k in range(3):
        spots = [idx[k, s * block : (s + 1) * block, :] for s in range(blocks)]
        offsets = [rank[k, s * block : (s + 1) * block, :] for s in range(blocks)]
        for v in range(variables):
            rows = slice(v * elems, (v + 1) * elems)
            if k == 0:
                faces = jnp.where(
                    low,
                    xj[rows, 0:pair].astype(F32),
                    xj[rows, nodes - pair : nodes].astype(F32),
                )
            else:
                faces = picked[rows, (k - 1) * pair : k * pair]
            own = [faces[s * block : (s + 1) * block] for s in range(blocks)]
            parts = []
            for s in range(blocks):
                before, here, after = [
                    jnp.take_along_axis(
                        own[(s + d) % blocks], spots[s], axis=0, mode="promise_in_bounds"
                    )
                    for d in (-1, 0, 1)
                ]
                across = jnp.where(
                    offsets[s] < 0, before, jnp.where(offsets[s] > 0, after, here)
                )
                parts.append(speed[v] * (across - pltpu.roll(own[s], pair // 2, 1)))
            xj[rows, nodes + k * pair : nodes + (k + 1) * pair] = jnp.concatenate(
                parts, axis=0
            ).astype(BF16)


def transport_react(c, weights, gain, finish):
    a, m, h, rates, used, made = c["a"], c["m"], c["h"], c["rate"], c["used"], c["made"]
    whole, part = c["whole"], c["part"]
    variables, elems, nodes = a.shape
    moved = jnp.dot(c["xj"][...], weights[...], preferred_element_type=F32)
    for v in range(variables):
        own = moved[v * elems : (v + 1) * elems]
        a[v] = own
        m[v] = own.astype(BF16)
        h[v] = (own * own + 0.5).astype(BF16)
    total = None
    for q in range(rates.shape[0]):
        s0, s1 = whole[0, q], whole[1, q]
        factor = (part[0, q] * gain).astype(BF16)
        rate = factor * (m[s0] * m[s1]) / (h[s0] + h[s1])
        rates[q] = rate
        total = rate if q == 0 else total * part[1, q].astype(BF16) + rate
        used[q] = total
    total = None
    for q in range(rates.shape[0]):
        rate = rates[whole[2, q]]
        total = rate if q == 0 else total * part[2, q].astype(BF16) + rate
        made[q] = total
    for v in range(variables):
        plus = made[whole[4, v]].astype(F32) * part[4, v]
        minus = used[whole[3, v]].astype(F32) * part[3, v]
        finish(v, a[v] + (plus - minus))


def sort_reactions(c, order, order_smem, sem):
    across = c["species_across"]
    count = across.shape[1]
    variables = c["a"].shape[0]
    r_down = lax.broadcasted_iota(jnp.int32, (count, 1), 0)
    r_across = lax.broadcasted_iota(jnp.int32, (1, count), 1)
    lane = lax.broadcasted_iota(jnp.int32, (count, 128), 1)

    def down(which):
        here = jnp.where(r_down == r_across, across[which : which + 1, :], 0)
        return jnp.sum(here, axis=1, keepdims=True)

    def places(which):
        key_down = down(which) * count + r_down
        key_across = across[which : which + 1, :] * count + r_across
        before = (key_across < key_down).astype(jnp.int32)
        place_down = jnp.sum(before, axis=1, keepdims=True)
        return place_down, jnp.where(lane == place_down, r_down, 0)

    place, ordered = places(0)
    _, ordered_made = places(2)
    order[...] = jnp.zeros(order.shape, jnp.int32)
    order[0:1, :] = jnp.sum(ordered, axis=0, keepdims=True)
    order[1:2, :] = jnp.sum(jnp.where(lane == r_down, place, 0), axis=0, keepdims=True)
    order[2:3, :] = jnp.sum(ordered_made, axis=0, keepdims=True)
    for row, which in ((3, 0), (5, 2)):
        species = down(which)
        order[row : row + 1, :] = jnp.sum(
            (species <= lane).astype(jnp.int32), axis=0, keepdims=True
        )
        order[row + 1 : row + 2, :] = jnp.sum(
            (species == lane).astype(jnp.int32), axis=0, keepdims=True
        )
    copy = pltpu.make_async_copy(order, order_smem, sem)
    copy.start()
    copy.wait()
    whole, part, flat = c["whole"], c["part"], c["species"]
    for q in range(count):
        r, s = order_smem[0, q], order_smem[2, q]
        whole[0, q] = flat[0, r]
        whole[1, q] = flat[1, r]
        whole[2, q] = order_smem[1, s]
        part[0, q] = c["rates"][r]
        if q > 0:
            r, s = order_smem[0, q - 1], order_smem[2, q - 1]
            part[1, q] = jnp.where(flat[0, r] == whole[0, q], 1.0, 0.0)
            now = flat[2, order_smem[2, q]]
            part[2, q] = jnp.where(flat[2, s] == now, 1.0, 0.0)
    for v in range(variables):
        for row, at in ((3, 3), (5, 4)):
            whole[at, v] = jnp.maximum(order_smem[row, v] - 1, 0)
            part[at, v] = jnp.where(order_smem[row + 1, v] > 0, 1.0, 0.0)


def store_x(c, v, new):
    elems, nodes = new.shape
    c["xj"][v * elems : (v + 1) * elems, 0:nodes] = new.astype(BF16)


def fine_substep(c):
    find_jumps(c)
    fine_rest(c)


def fine_rest(c):
    def finish(v, new):
        c["a"][v] = new
        store_x(c, v, new)

    transport_react(c, c["fine"], 1.0, finish)


def coarse_substep(c, finish):
    find_jumps(c)
    transport_react(c, c["coarse"], COARSE_GAIN, finish)


def unpack(ref, v, blocks, block):
    both = [ref[s, v * block : (v + 2) * block, :].astype(F32) for s in range(blocks)]
    return [
        jnp.concatenate([b[w * block : (w + 1) * block] for b in both], axis=0) for w in (0, 1)
    ]


def pack(values, ref, v, blocks, block):
    for s in range(blocks):
        both = jnp.concatenate([e[s * block : (s + 1) * block] for e in values], axis=0)
        ref[s, v * block : (v + 2) * block, :] = both.astype(BF16)


def loop(count, fn):
    def one(i, carry):
        fn(i)
        return carry

    lax.fori_loop(0, count, one, 0)


def remote(src, dst, send, recv, target):
    return pltpu.make_async_remote_copy(
        src_ref=src,
        dst_ref=dst,
        send_sem=send,
        recv_sem=recv,
        device_id=target,
        device_id_type=MESH,
    )


def places_of_chains(rows):
    if rows == 8:
        return [4, 2, 5, 3, 6, 7, 1]
    return [k + 2 for k in range(rows - 2)] + [1]


def choose(me, values):
    value = jnp.int32(values[0])
    for i, other in enumerate(values[1:], 1):
        value = jnp.where(me == i, other, value)
    return value


def routes(rows):
    home = places_of_chains(rows)
    out = []
    for k in range(rows - 2):
        src = home[k]
        core = src % 2
        needs = [i for i in range(k + 2, rows) if i != src]
        pairs = []
        for chip in range(rows // 2):
            mine = [i for i in needs if i // 2 == chip]
            if not mine:
                continue
            if chip == src // 2:
                pairs.append((src, mine[0]))
                continue
            front = 2 * chip + core
            if front not in mine:
                front = mine[0]
            if rows == 8 and k == 0 and chip == 1:
                pairs += [(src, 0), (0, front)]
            else:
                pairs.append((src, front))
            pairs += [(front, i) for i in mine if i != front]
        out.append(pairs)
    return out


INPUTS = (
    "guess",
    "initial",
    "element",
    "neighbour",
    "table_in",
    "lift_in",
    "fine_in",
    "coarse_in",
    "speed",
    "rates",
    "species",
    "species_across",
)
IN_SMEM = ("speed", "rates", "species")
IN_ANY = ("guess", "initial", "table_in", "lift_in", "fine_in", "coarse_in")


def whole_kernel(names, *refs):
    c = dict(zip(names, refs))
    me, size = lax.axis_index("space"), lax.axis_size("space")
    here, rows = lax.axis_index("tm"), lax.axis_size("tm")
    variables, elems, nodes = c["a"].shape
    block = c["block"] = elems // size
    blocks = size
    starts, messages, message, last = c["starts"], c["messages"], c["message"], c["last"]
    relaxed, codes, code, out = c["relaxed"], c["codes"], c["code"], c["out"]
    home = places_of_chains(rows)
    mine = pl.ds(pl.multiple_of(me * block, block), block)

    chain = [home.index(t) if t in home else -1 for t in range(rows)]
    target = choose(here, [0] + home[1:] + [home[0]])
    source = choose(here, [k if k > 0 else rows - 1 if k == 0 else -1 for k in chain])
    stays = jnp.logical_and(here >= 1, target == here)
    moves = jnp.logical_and(here >= 1, target != here)
    busy = choose(here, [int(k >= 0) for k in chain]) == 1
    zero = here == 0
    comes = jnp.logical_and(source >= 0, source != here)

    def mate(row, d):
        return {"tm": row, "space": lax.rem(me + d, size)}

    barrier = pltpu.get_barrier_semaphore()
    for d in range(1, rows):
        friend = {"tm": lax.rem(here + d, rows), "space": me}
        pl.semaphore_signal(barrier, inc=1, device_id=friend, device_id_type=MESH)
    for d in range(1, size):
        pl.semaphore_signal(barrier, inc=1, device_id=mate(here, d), device_id_type=MESH)

    @pl.when(comes)
    def _():
        for d in range(1, size):
            pl.semaphore_signal(barrier, inc=1, device_id=mate(source, d), device_id_type=MESH)

    fetches = [("guess_held", c["guess"].at[0]), ("initial_held", c["initial"])]
    fetches = [
        pltpu.make_async_copy(src, c[dst], c["fetch"].at[i]) for i, (dst, src) in enumerate(fetches)
    ]
    for fetch in fetches:
        fetch.start()
    table_load = pltpu.make_async_copy(c["table_in"], c["table"], c["fetch"].at[2])

    half = code.shape[2] // 2
    loads = []
    for i, (name, src) in enumerate((("fine", "fine_in"), ("coarse", "coarse_in"))):
        loads.append((c[src], c[name].at[0:nodes], c["load"].at[i, 6]))
        for f in range(6):
            rows_in = c["lift_in"].at[(f ^ 1) * half : (f ^ 1) * half + half]
            rows_out = c[name].at[nodes + f * half : nodes + (f + 1) * half]
            loads.append((rows_in, rows_out, c["load"].at[i, f]))
    loads = [pltpu.make_async_copy(*load) for load in loads]
    loads.append(table_load)
    for load in loads:
        load.start()

    lanes = code.shape[2]
    value = c["element"][...] + block * (c["neighbour"][...] + 1)
    low = lax.broadcasted_iota(jnp.int32, (block, lanes), 1) < lanes // 2
    for k in range(3):
        code[k] = jnp.where(low, value[:, 2 * k + 1 : 2 * k + 2], value[:, 2 * k : 2 * k + 1])
    for fetch in fetches:
        fetch.wait()

    def take(src, dst):
        for v in range(0, variables, 2):
            both = jnp.concatenate([src[v], src[v + 1]], axis=0)
            dst[v * block : (v + 2) * block, :] = both.astype(BF16)

    @pl.when(here == 0)
    def _():
        take(c["initial_held"], c["own_first"])

    @pl.when(jnp.logical_and(here > 0, here < rows - 1))
    def _():
        take(c["guess_held"], c["own_guess"])

    @pl.when(here == rows - 1)
    def _():
        take(c["initial_held"], c["own_guess"])

    pl.semaphore_wait(barrier, rows + size - 2 + (size - 1) * moves.astype(jnp.int32))

    def code_copy(d):
        return remote(code, codes.at[me], c["code_send"].at[d], c["code_recv"].at[d], mate(here, d))

    def start_copy(src, sems, row, d):
        return remote(src, starts.at[me], sems.at[d], c["start_recv"].at[d], mate(row, d))

    def first_copy(d):
        return start_copy(c["own_first"], c["first_send"], here, d)

    def guess_copy(row, d):
        return start_copy(c["own_guess"], c["guess_send"], row, d)

    keep_code = pltpu.make_async_copy(code, codes.at[me], c["local"].at[0])
    keep_first = pltpu.make_async_copy(c["own_first"], starts.at[me], c["local"].at[1])
    keep_guess = pltpu.make_async_copy(c["own_guess"], starts.at[me], c["local"].at[1])

    @pl.when(zero)
    def _():
        for d in range(1, size):
            first_copy(d).start()
        keep_first.start()

    @pl.when(stays)
    def _():
        for d in range(1, size):
            guess_copy(here, d).start()
        keep_guess.start()

    @pl.when(moves)
    def _():
        for d in range(size):
            guess_copy(target, d).start()

    for d in range(1, size):
        code_copy(d).start()
    keep_code.start()
    sort_reactions(c, c["order"], c["order_smem"], c["local"].at[2])
    keep_code.wait()
    for d in range(1, size):
        code_copy(d).wait_recv()
    for s in range(blocks):
        for k in range(3):
            found = codes[s, k]
            spots = slice(s * block, (s + 1) * block)
            c["idx"][k, spots, :] = lax.rem(found, block)
            c["rank"][k, spots, :] = lax.div(found, block) - 1
    for load in loads:
        load.wait()

    @pl.when(zero)
    def _():
        keep_first.wait()
        for d in range(1, size):
            first_copy(d).wait_recv()

    @pl.when(stays)
    def _():
        keep_guess.wait()
        for d in range(1, size):
            guess_copy(here, d).wait_recv()

    @pl.when(comes)
    def _():
        for d in range(size):
            guess_copy(target, d).wait_recv()

    def load_x(ref):
        for v in range(0, variables, 2):
            for w, part in enumerate(unpack(ref, v, blocks, block)):
                store_x(c, v + w, part)

    @pl.when(busy)
    def _():
        load_x(starts)
        loop(2 * STRIDE, lambda i: fine_substep(c))

        @pl.when(here == home[0])
        def _():
            for v in range(0, variables, 2):
                pack([c["a"][v], c["a"][v + 1]], relaxed, v, blocks, block)

        def finish(v, new):
            c["corr"][v] = new

        coarse_substep(c, finish)
        fine_rest(c)
        loop(2 * STRIDE - 1, lambda i: fine_substep(c))
        keep = jnp.where(here == home[0], 0.0, 1.0)
        for v in range(0, variables, 2):
            ends = [c["a"][v + w] - keep * c["corr"][v + w] for w in (0, 1)]
            pack(ends, message, v, blocks, block)

    plan = routes(rows)
    firsts = [k for k in (0, 1) if rows == 8]
    first_turn = [home[k] for k in firsts]

    def hop(k, n, q):
        sender, receiver = plan[k][n]
        src = message if sender == home[k] else messages.at[k]
        return remote(
            src.at[q],
            messages.at[k, q],
            c["send"].at[k, n, q],
            c["recv"].at[k, q],
            {"tm": receiver, "space": me},
        )

    def side(q):
        return remote(
            relaxed.at[q],
            messages.at[0, q],
            c["side_send"].at[q],
            c["recv"].at[0, q],
            {"tm": 1, "space": me},
        )

    def last_copy(src, to, n):
        return remote(
            src.at[me], last, c["last_send"].at[n], c["last_recv"], {"tm": to, "space": me}
        )

    next_row = choose(here, [k + 1 if k >= 0 else 0 for k in chain])

    for k in range(rows - 2):

        @pl.when(here == home[k])
        def _():
            if home[k] ^ 1 in first_turn and k not in firsts:
                pl.semaphore_wait(c["turn"], 1)
            far = [n for n, pair in enumerate(plan[k]) if pair[0] == home[k]]
            near = [n for n in far if plan[k][n][1] // 2 == home[k] // 2]
            far = [n for n in far if n not in near]
            for q in range(blocks):
                for n in far + near:
                    if n in far and k in firsts and q >= 2:
                        hop(k, n, q - 2).wait_send()
                    hop(k, n, q).start()
            if k in firsts:
                for q in range(blocks - 2, blocks):
                    for n in far:
                        hop(k, n, q).wait_send()
                pl.semaphore_signal(
                    c["turn"],
                    inc=1,
                    device_id={"tm": home[k] ^ 1, "space": me},
                    device_id_type=MESH,
                )

    sends_last = jnp.logical_and(busy, next_row != here)
    keep_last = pltpu.make_async_copy(message.at[me], last, c["local"].at[3])

    @pl.when(sends_last)
    def _():
        last_copy(message, next_row, 0).start()

    @pl.when(here == home[0])
    def _():
        for q in range(blocks):
            side(q).start()
        last_copy(relaxed, 0, 1).start()

    for k in range(rows - 2):
        if home[k] >= k + 2:

            @pl.when(here == home[k])
            def _():
                keep = pltpu.make_async_copy(message, messages.at[k], c["local"].at[3])
                keep.start()
                keep.wait()

    def receive(wanted):
        for t in range(rows):
            todo = []
            for k in wanted:
                for n, (sender, receiver) in enumerate(plan[k]):
                    if receiver == t:
                        todo.append((k, n))
            direct = [e for e in todo if plan[e[0]][e[1]][0] == home[e[0]]]
            rest = [e for e in todo if e not in direct]
            if todo:
                receive_at(t, (direct, rest))

    def receive_at(t, groups):
        @pl.when(here == t)
        def _():
            for group in groups:
                for q in range(blocks):
                    for k, n in group:
                        hop(k, n, q).wait_recv()
                        for n2, (sender, _) in enumerate(plan[k]):
                            if sender == t:
                                hop(k, n2, q).start()

    receive(range(2))

    @pl.when(here == 1)
    def _():
        for q in range(blocks):
            side(q).wait_recv()

    @pl.when(here == 0)
    def _():
        load_x(starts)

    @pl.when(here > 0)
    def _():
        load_x(messages.at[0])

    def advance(i):
        @pl.when(i == 1)
        def _():
            receive(range(2, rows - 2))

        terms = {}

        def finish(v, new):
            if v % 2 == 0:
                terms[v], terms[v + 1] = unpack(messages.at[i + 1], v, blocks, block)
            store_x(c, v, new + terms[v])

        coarse_substep(c, finish)

    loop(here - 2, advance)
    own_last = jnp.logical_and(busy, next_row == here)

    @pl.when(own_last)
    def _():
        keep_last.start()
        keep_last.wait()

    @pl.when(jnp.logical_not(own_last))
    def _():
        last_copy(message, next_row, 0).wait_recv()

    for v in range(0, variables, 2):
        both = last[v * block : (v + 2) * block, :].astype(F32)
        for w in (0, 1):
            out[STRIDE - 1, v + w] = both[w * block : (w + 1) * block]

    find_jumps(c)

    @pl.when(here >= 2)
    def _():
        def keep(v, new):
            c["a"][v] = new

        transport_react(c, c["coarse"], COARSE_GAIN, keep)
        for v in range(variables):
            out[STRIDE - 1, v] += c["a"][v, mine, :]

    fine_rest(c)

    def fine(i):
        fine_substep(c)

        @pl.when(i % 2 == 0)
        def _():
            out[i // 2] = c["a"][:, mine, :]

    loop(2 * (STRIDE - 1) - 1, fine)

    @pl.when(zero)
    def _():
        for d in range(1, size):
            first_copy(d).wait_send()

    @pl.when(stays)
    def _():
        for d in range(1, size):
            guess_copy(here, d).wait_send()

    @pl.when(moves)
    def _():
        for d in range(size):
            guess_copy(target, d).wait_send()

    for d in range(1, size):
        code_copy(d).wait_send()
    for k in range(rows - 2):
        for n, (sender, receiver) in enumerate(plan[k]):
            if k in firsts and sender == home[k] and receiver // 2 != sender // 2:
                continue

            @pl.when(here == sender)
            def _():
                for q in range(blocks):
                    hop(k, n, q).wait_send()

    @pl.when(sends_last)
    def _():
        last_copy(message, next_row, 0).wait_send()

    @pl.when(here == home[0])
    def _():
        for q in range(blocks):
            side(q).wait_send()
        last_copy(relaxed, 0, 1).wait_send()


def body(
    coarse_guess,
    initial_state,
    fine_volume,
    coarse_volume,
    lift_matrix,
    wave_speed,
    reaction_rate,
    species_map,
    neighbour_element,
    neighbour_rank,
):
    block, variables, nodes = initial_state.shape
    blocks, rows = lax.axis_size("space"), lax.axis_size("tm")
    faces, reactions = lift_matrix.shape[0], species_map.shape[0]
    elems, pair = blocks * block, faces // 3
    dma = pltpu.SemaphoreType.DMA
    packed = (variables * block, nodes)
    state = VMEM((blocks,) + packed, BF16)
    slab = VMEM((variables, elems, nodes), BF16)
    sums = VMEM((reactions, elems, nodes), BF16)
    full = VMEM((variables, elems, nodes), F32)
    weights = VMEM((nodes + faces, nodes), BF16)
    table = VMEM((3, elems, pair), jnp.int32)
    hops = max(len(pairs) for pairs in routes(rows))
    scratch = {
        "guess_held": VMEM((variables, block, nodes), F32),
        "initial_held": VMEM((variables, block, nodes), F32),
        "table": VMEM((nodes, 2 * pair), BF16),
        "starts": state,
        "message": state,
        "relaxed": state,
        "messages": VMEM((rows - 2, blocks) + packed, BF16),
        "last": VMEM(packed, BF16),
        "own_guess": VMEM(packed, BF16),
        "own_first": VMEM(packed, BF16),
        "code": VMEM((3, block, pair), jnp.int32),
        "codes": VMEM((blocks, 3, block, pair), jnp.int32),
        "xj": VMEM((variables * elems, nodes + faces), BF16),
        "a": full,
        "corr": full,
        "idx": table,
        "rank": table,
        "fine": weights,
        "coarse": weights,
        "m": slab,
        "h": slab,
        "rate": sums,
        "used": sums,
        "made": sums,
        "order": VMEM((8, 128), jnp.int32),
        "order_smem": SMEM((8, 128), jnp.int32),
        "whole": SMEM((5, reactions), jnp.int32),
        "part": SMEM((5, reactions), F32),
        "load": dma((2, 7)),
        "fetch": dma((3,)),
        "turn": pltpu.SemaphoreType.REGULAR,
        "local": dma((4,)),
        "code_send": dma((blocks,)),
        "code_recv": dma((blocks,)),
        "start_recv": dma((blocks,)),
        "first_send": dma((blocks,)),
        "guess_send": dma((blocks,)),
        "send": dma((rows - 2, hops, blocks)),
        "recv": dma((rows - 2, blocks)),
        "side_send": dma((blocks,)),
        "last_send": dma((2,)),
        "last_recv": dma(()),
    }
    inputs = (
        jnp.transpose(coarse_guess, (0, 2, 1, 3)),
        jnp.transpose(initial_state, (1, 0, 2)),
        neighbour_element,
        neighbour_rank,
        jnp.asarray(face_table(SIDE)).astype(BF16),
        lift_matrix,
        fine_volume,
        coarse_volume,
        wave_speed,
        reaction_rate,
        jnp.transpose(species_map),
        jnp.transpose(species_map),
    )
    spaces = [
        SMEM if name in IN_SMEM else pl.ANY if name in IN_ANY else VMEM for name in INPUTS
    ]
    out = pl.pallas_call(
        lambda *refs: whole_kernel(INPUTS + ("out",) + tuple(scratch), *refs),
        out_shape=jax.ShapeDtypeStruct((STRIDE, variables, block, nodes), F32),
        in_specs=[pl.BlockSpec(memory_space=space) for space in spaces],
        out_specs=pl.BlockSpec(memory_space=VMEM),
        scratch_shapes=list(scratch.values()),
        compiler_params=pltpu.CompilerParams(
            collective_id=0, has_side_effects=True, vmem_limit_bytes=60 * 1024 * 1024
        ),
    )(*inputs)
    return jnp.transpose(out, (0, 2, 1, 3))


def solution(mesh):
    placed = (
        P("tm", "space", None, None),
        P("space", None, None),
        P(),
        P(),
        P(),
        P(),
        P(),
        P(),
        P("space", None),
        P("space", None),
    )
    return jax.shard_map(
        body, mesh=mesh, in_specs=placed, out_specs=P("tm", "space", None, None), check_vma=False
    )
```

```python
import jax
import jax.numpy as jnp
import numpy as np
from jax import lax
from jax.experimental import pallas as pl
from jax.experimental.pallas import tpu as pltpu
from jax.sharding import PartitionSpec as P

SIDE = 8
STRIDE = 4
COARSE_GAIN = 4.0
VMEM = pltpu.VMEM
SMEM = pltpu.SMEM
MESH = pl.DeviceIdType.MESH
BF16 = jnp.bfloat16
F32 = jnp.float32


def face_table(side):
    plane = side * side
    inner = np.arange(plane)
    first, second = inner // side, inner % side
    last = side - 1
    node_lists = [
        first * plane + second,
        first * plane + last * side + second,
        first * plane + second * side,
        first * plane + second * side + last,
    ]
    table = np.zeros((side**3, 4 * plane), np.float32)
    for f in range(4):
        table[node_lists[f], f * plane + inner] = 1.0
    return table


def find_jumps(c):
    xj, idx, rank, speed = c["xj"], c["idx"], c["rank"], c["speed"]
    variables, elems, nodes = c["a"].shape
    block = c["block"]
    blocks = elems // block
    pair = idx.shape[2]
    picked = jnp.dot(xj[:, 0:nodes], c["table"][...], preferred_element_type=F32)
    low = lax.broadcasted_iota(jnp.int32, (elems, pair), 1) < pair // 2
    for k in range(3):
        spots = [idx[k, s * block : (s + 1) * block, :] for s in range(blocks)]
        offsets = [rank[k, s * block : (s + 1) * block, :] for s in range(blocks)]
        for v in range(variables):
            rows = slice(v * elems, (v + 1) * elems)
            if k == 0:
                faces = jnp.where(
                    low,
                    xj[rows, 0:pair].astype(F32),
                    xj[rows, nodes - pair : nodes].astype(F32),
                )
            else:
                faces = picked[rows, (k - 1) * pair : k * pair]
            own = [faces[s * block : (s + 1) * block] for s in range(blocks)]
            parts = []
            for s in range(blocks):
                before, here, after = [
                    jnp.take_along_axis(
                        own[(s + d) % blocks], spots[s], axis=0, mode="promise_in_bounds"
                    )
                    for d in (-1, 0, 1)
                ]
                across = jnp.where(
                    offsets[s] < 0, before, jnp.where(offsets[s] > 0, after, here)
                )
                parts.append(speed[v] * (across - pltpu.roll(own[s], pair // 2, 1)))
            xj[rows, nodes + k * pair : nodes + (k + 1) * pair] = jnp.concatenate(
                parts, axis=0
            ).astype(BF16)


def transport_react(c, weights, gain, finish):
    m, h, rates, used, made = c["m"], c["h"], c["rate"], c["used"], c["made"]
    whole, part = c["whole"], c["part"]
    variables, elems, nodes = m.shape
    moved = jnp.dot(c["xj"][...], weights[...], preferred_element_type=F32)
    for v in range(variables):
        own = moved[v * elems : (v + 1) * elems].astype(BF16)
        m[v] = own
        h[v] = own * own + 0.5
    total = None
    for q in range(rates.shape[0]):
        s0, s1 = whole[0, q], whole[1, q]
        factor = (part[0, q] * gain).astype(BF16)
        rate = factor * (m[s0] * m[s1]) / (h[s0] + h[s1])
        rates[q] = rate
        total = rate if q == 0 else total * part[1, q].astype(BF16) + rate
        used[q] = total
    total = None
    for q in range(rates.shape[0]):
        rate = rates[whole[2, q]]
        total = rate if q == 0 else total * part[2, q].astype(BF16) + rate
        made[q] = total
    for v in range(variables):
        finish(v, m[v] + (made[whole[4, v]] - used[whole[3, v]]))


def sort_reactions(c, order, order_smem, sem):
    across = c["species_across"]
    count = across.shape[1]
    variables = c["a"].shape[0]
    r_down = lax.broadcasted_iota(jnp.int32, (count, 1), 0)
    r_across = lax.broadcasted_iota(jnp.int32, (1, count), 1)
    lane = lax.broadcasted_iota(jnp.int32, (count, 128), 1)

    def down(which):
        here = jnp.where(r_down == r_across, across[which : which + 1, :], 0)
        return jnp.sum(here, axis=1, keepdims=True)

    def places(which):
        key_down = down(which) * count + r_down
        key_across = across[which : which + 1, :] * count + r_across
        before = (key_across < key_down).astype(jnp.int32)
        place_down = jnp.sum(before, axis=1, keepdims=True)
        return place_down, jnp.where(lane == place_down, r_down, 0)

    place, ordered = places(0)
    _, ordered_made = places(2)
    order[...] = jnp.zeros(order.shape, jnp.int32)
    order[0:1, :] = jnp.sum(ordered, axis=0, keepdims=True)
    order[1:2, :] = jnp.sum(jnp.where(lane == r_down, place, 0), axis=0, keepdims=True)
    order[2:3, :] = jnp.sum(ordered_made, axis=0, keepdims=True)
    for row, which in ((3, 0), (5, 2)):
        species = down(which)
        order[row : row + 1, :] = jnp.sum(
            (species <= lane).astype(jnp.int32), axis=0, keepdims=True
        )
        order[row + 1 : row + 2, :] = jnp.sum(
            (species == lane).astype(jnp.int32), axis=0, keepdims=True
        )
    copy = pltpu.make_async_copy(order, order_smem, sem)
    copy.start()
    copy.wait()
    whole, part, flat = c["whole"], c["part"], c["species"]
    for q in range(count):
        r, s = order_smem[0, q], order_smem[2, q]
        whole[0, q] = flat[0, r]
        whole[1, q] = flat[1, r]
        whole[2, q] = order_smem[1, s]
        part[0, q] = c["rates"][r]
        if q > 0:
            r, s = order_smem[0, q - 1], order_smem[2, q - 1]
            part[1, q] = jnp.where(flat[0, r] == whole[0, q], 1.0, 0.0)
            now = flat[2, order_smem[2, q]]
            part[2, q] = jnp.where(flat[2, s] == now, 1.0, 0.0)
    for v in range(variables):
        for row, at in ((3, 3), (5, 4)):
            found = order_smem[row + 1, v] > 0
            whole[at, v] = jnp.where(found, order_smem[row, v] - 1, count)
    for sums in (c["used"], c["made"]):
        sums[count] = jnp.zeros(sums.shape[1:], BF16)


def store_x(c, v, new):
    elems, nodes = new.shape
    c["xj"][v * elems : (v + 1) * elems, 0:nodes] = new.astype(BF16)


def fine_substep(c):
    find_jumps(c)
    fine_rest(c)


def fine_rest(c):
    def finish(v, new):
        store_x(c, v, new)

    transport_react(c, c["fine"], 1.0, finish)


def coarse_substep(c, finish):
    find_jumps(c)
    transport_react(c, c["coarse"], COARSE_GAIN, finish)


def state_of(c, v):
    _, elems, nodes = c["m"].shape
    return c["xj"][v * elems : (v + 1) * elems, 0:nodes].astype(F32)


def unpack(ref, v, blocks, block):
    both = [ref[s, v * block : (v + 2) * block, :].astype(F32) for s in range(blocks)]
    return [
        jnp.concatenate([b[w * block : (w + 1) * block] for b in both], axis=0) for w in (0, 1)
    ]


def pack(values, ref, v, blocks, block):
    for s in range(blocks):
        both = jnp.concatenate([e[s * block : (s + 1) * block] for e in values], axis=0)
        ref[s, v * block : (v + 2) * block, :] = both.astype(BF16)


def loop(count, fn):
    def one(i, carry):
        fn(i)
        return carry

    lax.fori_loop(0, count, one, 0)


def remote(src, dst, send, recv, target):
    return pltpu.make_async_remote_copy(
        src_ref=src,
        dst_ref=dst,
        send_sem=send,
        recv_sem=recv,
        device_id=target,
        device_id_type=MESH,
    )


def places_of_chains(rows):
    if rows == 8:
        return [4, 2, 5, 3, 6, 7, 1]
    return [k + 2 for k in range(rows - 2)] + [1]


def choose(me, values):
    value = jnp.int32(values[0])
    for i, other in enumerate(values[1:], 1):
        value = jnp.where(me == i, other, value)
    return value


def routes(rows):
    home = places_of_chains(rows)
    out = []
    for k in range(rows - 2):
        src = home[k]
        core = src % 2
        needs = [i for i in range(k + 2, rows) if i != src]
        pairs = []
        for chip in range(rows // 2):
            mine = [i for i in needs if i // 2 == chip]
            if not mine:
                continue
            if chip == src // 2:
                pairs.append((src, mine[0]))
                continue
            front = 2 * chip + core
            if front not in mine:
                front = mine[0]
            if rows == 8 and k == 0 and chip == 1:
                pairs += [(src, 0), (0, front)]
            else:
                pairs.append((src, front))
            pairs += [(front, i) for i in mine if i != front]
        out.append(pairs)
    return out


INPUTS = (
    "guess",
    "initial",
    "element",
    "neighbour",
    "table_in",
    "lift_in",
    "fine_in",
    "coarse_in",
    "speed",
    "rates",
    "species",
    "species_across",
)
IN_SMEM = ("speed", "rates", "species")
IN_ANY = ("guess", "initial", "table_in", "lift_in", "fine_in", "coarse_in")


def whole_kernel(names, *refs):
    c = dict(zip(names, refs))
    me, size = lax.axis_index("space"), lax.axis_size("space")
    here, rows = lax.axis_index("tm"), lax.axis_size("tm")
    variables, elems, nodes = c["a"].shape
    block = c["block"] = elems // size
    blocks = size
    starts, messages, message, last = c["starts"], c["messages"], c["message"], c["last"]
    relaxed, codes, code, out = c["relaxed"], c["codes"], c["code"], c["out"]
    home = places_of_chains(rows)
    mine = pl.ds(pl.multiple_of(me * block, block), block)

    chain = [home.index(t) if t in home else -1 for t in range(rows)]
    target = choose(here, [0] + home[1:] + [home[0]])
    source = choose(here, [k if k > 0 else rows - 1 if k == 0 else -1 for k in chain])
    stays = jnp.logical_and(here >= 1, target == here)
    moves = jnp.logical_and(here >= 1, target != here)
    busy = choose(here, [int(k >= 0) for k in chain]) == 1
    zero = here == 0
    comes = jnp.logical_and(source >= 0, source != here)

    def mate(row, d):
        return {"tm": row, "space": lax.rem(me + d, size)}

    barrier = pltpu.get_barrier_semaphore()
    for d in range(1, rows):
        friend = {"tm": lax.rem(here + d, rows), "space": me}
        pl.semaphore_signal(barrier, inc=1, device_id=friend, device_id_type=MESH)
    for d in range(1, size):
        pl.semaphore_signal(barrier, inc=1, device_id=mate(here, d), device_id_type=MESH)

    @pl.when(comes)
    def _():
        for d in range(1, size):
            pl.semaphore_signal(barrier, inc=1, device_id=mate(source, d), device_id_type=MESH)

    fetches = [("guess_held", c["guess"].at[0]), ("initial_held", c["initial"])]
    fetches = [
        pltpu.make_async_copy(src, c[dst], c["fetch"].at[i]) for i, (dst, src) in enumerate(fetches)
    ]
    for fetch in fetches:
        fetch.start()
    table_load = pltpu.make_async_copy(c["table_in"], c["table"], c["fetch"].at[2])

    half = code.shape[2] // 2
    loads = []
    for i, (name, src) in enumerate((("fine", "fine_in"), ("coarse", "coarse_in"))):
        loads.append((c[src], c[name].at[0:nodes], c["load"].at[i, 6]))
        for f in range(6):
            rows_in = c["lift_in"].at[(f ^ 1) * half : (f ^ 1) * half + half]
            rows_out = c[name].at[nodes + f * half : nodes + (f + 1) * half]
            loads.append((rows_in, rows_out, c["load"].at[i, f]))
    loads = [pltpu.make_async_copy(*load) for load in loads]
    loads.append(table_load)
    for load in loads:
        load.start()

    lanes = code.shape[2]
    value = c["element"][...] + block * (c["neighbour"][...] + 1)
    low = lax.broadcasted_iota(jnp.int32, (block, lanes), 1) < lanes // 2
    for k in range(3):
        code[k] = jnp.where(low, value[:, 2 * k + 1 : 2 * k + 2], value[:, 2 * k : 2 * k + 1])
    for fetch in fetches:
        fetch.wait()

    def take(src, dst):
        for v in range(0, variables, 2):
            both = jnp.concatenate([src[v], src[v + 1]], axis=0)
            dst[v * block : (v + 2) * block, :] = both.astype(BF16)

    @pl.when(here == 0)
    def _():
        take(c["initial_held"], c["own_first"])

    @pl.when(jnp.logical_and(here > 0, here < rows - 1))
    def _():
        take(c["guess_held"], c["own_guess"])

    @pl.when(here == rows - 1)
    def _():
        take(c["initial_held"], c["own_guess"])

    pl.semaphore_wait(barrier, rows + size - 2 + (size - 1) * moves.astype(jnp.int32))

    def code_copy(d):
        return remote(code, codes.at[me], c["code_send"].at[d], c["code_recv"].at[d], mate(here, d))

    def start_copy(src, sems, row, d):
        return remote(src, starts.at[me], sems.at[d], c["start_recv"].at[d], mate(row, d))

    def first_copy(d):
        return start_copy(c["own_first"], c["first_send"], here, d)

    def guess_copy(row, d):
        return start_copy(c["own_guess"], c["guess_send"], row, d)

    keep_code = pltpu.make_async_copy(code, codes.at[me], c["local"].at[0])
    keep_first = pltpu.make_async_copy(c["own_first"], starts.at[me], c["local"].at[1])
    keep_guess = pltpu.make_async_copy(c["own_guess"], starts.at[me], c["local"].at[1])

    @pl.when(zero)
    def _():
        for d in range(1, size):
            first_copy(d).start()
        keep_first.start()

    @pl.when(stays)
    def _():
        for d in range(1, size):
            guess_copy(here, d).start()
        keep_guess.start()

    @pl.when(moves)
    def _():
        for d in range(size):
            guess_copy(target, d).start()

    for d in range(1, size):
        code_copy(d).start()
    keep_code.start()
    sort_reactions(c, c["order"], c["order_smem"], c["local"].at[2])
    keep_code.wait()
    for d in range(1, size):
        code_copy(d).wait_recv()
    for s in range(blocks):
        for k in range(3):
            found = codes[s, k]
            spots = slice(s * block, (s + 1) * block)
            c["idx"][k, spots, :] = lax.rem(found, block)
            c["rank"][k, spots, :] = lax.div(found, block) - 1
    for load in loads:
        load.wait()

    @pl.when(zero)
    def _():
        keep_first.wait()
        for d in range(1, size):
            first_copy(d).wait_recv()

    @pl.when(stays)
    def _():
        keep_guess.wait()
        for d in range(1, size):
            guess_copy(here, d).wait_recv()

    @pl.when(comes)
    def _():
        for d in range(size):
            guess_copy(target, d).wait_recv()

    def load_x(ref):
        for v in range(0, variables, 2):
            for w, part in enumerate(unpack(ref, v, blocks, block)):
                store_x(c, v + w, part)

    @pl.when(busy)
    def _():
        load_x(starts)
        loop(2 * STRIDE, lambda i: fine_substep(c))

        @pl.when(here == home[0])
        def _():
            for v in range(0, variables, 2):
                pack([state_of(c, v), state_of(c, v + 1)], relaxed, v, blocks, block)

        def finish(v, new):
            c["corr"][v] = new.astype(F32)

        coarse_substep(c, finish)
        fine_rest(c)
        loop(2 * STRIDE - 1, lambda i: fine_substep(c))
        keep = jnp.where(here == home[0], 0.0, 1.0)
        for v in range(0, variables, 2):
            ends = [state_of(c, v + w) - keep * c["corr"][v + w] for w in (0, 1)]
            pack(ends, message, v, blocks, block)

    plan = routes(rows)
    firsts = [k for k in (0, 1) if rows == 8]
    first_turn = [home[k] for k in firsts]

    def hop(k, n, q):
        sender, receiver = plan[k][n]
        src = message if sender == home[k] else messages.at[k]
        return remote(
            src.at[q],
            messages.at[k, q],
            c["send"].at[k, n, q],
            c["recv"].at[k, q],
            {"tm": receiver, "space": me},
        )

    def side(q):
        return remote(
            relaxed.at[q],
            messages.at[0, q],
            c["side_send"].at[q],
            c["recv"].at[0, q],
            {"tm": 1, "space": me},
        )

    def last_copy(src, to, n):
        return remote(
            src.at[me], last, c["last_send"].at[n], c["last_recv"], {"tm": to, "space": me}
        )

    next_row = choose(here, [k + 1 if k >= 0 else 0 for k in chain])

    for k in range(rows - 2):

        @pl.when(here == home[k])
        def _():
            if home[k] ^ 1 in first_turn and k not in firsts:
                pl.semaphore_wait(c["turn"], 1)
            far = [n for n, pair in enumerate(plan[k]) if pair[0] == home[k]]
            near = [n for n in far if plan[k][n][1] // 2 == home[k] // 2]
            far = [n for n in far if n not in near]
            for q in range(blocks):
                for n in far + near:
                    if n in far and k in firsts and q >= 2:
                        hop(k, n, q - 2).wait_send()
                    hop(k, n, q).start()
            if k in firsts:
                for q in range(blocks - 2, blocks):
                    for n in far:
                        hop(k, n, q).wait_send()
                pl.semaphore_signal(
                    c["turn"],
                    inc=1,
                    device_id={"tm": home[k] ^ 1, "space": me},
                    device_id_type=MESH,
                )

    sends_last = jnp.logical_and(busy, next_row != here)
    keep_last = pltpu.make_async_copy(message.at[me], last, c["local"].at[3])

    @pl.when(sends_last)
    def _():
        last_copy(message, next_row, 0).start()

    @pl.when(here == home[0])
    def _():
        for q in range(blocks):
            side(q).start()
        last_copy(relaxed, 0, 1).start()

    for k in range(rows - 2):
        if home[k] >= k + 2:

            @pl.when(here == home[k])
            def _():
                keep = pltpu.make_async_copy(message, messages.at[k], c["local"].at[3])
                keep.start()
                keep.wait()

    def receive(wanted):
        for t in range(rows):
            todo = []
            for k in wanted:
                for n, (sender, receiver) in enumerate(plan[k]):
                    if receiver == t:
                        todo.append((k, n))
            direct = [e for e in todo if plan[e[0]][e[1]][0] == home[e[0]]]
            rest = [e for e in todo if e not in direct]
            if todo:
                receive_at(t, (direct, rest))

    def receive_at(t, groups):
        @pl.when(here == t)
        def _():
            for group in groups:
                for q in range(blocks):
                    for k, n in group:
                        hop(k, n, q).wait_recv()
                        for n2, (sender, _) in enumerate(plan[k]):
                            if sender == t:
                                hop(k, n2, q).start()

    receive(range(2))

    @pl.when(here == 1)
    def _():
        for q in range(blocks):
            side(q).wait_recv()

    @pl.when(here == 0)
    def _():
        load_x(starts)

    @pl.when(here > 0)
    def _():
        load_x(messages.at[0])

    def advance(i):
        @pl.when(i == 1)
        def _():
            receive(range(2, rows - 2))

        terms = {}

        def finish(v, new):
            if v % 2 == 0:
                terms[v], terms[v + 1] = unpack(messages.at[i + 1], v, blocks, block)
            store_x(c, v, new.astype(F32) + terms[v])

        coarse_substep(c, finish)

    loop(here - 2, advance)
    own_last = jnp.logical_and(busy, next_row == here)

    @pl.when(own_last)
    def _():
        keep_last.start()
        keep_last.wait()

    @pl.when(jnp.logical_not(own_last))
    def _():
        last_copy(message, next_row, 0).wait_recv()

    for v in range(0, variables, 2):
        both = last[v * block : (v + 2) * block, :].astype(F32)
        for w in (0, 1):
            out[STRIDE - 1, v + w] = both[w * block : (w + 1) * block].astype(BF16)

    find_jumps(c)

    @pl.when(here >= 2)
    def _():
        def keep(v, new):
            c["a"][v] = new.astype(F32)

        transport_react(c, c["coarse"], COARSE_GAIN, keep)
        for v in range(variables):
            term = out[STRIDE - 1, v].astype(F32)
            out[STRIDE - 1, v] = (c["a"][v, mine, :] + term).astype(BF16)

    fine_rest(c)

    def fine(i):
        fine_substep(c)

        @pl.when(i % 2 == 0)
        def _():
            for v in range(variables):
                c["a"][v] = state_of(c, v)
            for v in range(variables):
                out[i // 2, v] = c["a"][v, mine, :].astype(BF16)

    loop(2 * (STRIDE - 1) - 1, fine)

    @pl.when(zero)
    def _():
        for d in range(1, size):
            first_copy(d).wait_send()

    @pl.when(stays)
    def _():
        for d in range(1, size):
            guess_copy(here, d).wait_send()

    @pl.when(moves)
    def _():
        for d in range(size):
            guess_copy(target, d).wait_send()

    for d in range(1, size):
        code_copy(d).wait_send()
    for k in range(rows - 2):
        for n, (sender, receiver) in enumerate(plan[k]):
            if k in firsts and sender == home[k] and receiver // 2 != sender // 2:
                continue

            @pl.when(here == sender)
            def _():
                for q in range(blocks):
                    hop(k, n, q).wait_send()

    @pl.when(sends_last)
    def _():
        last_copy(message, next_row, 0).wait_send()

    @pl.when(here == home[0])
    def _():
        for q in range(blocks):
            side(q).wait_send()
        last_copy(relaxed, 0, 1).wait_send()


def body(
    coarse_guess,
    initial_state,
    fine_volume,
    coarse_volume,
    lift_matrix,
    wave_speed,
    reaction_rate,
    species_map,
    neighbour_element,
    neighbour_rank,
):
    block, variables, nodes = initial_state.shape
    blocks, rows = lax.axis_size("space"), lax.axis_size("tm")
    faces, reactions = lift_matrix.shape[0], species_map.shape[0]
    elems, pair = blocks * block, faces // 3
    dma = pltpu.SemaphoreType.DMA
    packed = (variables * block, nodes)
    state = VMEM((blocks,) + packed, BF16)
    slab = VMEM((variables, elems, nodes), BF16)
    rates = VMEM((reactions, elems, nodes), BF16)
    sums = VMEM((reactions + 1, elems, nodes), BF16)
    full = VMEM((variables, elems, nodes), F32)
    weights = VMEM((nodes + faces, nodes), BF16)
    table = VMEM((3, elems, pair), jnp.int32)
    hops = max(len(pairs) for pairs in routes(rows))
    scratch = {
        "guess_held": VMEM((variables, block, nodes), F32),
        "initial_held": VMEM((variables, block, nodes), F32),
        "table": VMEM((nodes, 2 * pair), BF16),
        "starts": state,
        "message": state,
        "relaxed": state,
        "messages": VMEM((rows - 2, blocks) + packed, BF16),
        "last": VMEM(packed, BF16),
        "own_guess": VMEM(packed, BF16),
        "own_first": VMEM(packed, BF16),
        "code": VMEM((3, block, pair), jnp.int32),
        "codes": VMEM((blocks, 3, block, pair), jnp.int32),
        "xj": VMEM((variables * elems, nodes + faces), BF16),
        "a": full,
        "corr": full,
        "idx": table,
        "rank": table,
        "fine": weights,
        "coarse": weights,
        "m": slab,
        "h": slab,
        "rate": rates,
        "used": sums,
        "made": sums,
        "order": VMEM((8, 128), jnp.int32),
        "order_smem": SMEM((8, 128), jnp.int32),
        "whole": SMEM((5, reactions), jnp.int32),
        "part": SMEM((3, reactions), F32),
        "load": dma((2, 7)),
        "fetch": dma((3,)),
        "turn": pltpu.SemaphoreType.REGULAR,
        "local": dma((4,)),
        "code_send": dma((blocks,)),
        "code_recv": dma((blocks,)),
        "start_recv": dma((blocks,)),
        "first_send": dma((blocks,)),
        "guess_send": dma((blocks,)),
        "send": dma((rows - 2, hops, blocks)),
        "recv": dma((rows - 2, blocks)),
        "side_send": dma((blocks,)),
        "last_send": dma((2,)),
        "last_recv": dma(()),
    }
    inputs = (
        jnp.transpose(coarse_guess, (0, 2, 1, 3)),
        jnp.transpose(initial_state, (1, 0, 2)),
        neighbour_element,
        neighbour_rank,
        jnp.asarray(face_table(SIDE)).astype(BF16),
        lift_matrix,
        fine_volume,
        coarse_volume,
        wave_speed,
        reaction_rate,
        jnp.transpose(species_map),
        jnp.transpose(species_map),
    )
    spaces = [
        SMEM if name in IN_SMEM else pl.ANY if name in IN_ANY else VMEM for name in INPUTS
    ]
    out = pl.pallas_call(
        lambda *refs: whole_kernel(INPUTS + ("out",) + tuple(scratch), *refs),
        out_shape=jax.ShapeDtypeStruct((STRIDE, variables, block, nodes), BF16),
        in_specs=[pl.BlockSpec(memory_space=space) for space in spaces],
        out_specs=pl.BlockSpec(memory_space=VMEM),
        scratch_shapes=list(scratch.values()),
        compiler_params=pltpu.CompilerParams(
            collective_id=0, has_side_effects=True, vmem_limit_bytes=60 * 1024 * 1024
        ),
    )(*inputs)
    return jnp.transpose(out, (0, 2, 1, 3)).astype(F32)


def solution(mesh):
    placed = (
        P("tm", "space", None, None),
        P("space", None, None),
        P(),
        P(),
        P(),
        P(),
        P(),
        P(),
        P("space", None),
        P("space", None),
    )
    return jax.shard_map(
        body, mesh=mesh, in_specs=placed, out_specs=P("tm", "space", None, None), check_vma=False
    )
```

```python
from types import SimpleNamespace

import jax
import jax.numpy as jnp
import numpy as np
from jax import lax
from jax.experimental import pallas as pl
from jax.experimental.pallas import tpu as pltpu
from jax.sharding import PartitionSpec as P

SIDE = 8
STRIDE = 4
COARSE_GAIN = 4.0
VMEM = pltpu.VMEM
SMEM = pltpu.SMEM
MESH = pl.DeviceIdType.MESH
BF16 = jnp.bfloat16
F32 = jnp.float32


def face_table(side):
    plane = side * side
    inner = np.arange(plane)
    first, second = inner // side, inner % side
    last = side - 1
    node_lists = [
        first * plane + second,
        first * plane + last * side + second,
        first * plane + second * side,
        first * plane + second * side + last,
    ]
    table = np.zeros((side**3, 4 * plane), np.float32)
    for f in range(4):
        table[node_lists[f], f * plane + inner] = 1.0
    return table


def find_jumps(c):
    xj, idx, rank, speed = c.xj, c.idx, c.rank, c.speed
    variables, elems, nodes = c.a.shape
    block = c.block
    blocks = elems // block
    pair = idx.shape[2]
    picked = jnp.dot(xj[:, 0:nodes], c.table[...], preferred_element_type=F32)
    low = lax.broadcasted_iota(jnp.int32, (elems, pair), 1) < pair // 2
    for k in range(3):
        spots = [idx[k, s * block : (s + 1) * block, :] for s in range(blocks)]
        offsets = [rank[k, s * block : (s + 1) * block, :] for s in range(blocks)]
        for v in range(variables):
            rows = slice(v * elems, (v + 1) * elems)
            if k == 0:
                faces = jnp.where(
                    low,
                    xj[rows, 0:pair].astype(F32),
                    xj[rows, nodes - pair : nodes].astype(F32),
                )
            else:
                faces = picked[rows, (k - 1) * pair : k * pair]
            own = [faces[s * block : (s + 1) * block] for s in range(blocks)]
            parts = []
            for s in range(blocks):
                before, here, after = [
                    jnp.take_along_axis(
                        own[(s + d) % blocks], spots[s], axis=0, mode="promise_in_bounds"
                    )
                    for d in (-1, 0, 1)
                ]
                across = jnp.where(
                    offsets[s] < 0, before, jnp.where(offsets[s] > 0, after, here)
                )
                parts.append(speed[v] * (across - pltpu.roll(own[s], pair // 2, 1)))
            xj[rows, nodes + k * pair : nodes + (k + 1) * pair] = jnp.concatenate(
                parts, axis=0
            ).astype(BF16)


def transport_react(c, weights, gain, finish):
    m, h, rates, used, made = c.m, c.h, c.rate, c.used, c.made
    whole, part = c.whole, c.part
    variables, elems, nodes = m.shape
    moved = jnp.dot(c.xj[...], weights[...], preferred_element_type=F32)
    for v in range(variables):
        own = moved[v * elems : (v + 1) * elems].astype(BF16)
        m[v] = own
        h[v] = own * own + 0.5
    total = None
    for q in range(rates.shape[0]):
        s0, s1 = whole[0, q], whole[1, q]
        factor = (part[0, q] * gain).astype(BF16)
        rate = factor * (m[s0] * m[s1]) / (h[s0] + h[s1])
        rates[q] = rate
        total = rate if q == 0 else total * part[1, q].astype(BF16) + rate
        used[q] = total
    total = None
    for q in range(rates.shape[0]):
        rate = rates[whole[2, q]]
        total = rate if q == 0 else total * part[2, q].astype(BF16) + rate
        made[q] = total
    for v in range(variables):
        finish(v, m[v] + (made[whole[4, v]] - used[whole[3, v]]))


def sort_reactions(c, order, order_smem, sem):
    across = c.species_across
    count = across.shape[1]
    variables = c.a.shape[0]
    r_down = lax.broadcasted_iota(jnp.int32, (count, 1), 0)
    r_across = lax.broadcasted_iota(jnp.int32, (1, count), 1)
    lane = lax.broadcasted_iota(jnp.int32, (count, 128), 1)

    def down(which):
        here = jnp.where(r_down == r_across, across[which : which + 1, :], 0)
        return jnp.sum(here, axis=1, keepdims=True)

    def places(which):
        key_down = down(which) * count + r_down
        key_across = across[which : which + 1, :] * count + r_across
        before = (key_across < key_down).astype(jnp.int32)
        place_down = jnp.sum(before, axis=1, keepdims=True)
        return place_down, jnp.where(lane == place_down, r_down, 0)

    place, ordered = places(0)
    _, ordered_made = places(2)
    order[...] = jnp.zeros(order.shape, jnp.int32)
    order[0:1, :] = jnp.sum(ordered, axis=0, keepdims=True)
    order[1:2, :] = jnp.sum(jnp.where(lane == r_down, place, 0), axis=0, keepdims=True)
    order[2:3, :] = jnp.sum(ordered_made, axis=0, keepdims=True)
    for row, which in ((3, 0), (5, 2)):
        species = down(which)
        order[row : row + 1, :] = jnp.sum(
            (species <= lane).astype(jnp.int32), axis=0, keepdims=True
        )
        order[row + 1 : row + 2, :] = jnp.sum(
            (species == lane).astype(jnp.int32), axis=0, keepdims=True
        )
    copy = pltpu.make_async_copy(order, order_smem, sem)
    copy.start()
    copy.wait()
    whole, part, flat = c.whole, c.part, c.species
    for q in range(count):
        r, s = order_smem[0, q], order_smem[2, q]
        whole[0, q] = flat[0, r]
        whole[1, q] = flat[1, r]
        whole[2, q] = order_smem[1, s]
        part[0, q] = c.rates[r]
        if q > 0:
            r, s = order_smem[0, q - 1], order_smem[2, q - 1]
            part[1, q] = jnp.where(flat[0, r] == whole[0, q], 1.0, 0.0)
            now = flat[2, order_smem[2, q]]
            part[2, q] = jnp.where(flat[2, s] == now, 1.0, 0.0)
    for v in range(variables):
        for row, at in ((3, 3), (5, 4)):
            found = order_smem[row + 1, v] > 0
            whole[at, v] = jnp.where(found, order_smem[row, v] - 1, count)
    for sums in (c.used, c.made):
        sums[count] = jnp.zeros(sums.shape[1:], BF16)


def store_x(c, v, new):
    elems, nodes = new.shape
    c.xj[v * elems : (v + 1) * elems, 0:nodes] = new.astype(BF16)


def fine_substep(c):
    find_jumps(c)
    fine_rest(c)


def fine_rest(c):
    def finish(v, new):
        store_x(c, v, new)

    transport_react(c, c.fine, 1.0, finish)


def coarse_substep(c, finish):
    find_jumps(c)
    transport_react(c, c.coarse, COARSE_GAIN, finish)


def state_of(c, v):
    _, elems, nodes = c.m.shape
    return c.xj[v * elems : (v + 1) * elems, 0:nodes].astype(F32)


def unpack(ref, v, blocks, block):
    both = [ref[s, v * block : (v + 2) * block, :].astype(F32) for s in range(blocks)]
    return [
        jnp.concatenate([b[w * block : (w + 1) * block] for b in both], axis=0) for w in (0, 1)
    ]


def pack(values, ref, v, blocks, block):
    for s in range(blocks):
        both = jnp.concatenate([e[s * block : (s + 1) * block] for e in values], axis=0)
        ref[s, v * block : (v + 2) * block, :] = both.astype(BF16)


def loop(count, fn):
    def one(i, carry):
        fn(i)
        return carry

    lax.fori_loop(0, count, one, 0)


def remote(src, dst, send, recv, target):
    return pltpu.make_async_remote_copy(
        src_ref=src,
        dst_ref=dst,
        send_sem=send,
        recv_sem=recv,
        device_id=target,
        device_id_type=MESH,
    )


def places_of_chains(rows):
    if rows == 8:
        return [4, 2, 5, 3, 6, 7, 1]
    return [k + 2 for k in range(rows - 2)] + [1]


def choose(me, values):
    value = jnp.int32(values[0])
    for i, other in enumerate(values[1:], 1):
        value = jnp.where(me == i, other, value)
    return value


def routes(rows):
    home = places_of_chains(rows)
    out = []
    for k in range(rows - 2):
        src = home[k]
        core = src % 2
        needs = [i for i in range(k + 2, rows) if i != src]
        pairs = []
        for chip in range(rows // 2):
            mine = [i for i in needs if i // 2 == chip]
            if not mine:
                continue
            if chip == src // 2:
                pairs.append((src, mine[0]))
                continue
            front = 2 * chip + core
            if front not in mine:
                front = mine[0]
            if rows == 8 and k == 0 and chip == 1:
                pairs += [(src, 0), (0, front)]
            else:
                pairs.append((src, front))
            pairs += [(front, i) for i in mine if i != front]
        out.append(pairs)
    return out


def whole_kernel(names, *refs):
    c = SimpleNamespace(**dict(zip(names, refs)))
    me, size = lax.axis_index("space"), lax.axis_size("space")
    here, rows = lax.axis_index("tm"), lax.axis_size("tm")
    variables, elems, nodes = c.a.shape
    block = c.block = elems // size
    blocks = size
    starts, messages, message, last = c.starts, c.messages, c.message, c.last
    relaxed, codes, code, out = c.relaxed, c.codes, c.code, c.out
    home = places_of_chains(rows)
    mine = pl.ds(pl.multiple_of(me * block, block), block)

    chain = [home.index(t) if t in home else -1 for t in range(rows)]
    target = choose(here, [0] + home[1:] + [home[0]])
    source = choose(here, [k if k > 0 else rows - 1 if k == 0 else -1 for k in chain])
    stays = jnp.logical_and(here >= 1, target == here)
    moves = jnp.logical_and(here >= 1, target != here)
    busy = choose(here, [int(k >= 0) for k in chain]) == 1
    zero = here == 0
    comes = jnp.logical_and(source >= 0, source != here)

    def mate(row, d):
        return {"tm": row, "space": lax.rem(me + d, size)}

    barrier = pltpu.get_barrier_semaphore()
    for d in range(1, rows):
        friend = {"tm": lax.rem(here + d, rows), "space": me}
        pl.semaphore_signal(barrier, inc=1, device_id=friend, device_id_type=MESH)
    for d in range(1, size):
        pl.semaphore_signal(barrier, inc=1, device_id=mate(here, d), device_id_type=MESH)

    @pl.when(comes)
    def _():
        for d in range(1, size):
            pl.semaphore_signal(barrier, inc=1, device_id=mate(source, d), device_id_type=MESH)

    fetches = [(c.guess_held, c.guess.at[0]), (c.initial_held, c.initial)]
    fetches = [
        pltpu.make_async_copy(src, dst, c.fetch.at[i]) for i, (dst, src) in enumerate(fetches)
    ]
    for fetch in fetches:
        fetch.start()
    table_load = pltpu.make_async_copy(c.table_in, c.table, c.fetch.at[2])

    half = code.shape[2] // 2
    loads = []
    for i, (dst, src) in enumerate(((c.fine, c.fine_in), (c.coarse, c.coarse_in))):
        loads.append((src, dst.at[0:nodes], c.load.at[i, 6]))
        for f in range(6):
            rows_in = c.lift_in.at[(f ^ 1) * half : (f ^ 1) * half + half]
            rows_out = dst.at[nodes + f * half : nodes + (f + 1) * half]
            loads.append((rows_in, rows_out, c.load.at[i, f]))
    loads = [pltpu.make_async_copy(*load) for load in loads]
    loads.append(table_load)
    for load in loads:
        load.start()

    lanes = code.shape[2]
    value = c.element[...] + block * (c.neighbour[...] + 1)
    low = lax.broadcasted_iota(jnp.int32, (block, lanes), 1) < lanes // 2
    for k in range(3):
        code[k] = jnp.where(low, value[:, 2 * k + 1 : 2 * k + 2], value[:, 2 * k : 2 * k + 1])
    for fetch in fetches:
        fetch.wait()

    def take(src, dst):
        for v in range(0, variables, 2):
            both = jnp.concatenate([src[v], src[v + 1]], axis=0)
            dst[v * block : (v + 2) * block, :] = both.astype(BF16)

    @pl.when(here == 0)
    def _():
        take(c.initial_held, c.own_first)

    @pl.when(jnp.logical_and(here > 0, here < rows - 1))
    def _():
        take(c.guess_held, c.own_guess)

    @pl.when(here == rows - 1)
    def _():
        take(c.initial_held, c.own_guess)

    pl.semaphore_wait(barrier, rows + size - 2 + (size - 1) * moves.astype(jnp.int32))

    def code_copy(d):
        return remote(code, codes.at[me], c.code_send.at[d], c.code_recv.at[d], mate(here, d))

    def start_copy(src, sems, row, d):
        return remote(src, starts.at[me], sems.at[d], c.start_recv.at[d], mate(row, d))

    def first_copy(d):
        return start_copy(c.own_first, c.first_send, here, d)

    def guess_copy(row, d):
        return start_copy(c.own_guess, c.guess_send, row, d)

    keep_code = pltpu.make_async_copy(code, codes.at[me], c.local.at[0])
    keep_first = pltpu.make_async_copy(c.own_first, starts.at[me], c.local.at[1])
    keep_guess = pltpu.make_async_copy(c.own_guess, starts.at[me], c.local.at[1])

    late = here == rows - 2
    moves_now = jnp.logical_and(moves, jnp.logical_not(late))

    @pl.when(zero)
    def _():
        keep_first.start()

    @pl.when(stays)
    def _():
        for d in range(1, size):
            guess_copy(here, d).start()
        keep_guess.start()

    @pl.when(moves_now)
    def _():
        for d in range(size):
            guess_copy(target, d).start()

    for d in range(1, size):
        code_copy(d).start()
    keep_code.start()
    sort_reactions(c, c.order, c.order_smem, c.local.at[2])
    keep_code.wait()
    for d in range(1, size):
        code_copy(d).wait_recv()
    for s in range(blocks):
        for k in range(3):
            found = codes[s, k]
            spots = slice(s * block, (s + 1) * block)
            c.idx[k, spots, :] = lax.rem(found, block)
            c.rank[k, spots, :] = lax.div(found, block) - 1
    for load in loads:
        load.wait()

    @pl.when(here == 1)
    def _():
        for d in range(size):
            guess_copy(target, d).wait_send()
        friend = {"tm": 0, "space": me}
        pl.semaphore_signal(c.turn, inc=1, device_id=friend, device_id_type=MESH)

    @pl.when(zero)
    def _():
        pl.semaphore_wait(c.turn, 1)
        for d in range(1, size):
            first_copy(d).start()
        keep_first.wait()
        for d in range(1, size):
            first_copy(d).wait_recv()

    @pl.when(stays)
    def _():
        keep_guess.wait()
        for d in range(1, size):
            guess_copy(here, d).wait_recv()

    @pl.when(comes)
    def _():
        for d in range(size):
            guess_copy(target, d).wait_recv()

    @pl.when(late)
    def _():
        for d in range(size):
            guess_copy(target, d).start()

    def load_x(ref):
        for v in range(0, variables, 2):
            for w, part in enumerate(unpack(ref, v, blocks, block)):
                store_x(c, v + w, part)

    @pl.when(busy)
    def _():
        load_x(starts)
        loop(2 * STRIDE, lambda i: fine_substep(c))

        @pl.when(here == home[0])
        def _():
            for v in range(0, variables, 2):
                pack([state_of(c, v), state_of(c, v + 1)], relaxed, v, blocks, block)

        def finish(v, new):
            c.corr[v] = new.astype(F32)

        coarse_substep(c, finish)
        fine_rest(c)
        loop(2 * STRIDE - 1, lambda i: fine_substep(c))
        keep = jnp.where(here == home[0], 0.0, 1.0)
        for v in range(0, variables, 2):
            ends = [state_of(c, v + w) - keep * c.corr[v + w] for w in (0, 1)]
            pack(ends, message, v, blocks, block)

    plan = routes(rows)
    firsts = [k for k in (0, 1) if rows == 8]
    first_turn = [home[k] for k in firsts]

    def hop(k, n, q):
        sender, receiver = plan[k][n]
        src = message if sender == home[k] else messages.at[k]
        return remote(
            src.at[q],
            messages.at[k, q],
            c.send.at[k, n, q],
            c.recv.at[k, q],
            {"tm": receiver, "space": me},
        )

    def side(q):
        return remote(
            relaxed.at[q],
            messages.at[0, q],
            c.side_send.at[q],
            c.recv.at[0, q],
            {"tm": 1, "space": me},
        )

    def last_copy(src, to, n):
        return remote(
            src.at[me], last, c.last_send.at[n], c.last_recv, {"tm": to, "space": me}
        )

    next_row = choose(here, [k + 1 if k >= 0 else 0 for k in chain])

    for k in range(rows - 2):

        @pl.when(here == home[k])
        def _():
            if home[k] ^ 1 in first_turn and k not in firsts:
                pl.semaphore_wait(c.turn, 1)
            far = [n for n, pair in enumerate(plan[k]) if pair[0] == home[k]]
            near = [n for n in far if plan[k][n][1] // 2 == home[k] // 2]
            far = [n for n in far if n not in near]
            for q in range(blocks):
                for n in far + near:
                    if n in far and k in firsts and q >= 2:
                        hop(k, n, q - 2).wait_send()
                    hop(k, n, q).start()
            if k in firsts:
                for q in range(blocks - 2, blocks):
                    for n in far:
                        hop(k, n, q).wait_send()
                pl.semaphore_signal(
                    c.turn,
                    inc=1,
                    device_id={"tm": home[k] ^ 1, "space": me},
                    device_id_type=MESH,
                )

    sends_last = jnp.logical_and(busy, next_row != here)
    keep_last = pltpu.make_async_copy(message.at[me], last, c.local.at[3])

    @pl.when(sends_last)
    def _():
        last_copy(message, next_row, 0).start()

    @pl.when(here == home[0])
    def _():
        for q in range(blocks):
            side(q).start()
        last_copy(relaxed, 0, 1).start()

    for k in range(rows - 2):
        if home[k] >= k + 2:

            @pl.when(here == home[k])
            def _():
                keep = pltpu.make_async_copy(message, messages.at[k], c.local.at[3])
                keep.start()
                keep.wait()

    def receive(wanted):
        for t in range(rows):
            todo = []
            for k in wanted:
                for n, (sender, receiver) in enumerate(plan[k]):
                    if receiver == t:
                        todo.append((k, n))
            direct = [e for e in todo if plan[e[0]][e[1]][0] == home[e[0]]]
            rest = [e for e in todo if e not in direct]
            if todo:
                receive_at(t, (direct, rest))

    def receive_at(t, groups):
        @pl.when(here == t)
        def _():
            for group in groups:
                for q in range(blocks):
                    for k, n in group:
                        hop(k, n, q).wait_recv()
                        for n2, (sender, _) in enumerate(plan[k]):
                            if sender == t:
                                hop(k, n2, q).start()

    receive(range(2))

    @pl.when(here == 1)
    def _():
        for q in range(blocks):
            side(q).wait_recv()

    @pl.when(here == 0)
    def _():
        load_x(starts)

    @pl.when(here > 0)
    def _():
        load_x(messages.at[0])

    def advance(i):
        @pl.when(i == 1)
        def _():
            receive(range(2, rows - 2))

        terms = {}

        def finish(v, new):
            if v % 2 == 0:
                terms[v], terms[v + 1] = unpack(messages.at[i + 1], v, blocks, block)
            store_x(c, v, new.astype(F32) + terms[v])

        coarse_substep(c, finish)

    loop(here - 2, advance)
    find_jumps(c)

    @pl.when(here >= 2)
    def _():
        def keep(v, new):
            c.corr[v] = new.astype(F32)

        transport_react(c, c.coarse, COARSE_GAIN, keep)

    fine_rest(c)

    def fine(i):
        fine_substep(c)

        @pl.when(i % 2 == 0)
        def _():
            for v in range(variables):
                c.a[v] = state_of(c, v)
            for v in range(variables):
                out[i // 2, v] = c.a[v, mine, :].astype(BF16)

    loop(2 * (STRIDE - 1) - 1, fine)

    own_last = jnp.logical_and(busy, next_row == here)

    @pl.when(own_last)
    def _():
        keep_last.start()
        keep_last.wait()

    @pl.when(jnp.logical_not(own_last))
    def _():
        last_copy(message, next_row, 0).wait_recv()

    for v in range(0, variables, 2):
        both = last[v * block : (v + 2) * block, :].astype(F32)
        for w in (0, 1):
            out[STRIDE - 1, v + w] = both[w * block : (w + 1) * block].astype(BF16)

    @pl.when(here >= 2)
    def _():
        for v in range(variables):
            term = out[STRIDE - 1, v].astype(F32)
            out[STRIDE - 1, v] = (c.corr[v, mine, :] + term).astype(BF16)

    @pl.when(zero)
    def _():
        for d in range(1, size):
            first_copy(d).wait_send()

    @pl.when(stays)
    def _():
        for d in range(1, size):
            guess_copy(here, d).wait_send()

    @pl.when(jnp.logical_and(moves, here != 1))
    def _():
        for d in range(size):
            guess_copy(target, d).wait_send()

    for d in range(1, size):
        code_copy(d).wait_send()
    for k in range(rows - 2):
        for n, (sender, receiver) in enumerate(plan[k]):
            if k in firsts and sender == home[k] and receiver // 2 != sender // 2:
                continue

            @pl.when(here == sender)
            def _():
                for q in range(blocks):
                    hop(k, n, q).wait_send()

    @pl.when(sends_last)
    def _():
        last_copy(message, next_row, 0).wait_send()

    @pl.when(here == home[0])
    def _():
        for q in range(blocks):
            side(q).wait_send()
        last_copy(relaxed, 0, 1).wait_send()


def body(
    coarse_guess,
    initial_state,
    fine_volume,
    coarse_volume,
    lift_matrix,
    wave_speed,
    reaction_rate,
    species_map,
    neighbour_element,
    neighbour_rank,
):
    block, variables, nodes = initial_state.shape
    blocks, rows = lax.axis_size("space"), lax.axis_size("tm")
    faces, reactions = lift_matrix.shape[0], species_map.shape[0]
    elems, pair = blocks * block, faces // 3
    dma = pltpu.SemaphoreType.DMA
    packed = (variables * block, nodes)
    state = VMEM((blocks,) + packed, BF16)
    slab = VMEM((variables, elems, nodes), BF16)
    rates = VMEM((reactions, elems, nodes), BF16)
    sums = VMEM((reactions + 1, elems, nodes), BF16)
    full = VMEM((variables, elems, nodes), F32)
    weights = VMEM((nodes + faces, nodes), BF16)
    table = VMEM((3, elems, pair), jnp.int32)
    hops = max(len(pairs) for pairs in routes(rows))
    scratch = dict(
        guess_held=VMEM((variables, block, nodes), F32),
        initial_held=VMEM((variables, block, nodes), F32),
        table=VMEM((nodes, 2 * pair), BF16),
        starts=state,
        message=state,
        relaxed=state,
        messages=VMEM((rows - 2, blocks) + packed, BF16),
        last=VMEM(packed, BF16),
        own_guess=VMEM(packed, BF16),
        own_first=VMEM(packed, BF16),
        code=VMEM((3, block, pair), jnp.int32),
        codes=VMEM((blocks, 3, block, pair), jnp.int32),
        xj=VMEM((variables * elems, nodes + faces), BF16),
        a=full,
        corr=full,
        idx=table,
        rank=table,
        fine=weights,
        coarse=weights,
        m=slab,
        h=slab,
        rate=rates,
        used=sums,
        made=sums,
        order=VMEM((8, 128), jnp.int32),
        order_smem=SMEM((8, 128), jnp.int32),
        whole=SMEM((5, reactions), jnp.int32),
        part=SMEM((3, reactions), F32),
        load=dma((2, 7)),
        fetch=dma((3,)),
        turn=pltpu.SemaphoreType.REGULAR,
        local=dma((4,)),
        code_send=dma((blocks,)),
        code_recv=dma((blocks,)),
        start_recv=dma((blocks,)),
        first_send=dma((blocks,)),
        guess_send=dma((blocks,)),
        send=dma((rows - 2, hops, blocks)),
        recv=dma((rows - 2, blocks)),
        side_send=dma((blocks,)),
        last_send=dma((2,)),
        last_recv=dma(()),
    )
    inputs = dict(
        guess=(pl.ANY, jnp.transpose(coarse_guess, (0, 2, 1, 3))),
        initial=(pl.ANY, jnp.transpose(initial_state, (1, 0, 2))),
        element=(VMEM, neighbour_element),
        neighbour=(VMEM, neighbour_rank),
        table_in=(pl.ANY, jnp.asarray(face_table(SIDE)).astype(BF16)),
        lift_in=(pl.ANY, lift_matrix),
        fine_in=(pl.ANY, fine_volume),
        coarse_in=(pl.ANY, coarse_volume),
        speed=(SMEM, wave_speed),
        rates=(SMEM, reaction_rate),
        species=(SMEM, jnp.transpose(species_map)),
        species_across=(VMEM, jnp.transpose(species_map)),
    )
    names = tuple(inputs) + ("out",) + tuple(scratch)
    out = pl.pallas_call(
        lambda *refs: whole_kernel(names, *refs),
        out_shape=jax.ShapeDtypeStruct((STRIDE, variables, block, nodes), BF16),
        in_specs=[pl.BlockSpec(memory_space=space) for space, _ in inputs.values()],
        out_specs=pl.BlockSpec(memory_space=VMEM),
        scratch_shapes=list(scratch.values()),
        compiler_params=pltpu.CompilerParams(
            collective_id=0, has_side_effects=True, vmem_limit_bytes=60 * 1024 * 1024
        ),
    )(*[value for _, value in inputs.values()])
    return jnp.transpose(out, (0, 2, 1, 3)).astype(F32)


def solution(mesh):
    placed = (
        P("tm", "space", None, None),
        P("space", None, None),
        P(),
        P(),
        P(),
        P(),
        P(),
        P(),
        P("space", None),
        P("space", None),
    )
    return jax.shard_map(
        body, mesh=mesh, in_specs=placed, out_specs=P("tm", "space", None, None), check_vma=False
    )
```
